128 devices in a mesh: wide: 8 (over y, core), sixteen: 16 (over z, x).
Axes of the slice: x: 4, y: 4, z: 4, core: 2. Of those that a mesh axis runs over, the one named last changes fastest.
Arguments:
- observations: float32 [64, 512, 1024], P(None, 'sixteen', 'wide'), may hold values from -60 to 60
- huber_scale: float32 [64], replicated, may hold values from 0.5 to 2
- observed: int32 [512, 1024], P('sixteen', 'wide'), may hold values from 0 to 1, as said below
- jitter: float32 [2, 512, 1024], P(None, 'sixteen', 'wide'), may hold values from -0.4 to 0.4
- owner_map: int32 [8, 128], P('wide'), may hold values from 0 to 15, as said below
- neighbours: int32 [8, 128, 6], P('wide'), may hold values from 0 to 127, as said below
Outputs:
- solution: float32 [8, 16, 64, 8, 512], P('wide', 'sixteen')
- residual: float32 [8, 16, 64, 8, 512], P('wide', 'sixteen')
The draws below stay inside these ranges and needn't reach their ends.
Inputs may be any that keep to these rules, and one draw needn't show every extreme that they name: At least one whole lattice row and at least one whole lattice column hold no observed point. `owner_map`: in each column group every device along sixteen holds 8 blocks (block g on device g // 8) and sends them to 8 different owners; every owner receives exactly 8 blocks, each from a different device. `neighbours`: block g of a column group lists g + d and g - d modulo 128 for each of half of 6 different offsets d between 1 and 4; all blocks of one group use the same offsets, so every list holds 6 different blocks and the relation is symmetric.
All inputs are finite; a program needn't handle non-finite values.
Results may differ from the reference program's by a relative error of at most 0.0003.
Values sent between devices are 32-bit elements; how exact they have to be, the bound alone decides.
No kernel may reach another device: no remote copies, remote signals or barrier semaphores. Data moves between devices by JAX's collectives and lax.ppermute only.
A program may use at most 192 MiB of HBM per device.

```python
import math
import jax
import jax.numpy as jnp
from jax import lax

FIELDS = 64
BLOCK = 512
COL_DEV = 128
BLOCKS_DEV = 8
REACH = 4
NEIGHBOURS = 6
SWEEPS = 2
ITERS = 2
STRIP = 4
NSTRIPS = 128
NROW = 512
NCOL = 1024
N_WIDE = 8
N_SIXTEEN = 16


def draw_observations(key, part):
    first_key, second_key, third_key, random_key_four = jax.random.split(jax.random.fold_in(key, 11), 4)
    lattice_dimensions = (FIELDS, NROW, NCOL)
    row_coefficients = jax.random.normal(first_key, (FIELDS, NROW, 1), jnp.float32)
    column_coefficients = jax.random.normal(second_key, (FIELDS, 1, NCOL), jnp.float32)
    gaussian_jitter = jax.random.normal(third_key, lattice_dimensions, jnp.float32)
    outlier_spikes = jnp.where(jax.random.uniform(random_key_four, lattice_dimensions, jnp.float32) < 0.05, 6.0, 0.0) * jnp.sign(gaussian_jitter + 0.001)
    observed_values = 1.5 * row_coefficients + 1.5 * column_coefficients + gaussian_jitter + outlier_spikes
    return jnp.clip(observed_values, -60.0, 60.0).astype(jnp.float32)


def draw_observed(key, part):
    first_key, second_key, third_key = jax.random.split(jax.random.fold_in(key, 53), 3)
    base = jax.random.randint(first_key, (NROW, NCOL), 0, 8) < 7
    empty_rows = jax.random.randint(second_key, (2,), 0, NROW)
    empty_cols = jax.random.randint(third_key, (2,), 0, NCOL)
    rows_hit = jnp.any(jnp.arange(NROW, dtype=jnp.int32)[:, None] == empty_rows[None, :], axis=1)
    cols_hit = jnp.any(jnp.arange(NCOL, dtype=jnp.int32)[:, None] == empty_cols[None, :], axis=1)
    cleared = rows_hit[:, None] | cols_hit[None, :]
    return jnp.where(cleared, 0, base.astype(jnp.int32)).astype(jnp.int32)


def draw_owner_map(key, part):

    def one_group(group_key):
        first_key, second_key, third_key = jax.random.split(group_key, 3)
        sources = jax.random.permutation(first_key, N_SIXTEEN)
        owners = jax.random.permutation(second_key, N_SIXTEEN)
        orders = jax.vmap(lambda order_key: jax.random.permutation(order_key, BLOCKS_DEV))(jax.random.split(third_key, N_SIXTEEN))
        return owners[(sources[:, None] + orders) % N_SIXTEEN].reshape(-1)
    group_keys = jax.random.split(jax.random.fold_in(key, 23), N_WIDE)
    return jax.vmap(one_group)(group_keys).astype(jnp.int32)


def draw_neighbours(key, part):
    total_strips = BLOCKS_DEV * N_SIXTEEN

    def one_group(group_key):
        offsets = jax.random.permutation(group_key, REACH)[:NEIGHBOURS // 2] + 1
        signed = jnp.stack([offsets, -offsets], axis=1).reshape(-1)
        numbers = jnp.arange(total_strips, dtype=jnp.int32)
        return (numbers[:, None] + signed[None, :]) % total_strips
    group_keys = jax.random.split(jax.random.fold_in(key, 37), N_WIDE)
    return jax.vmap(one_group)(group_keys).astype(jnp.int32)


def level_of(key, shape, cuts, least, top_value):
    def one(position, blocks):
        draws = jax.random.uniform(jax.random.fold_in(jax.random.fold_in(key, 6), position), (blocks,), jnp.float32, least / len(cuts), top_value / len(cuts))
        return jnp.repeat(jnp.exp(draws), shape[position] // blocks).reshape((-1,) + (1,) * (len(shape) - position - 1))

    level = one(*cuts[0])
    for cut in cuts[1:]:
        level = level * one(*cut)
    return level


def setup_inputs(seed: int = 0) -> dict:
    arg_keys = jax.random.split(jax.random.key(seed), 7)
    observations = draw_observations(jax.random.fold_in(arg_keys[6], 71), 0)
    huber_scale = jnp.clip(jnp.exp(jax.random.uniform(arg_keys[1], (FIELDS,), jnp.float32, math.log(0.5), math.log(2.0))), 0.5, 2.0)
    observed = draw_observed(jax.random.fold_in(arg_keys[6], 71), 0)
    jitter = jnp.clip(jax.random.uniform(arg_keys[3], (2, NROW, NCOL), jnp.float32, -0.4, 0.4) * level_of(arg_keys[3], (2, NROW, NCOL), ((1, 16), (2, 8)), -0.4, 0.0), -0.4, 0.4)
    owner_map = draw_owner_map(jax.random.fold_in(arg_keys[6], 71), 0)
    neighbours = draw_neighbours(jax.random.fold_in(arg_keys[6], 71), 0)
    return {"observations": observations, "huber_scale": huber_scale, "observed": observed, "jitter": jitter, "owner_map": owner_map, "neighbours": neighbours}


HUBER_EDGE = 1.345
NUGGET_TERM = 1.0
SILL_TERM = 0.02
ROOT_THREE = 1.7320508075688772
EXACT = lax.Precision.HIGHEST

def covariance(centre, others, strip_rows):
    spread = 2.0 * strip_rows
    cutoff = 6.0 * strip_rows
    row_gap = others[0][:, :, None] - centre[0][None, None, :]
    col_gap = others[1][:, :, None] - centre[1][None, None, :]
    distance = jnp.sqrt(row_gap * row_gap + col_gap * col_gap)
    scaled = ROOT_THREE * distance / spread
    fading = jnp.maximum(1.0 - distance / cutoff, 0.0)
    return SILL_TERM * (1.0 + scaled) * jnp.exp(-scaled) * fading ** 4 * (1.0 + 4.0 * distance / cutoff)

def owned_table(group_map, owners, per_owner):
    total_strips = group_map.shape[0]
    member = (group_map[None, :] == jnp.arange(owners, dtype=jnp.int32)[:, None]).astype(jnp.int32)
    ranked = jnp.cumsum(member, axis=1, dtype=jnp.int32) - 1
    slot_hit = (ranked[:, :, None] == jnp.arange(per_owner, dtype=jnp.int32)[None, None, :]).astype(jnp.int32) * member[:, :, None]
    numbers = jnp.arange(total_strips, dtype=jnp.int32)
    return lax.optimization_barrier(jnp.sum(slot_hit * numbers[None, :, None], axis=1, dtype=jnp.int32))

def apply_operator(direction, centres, neighbours):

    def one_block(flat_index):
        group = flat_index // NSTRIPS
        strip_number = flat_index % NSTRIPS
        group_values = direction[group]
        group_places = centres[group]
        listed = neighbours[group, strip_number]
        own = group_values[:, strip_number]
        near = jnp.take(group_values, listed, axis=1)
        centre = group_places[:, strip_number]
        others = jnp.concatenate([centre[:, None], jnp.take(group_places, listed, axis=1)], axis=1)
        kernel = covariance(centre, others, STRIP)
        stacked = jnp.concatenate([(NEIGHBOURS + 1.0) * own[:, None], near], axis=1)
        return NUGGET_TERM * own + jnp.einsum('fmb,mba->fa', stacked, kernel, precision=EXACT)
    result = lax.map(one_block, jnp.arange(N_WIDE * NSTRIPS, dtype=jnp.int32))
    return result.reshape(N_WIDE, NSTRIPS, FIELDS, BLOCK).transpose(0, 2, 1, 3)

def blocked(observed_values):
    depth = observed_values.shape[0]
    shaped = observed_values.reshape(depth, NSTRIPS, STRIP, N_WIDE, COL_DEV)
    return shaped.transpose(3, 0, 1, 2, 4).reshape(N_WIDE, depth, NSTRIPS, BLOCK)

def reference(observations, huber_scale, observed, jitter, owner_map, neighbours):
    weight = observed.astype(jnp.float32)
    row_count = jnp.maximum(lax.optimization_barrier(jnp.sum(weight, axis=1)), 1.0)
    col_count = jnp.maximum(lax.optimization_barrier(jnp.sum(weight, axis=0)), 1.0)
    spread_scale = huber_scale[:, None, None]
    row_effect = jnp.zeros((FIELDS, NROW), jnp.float32)
    col_effect = jnp.zeros((FIELDS, NCOL), jnp.float32)
    for sweep_number in range(SWEEPS):
        clipped = jnp.clip((observations - row_effect[:, :, None] - col_effect[:, None, :]) / spread_scale, -HUBER_EDGE, HUBER_EDGE)
        row_effect = row_effect + huber_scale[:, None] * lax.optimization_barrier(jnp.sum(weight[None] * clipped, axis=2)) / row_count[None, :]
        clipped = jnp.clip((observations - row_effect[:, :, None] - col_effect[:, None, :]) / spread_scale, -HUBER_EDGE, HUBER_EDGE)
        col_effect = col_effect + huber_scale[:, None] * lax.optimization_barrier(jnp.sum(weight[None] * clipped, axis=1)) / col_count[None, :]
    residual_field = weight[None] * (observations - row_effect[:, :, None] - col_effect[:, None, :])
    row_place = jnp.arange(NROW, dtype=jnp.int32).astype(jnp.float32)
    col_place = jnp.arange(NCOL, dtype=jnp.int32).astype(jnp.float32)
    location = jnp.stack([row_place[:, None] + jitter[0], col_place[None, :] + jitter[1]])
    right_side = blocked(residual_field)
    centres = blocked(location)
    solution_now = jnp.zeros_like(right_side)
    residual_now = right_side
    direction = right_side
    norm_now = lax.optimization_barrier(jnp.sum(residual_now * residual_now, axis=(0, 2, 3)))
    for number in range(ITERS):
        image = apply_operator(direction, centres, neighbours)
        alpha = norm_now / lax.optimization_barrier(jnp.sum(direction * image, axis=(0, 2, 3)))
        solution_now = solution_now + alpha[None, :, None, None] * direction
        residual_now = residual_now - alpha[None, :, None, None] * image
        if number + 1 < ITERS:
            norm_next = lax.optimization_barrier(jnp.sum(residual_now * residual_now, axis=(0, 2, 3)))
            direction = residual_now + (norm_next / norm_now)[None, :, None, None] * direction
            norm_now = norm_next
    table = jax.vmap(lambda group_map: owned_table(group_map, N_SIXTEEN, BLOCKS_DEV))(owner_map)

    def place(observed_values):

        def one_group(group_values, group_table):
            picked = jnp.take(group_values, group_table.reshape(-1), axis=1)
            return picked.reshape(FIELDS, N_SIXTEEN, BLOCKS_DEV, BLOCK).transpose(1, 0, 2, 3)
        return jax.vmap(one_group)(observed_values, table)
    return (place(solution_now), place(residual_now))
```

```python
import functools

import jax
import jax.numpy as jnp
from jax import lax
from jax.experimental import pallas as pl
from jax.experimental.pallas import tpu as pltpu
from jax.sharding import Mesh
from jax.sharding import PartitionSpec as P

BLOCK = 512
BLOCKS_DEV = 8
REACH = 4
NEIGHBOURS = 6
PAIRED = NEIGHBOURS // 2
SWEEPS = 2
STRIP = 4
COL_DEV = 128
WIDE = ("wide_0", "wide_1")
SIXTEEN = ("sixteen_0", "sixteen_1")

HUBER_EDGE = 1.345
SILL_TERM = 0.02
ROOT_THREE = 1.7320508075688772
SPREAD = 2.0 * STRIP
CUTOFF = 6.0 * STRIP
BAND = 24
GROUP = 16

OWN_TILES = BLOCKS_DEV + PAIRED * BLOCKS_DEV - 6
HALO_TILES = 2 * (2 + 3 + 4)


def sent_to_all(shard, axis):
    peers = lax.axis_size(axis)
    return lax.all_to_all(
        jnp.broadcast_to(shard[None], (peers, *shard.shape)), axis, 0, 0, tiled=True
    )


def over_copies(shard, axis):
    return jnp.sum(sent_to_all(shard, axis), axis=0)


def beside(shard, width):
    peers, length = lax.axis_size(SIXTEEN), shard.shape[0]
    up = [(i, (i + 1) % peers) for i in range(peers)]
    down = [(j, i) for i, j in up]
    before = lax.ppermute(lax.slice_in_dim(shard, length - width, length, axis=0), SIXTEEN, up)
    after = lax.ppermute(lax.slice_in_dim(shard, 0, width, axis=0), SIXTEEN, down)
    return before, after


def owned_table(group_map, owners, per_owner):
    total_strips = group_map.shape[0]
    member = (group_map[None, :] == jnp.arange(owners, dtype=jnp.int32)[:, None]).astype(jnp.int32)
    ranked = jnp.cumsum(member, axis=1, dtype=jnp.int32) - 1
    slot_hit = (ranked[:, :, None] == jnp.arange(per_owner, dtype=jnp.int32)[None, None, :]).astype(
        jnp.int32
    ) * member[:, :, None]
    numbers = jnp.arange(total_strips, dtype=jnp.int32)
    return jnp.sum(slot_hit * numbers[None, :, None], axis=1, dtype=jnp.int32)


def tile_lists(first_list, first_block, total):
    steps = jnp.arange(1, REACH + 1, dtype=jnp.int32)
    held = jnp.any(
        first_list[None, :] == ((first_block + steps) % total)[:, None], axis=1
    )
    missing = jnp.min(jnp.where(held, REACH + 1, steps))
    offsets = [k + (missing <= k).astype(jnp.int32) for k in range(1, PAIRED + 1)]
    d1, d2, d3 = offsets
    t = jnp.arange(OWN_TILES - BLOCKS_DEV, dtype=jnp.int32)
    n1, n2, n3 = BLOCKS_DEV - d1, BLOCKS_DEV - d2, BLOCKS_DEV - d3
    count = n1 + n2 + n3
    t = jnp.minimum(t, count - 1)
    a = jnp.where(t < n1, t, jnp.where(t < n1 + n2, t - n1, t - n1 - n2))
    b = a + jnp.where(t < n1, d1, jnp.where(t < n1 + n2, d2, d3))
    own = jnp.arange(BLOCKS_DEV, dtype=jnp.int32)
    own_a, own_b = jnp.concatenate([own, a]), jnp.concatenate([own, b])
    own_count = BLOCKS_DEV + count
    half = HALO_TILES // 2
    t = jnp.arange(half, dtype=jnp.int32)
    halo = d1 + d2 + d3
    t = jnp.minimum(t, halo - 1)
    step = jnp.where(t < d1, d1, jnp.where(t < d1 + d2, d2, d3))
    pos = jnp.where(t < d1, t, jnp.where(t < d1 + d2, t - d1, t - d1 - d2))
    left_a, left_b = pos, pos - step
    right_a, right_b = BLOCKS_DEV - 1 - pos, BLOCKS_DEV - 1 - pos + step
    halo_a = jnp.concatenate([left_a, right_a])
    halo_b = jnp.concatenate([left_b, right_b])
    live = jnp.concatenate(
        [
            jnp.arange(OWN_TILES, dtype=jnp.int32) < own_count,
            jnp.tile(jnp.arange(half, dtype=jnp.int32) < halo, 2),
        ]
    ).astype(jnp.int32)
    return jnp.concatenate([own_a, halo_a]), jnp.concatenate([own_b, halo_b]), live


def tiles_kernel(a_ref, b_ref, live_ref, rows_ref, cols_ref, hi_ref, lo_ref):
    t = pl.program_id(0)

    @pl.when(live_ref[t] == 1)
    def _():
        one, other = a_ref[t] + REACH, b_ref[t] + REACH
        sill = jnp.where(one == other, (NEIGHBOURS + 1.0) * SILL_TERM, SILL_TERM)
        lane = lax.broadcasted_iota(jnp.int32, (GROUP, COL_DEV), 1)
        to = rows_ref[one]
        frm = cols_ref[other]
        a, b = ROOT_THREE * CUTOFF / SPREAD, 4.0
        for rb in range(STRIP):
            row_b = jnp.broadcast_to(frm[:, rb : rb + 1], (COL_DEV, COL_DEV))
            col_b = jnp.broadcast_to(frm[:, STRIP + rb : STRIP + rb + 1], (COL_DEV, COL_DEV))
            for u in range(COL_DEV // 2 // GROUP):
                lo_s = slice(GROUP * u, GROUP * (u + 1))
                hi_s = slice(64 + GROUP * u, 64 + GROUP * (u + 1))
                near = (lane >= GROUP * u - BAND) & (lane < GROUP * (u + 1) + BAND)
                one_m = jnp.where(near, 1.0, 0.0).astype(jnp.bfloat16)
                other_m = jnp.where(near, 0.0, 1.0).astype(jnp.bfloat16)
                row_s = jnp.where(near, row_b[lo_s], row_b[hi_s])
                col_s = jnp.where(near, col_b[lo_s], col_b[hi_s])
                for ra in range(STRIP):
                    dr = row_s - to[ra : ra + 1]
                    dc = col_s - to[STRIP + ra : STRIP + ra + 1]
                    square = dr * dr + dc * dc
                    far = square * lax.rsqrt(jnp.maximum(square, 1e-30))
                    fading = jnp.maximum(1.0 - far, 0.0)
                    fading = fading * fading
                    fading = fading * fading
                    shape = (1.0 + a * far) * (sill + (sill * b) * far)
                    value = shape * fading * jnp.exp(-a * far)
                    hi = value.astype(jnp.bfloat16)
                    lo = (value - hi.astype(jnp.float32)).astype(jnp.bfloat16)
                    lanes = slice(COL_DEV * ra, COL_DEV * (ra + 1))
                    top = rb * COL_DEV + GROUP * u
                    hi_ref[0, top : top + GROUP, lanes] = hi * one_m
                    hi_ref[0, top + 64 : top + 64 + GROUP, lanes] = hi * other_m
                    lo_ref[0, top : top + GROUP, lanes] = lo * one_m
                    lo_ref[0, top + 64 : top + 64 + GROUP, lanes] = lo * other_m


def covariance_tiles(one, other, live, rows, cols):
    count = one.shape[0]
    tile = pl.BlockSpec((1, BLOCK, BLOCK), lambda t, *_: (t, 0, 0))
    whole = lambda shape: pl.BlockSpec(shape, lambda t, *_: (0, 0, 0))
    shape = jax.ShapeDtypeStruct((count, BLOCK, BLOCK), jnp.bfloat16)
    return pl.pallas_call(
        tiles_kernel,
        grid_spec=pltpu.PrefetchScalarGridSpec(
            num_scalar_prefetch=3,
            grid=(count,),
            in_specs=[whole(rows.shape), whole(cols.shape)],
            out_specs=[tile, tile],
        ),
        out_shape=[shape, shape],
        compiler_params=pltpu.CompilerParams(vmem_limit_bytes=32 << 20),
        name="tiles",
    )(one, other, live, rows, cols)


def halves(v):
    hi = v.astype(jnp.bfloat16)
    lo = (v - hi.astype(jnp.float32)).astype(jnp.bfloat16)
    return hi, lo


NN = (((1,), (0,)), ((), ()))
NT = (((1,), (1,)), ((), ()))


def product(both, hi_tile, lo_tile, dims):
    fields = both.shape[0] // 2
    main = lax.dot_general(both, hi_tile, dims, preferred_element_type=jnp.float32)
    rest = lax.dot_general(both[:fields], lo_tile, dims, preferred_element_type=jnp.float32)
    return main[:fields] + (main[fields:] + rest)


def own_kernel(a_ref, b_ref, live_ref, v_ref, hi_ref, lo_ref, out_ref, both_ref):
    t = pl.program_id(0)
    fields = v_ref.shape[1]

    @pl.when(t == 0)
    def _():
        for g in range(BLOCKS_DEV):
            hi, lo = halves(v_ref[g])
            both_ref[g, :fields] = hi
            both_ref[g, fields:] = lo

    @pl.when(t < BLOCKS_DEV)
    def _():
        out_ref[t] = product(both_ref[t], hi_ref[0], lo_ref[0], NN)

    @pl.when((t >= BLOCKS_DEV) & (live_ref[t] == 1))
    def _():
        one, other = a_ref[t], b_ref[t]
        out_ref[one] += product(both_ref[other], hi_ref[0], lo_ref[0], NN)
        out_ref[other] += product(both_ref[one], hi_ref[0], lo_ref[0], NT)


def halo_kernel(
    a_ref, b_ref, live_ref, before_ref, after_ref, part_ref, hi_ref, lo_ref, out_ref, both_ref
):
    t = pl.program_id(0)
    fields = before_ref.shape[1]

    @pl.when(t == 0)
    def _():
        for g in range(REACH):
            for side, ref in enumerate((before_ref, after_ref)):
                hi, lo = halves(ref[g])
                both_ref[side * REACH + g, :fields] = hi
                both_ref[side * REACH + g, fields:] = lo
        out_ref[...] = part_ref[...]

    @pl.when(live_ref[t + OWN_TILES] == 1)
    def _():
        one, other = a_ref[t + OWN_TILES], b_ref[t + OWN_TILES]
        slot = jnp.where(other < 0, other + REACH, other - BLOCKS_DEV + REACH)
        out_ref[one] += product(both_ref[slot], hi_ref[0], lo_ref[0], NN)


def own_product(one, other, live, v, hi, lo):
    blocks, fields, _ = v.shape
    whole = pl.BlockSpec(v.shape, lambda t, *_: (0, 0, 0))
    tile = pl.BlockSpec((1, BLOCK, BLOCK), lambda t, *_: (t, 0, 0))
    return pl.pallas_call(
        own_kernel,
        grid_spec=pltpu.PrefetchScalarGridSpec(
            num_scalar_prefetch=3,
            grid=(OWN_TILES,),
            in_specs=[whole, tile, tile],
            out_specs=whole,
            scratch_shapes=[pltpu.VMEM((blocks, 2 * fields, BLOCK), jnp.bfloat16)],
        ),
        out_shape=jax.ShapeDtypeStruct(v.shape, jnp.float32),
        compiler_params=pltpu.CompilerParams(vmem_limit_bytes=32 << 20),
        name="own",
    )(one, other, live, v, hi, lo)


def halo_product(one, other, live, before, after, part, hi, lo):
    blocks, fields, _ = part.shape
    whole = lambda x: pl.BlockSpec(x.shape, lambda t, *_: (0, 0, 0))
    tile = pl.BlockSpec((1, BLOCK, BLOCK), lambda t, *_: (t + OWN_TILES, 0, 0))
    return pl.pallas_call(
        halo_kernel,
        grid_spec=pltpu.PrefetchScalarGridSpec(
            num_scalar_prefetch=3,
            grid=(HALO_TILES,),
            in_specs=[whole(before), whole(after), whole(part), tile, tile],
            out_specs=whole(part),
            scratch_shapes=[pltpu.VMEM((2 * REACH, 2 * fields, BLOCK), jnp.bfloat16)],
        ),
        out_shape=jax.ShapeDtypeStruct(part.shape, jnp.float32),
        compiler_params=pltpu.CompilerParams(vmem_limit_bytes=32 << 20),
        name="halo",
    )(one, other, live, before, after, part, hi, lo)


def sum_rows(parts):
    return jax.tree.map(lambda part: over_copies(part, WIDE), parts)


def sum_columns(parts):
    return jax.tree.map(lambda part: over_copies(part, SIXTEEN), parts)


def combine_kernel(src_ref, scale_ref, *refs):
    ins, (x_ref, r_ref) = refs[:-2], refs[-2:]
    scale = scale_ref[...]
    for j in range(BLOCKS_DEV):
        r0, m1, m2 = (ref[0] for ref in ins[3 * j : 3 * j + 3])
        x_ref[:, j, :] = scale[:, 0:1] * r0 + scale[:, 1:2] * m1
        r_ref[:, j, :] = scale[:, 2:3] * r0 + scale[:, 3:4] * m1 + scale[:, 4:5] * m2


def combined(sources, scale, r0, m1, m2):
    fields = r0.shape[1]
    part = 8
    ins, specs = [], []
    for j in range(BLOCKS_DEV):
        for v in (r0, m1, m2):
            ins.append(v)
            specs.append(
                pl.BlockSpec(
                    (1, part, BLOCK), functools.partial(lambda j, i, s: (s[j], i, 0), j)
                )
            )
    out = pl.BlockSpec((part, BLOCKS_DEV, BLOCK), lambda i, s: (i, 0, 0))
    shape = jax.ShapeDtypeStruct((fields, BLOCKS_DEV, BLOCK), jnp.float32)
    return pl.pallas_call(
        combine_kernel,
        grid_spec=pltpu.PrefetchScalarGridSpec(
            num_scalar_prefetch=1,
            grid=(fields // part,),
            in_specs=[pl.BlockSpec((part, 8), lambda i, s: (i, 0))] + specs,
            out_specs=[out, out],
        ),
        out_shape=[shape, shape],
        compiler_params=pltpu.CompilerParams(vmem_limit_bytes=32 << 20),
        name="combine",
    )(sources, scale, *ins)


def spread_kernel(slot_ref, v_ref, out_ref):
    out_ref[...] = v_ref[...]


def to_owners(v, targets):
    owners = lax.axis_size(SIXTEEN)
    _, fields, _ = v.shape
    block = (1, fields, BLOCK)
    slots = pl.pallas_call(
        spread_kernel,
        grid_spec=pltpu.PrefetchScalarGridSpec(
            num_scalar_prefetch=1,
            grid=(BLOCKS_DEV,),
            in_specs=[pl.BlockSpec(block, lambda g, s: (g, 0, 0))],
            out_specs=pl.BlockSpec(block, lambda g, s: (s[g], 0, 0)),
        ),
        out_shape=jax.ShapeDtypeStruct((owners, fields, BLOCK), jnp.float32),
        name="spread",
    )(targets, v)
    return lax.all_to_all(slots, SIXTEEN, 0, 0, tiled=True)


def step_scales(h00, h01, h11, h12):
    mu = h01 / h00
    var = (h11 - mu * h01) / h00
    a0 = 1.0 / (1.0 + mu)
    beta = var * a0 * a0
    skew = (h12 - mu * h11 - mu * (h11 - mu * h01)) / h00
    a1 = var / (var + skew - var * var * a0)
    x_r0 = a0 + a1 * beta + a1 * a0 * mu
    x_m1 = -a1 * a0
    r_r0 = a0 * mu * (1.0 - a1) - a1 * beta
    r_m1 = -a0 * (1.0 - a1) - a1 * a0 * mu - a1 * beta
    r_m2 = a1 * a0
    zero = jnp.zeros_like(mu)
    return jnp.stack([x_r0, x_m1, r_r0, r_m1, r_m2, zero, zero, zero], axis=1)


def on_device(observations, huber_scale, observed, jitter, owner_map, neighbours):
    fields, row_dev, col_dev = observations.shape
    sixteen_size = lax.axis_size(SIXTEEN)
    my_place = lax.axis_index(SIXTEEN)
    group_place = lax.axis_index(WIDE)
    total_strips = BLOCKS_DEV * sixteen_size
    group_map = owner_map[0]
    group_lists = neighbours[0]
    table = owned_table(group_map, sixteen_size, BLOCKS_DEV)
    my_ids = lax.dynamic_index_in_dim(table, my_place, 0, keepdims=False)
    sources = my_ids // BLOCKS_DEV
    my_targets = lax.dynamic_slice_in_dim(group_map, my_place * BLOCKS_DEV, BLOCKS_DEV)
    first_block = jnp.zeros((), jnp.int32)
    one, other, live = tile_lists(group_lists[0], first_block, total_strips)

    row_place = (my_place * row_dev + jnp.arange(row_dev, dtype=jnp.int32)).astype(jnp.float32)
    col_place = (group_place * col_dev + jnp.arange(col_dev, dtype=jnp.int32)).astype(jnp.float32)
    location = jnp.stack(
        [row_place[:, None] + jitter[0], col_place[None, :] + jitter[1]], axis=0
    ).reshape(2, BLOCKS_DEV, STRIP, col_dev)
    location = location.transpose(1, 0, 2, 3).reshape(BLOCKS_DEV, 2 * STRIP, col_dev)
    before, after = beside(location, REACH)
    wider = jnp.concatenate([before, location, after], axis=0) * (1.0 / CUTOFF)
    hi_tiles, lo_tiles = covariance_tiles(one, other, live, wider, wider.transpose(0, 2, 1))

    weight = observed.astype(jnp.float32)
    spread_scale = huber_scale[:, None, None]
    row_effect = jnp.zeros((fields, row_dev), jnp.float32)
    col_effect = jnp.zeros((fields, col_dev), jnp.float32)
    row_count = jnp.ones((row_dev,), jnp.float32)
    col_count = jnp.ones((col_dev,), jnp.float32)
    for sweep_number in range(SWEEPS):
        clipped = jnp.clip(
            (observations - row_effect[:, :, None] - col_effect[:, None, :]) / spread_scale,
            -HUBER_EDGE,
            HUBER_EDGE,
        )
        row_part = jnp.sum(weight[None] * clipped, axis=2)
        if sweep_number == 0:
            row_part, row_total = sum_rows((row_part, jnp.sum(weight, axis=1)))
            row_count = jnp.maximum(row_total, 1.0)
        else:
            row_part = sum_rows(row_part)
        row_effect = row_effect + huber_scale[:, None] * row_part / row_count[None, :]
        clipped = jnp.clip(
            (observations - row_effect[:, :, None] - col_effect[:, None, :]) / spread_scale,
            -HUBER_EDGE,
            HUBER_EDGE,
        )
        col_part = jnp.sum(weight[None] * clipped, axis=1)
        if sweep_number == 0:
            col_part, col_total = sum_columns((col_part, jnp.sum(weight, axis=0)))
            col_count = jnp.maximum(col_total, 1.0)
        else:
            col_part = sum_columns(col_part)
        col_effect = col_effect + huber_scale[:, None] * col_part / col_count[None, :]
    residual_field = weight[None] * (observations - row_effect[:, :, None] - col_effect[:, None, :])
    r0 = residual_field.reshape(fields, BLOCKS_DEV, BLOCK).transpose(1, 0, 2)

    def apply_tiles(v):
        before, after = beside(v, REACH)
        part = own_product(one, other, live, v, hi_tiles, lo_tiles)
        return halo_product(one, other, live, before, after, part, hi_tiles, lo_tiles)

    m1 = apply_tiles(r0)
    owned_r0 = to_owners(r0, my_targets)
    m2 = apply_tiles(m1)
    owned_m1 = to_owners(m1, my_targets)
    dots = jnp.stack([jnp.sum(p * q, axis=(0, 2)) for p, q in ((r0, r0), (r0, m1), (m1, m1), (m1, m2))])
    owned_m2 = to_owners(m2, my_targets)
    dots = over_copies(over_copies(dots, WIDE), SIXTEEN)
    scale = step_scales(*dots)
    solution_now, residual_now = combined(sources, scale, owned_r0, owned_m1, owned_m2)
    return (solution_now[None, None], residual_now[None, None])


def solution(mesh):
    finer = Mesh(mesh.devices.reshape(4, 2, 4, 4), ("wide_0", "wide_1", "sixteen_0", "sixteen_1"))
    in_specs = (
        P(None, SIXTEEN, WIDE),
        P(),
        P(SIXTEEN, WIDE),
        P(None, SIXTEEN, WIDE),
        P(WIDE, None),
        P(WIDE, None, None),
    )
    out_specs = (P(WIDE, SIXTEEN, None, None, None), P(WIDE, SIXTEEN, None, None, None))
    return jax.shard_map(
        on_device, mesh=finer, in_specs=in_specs, out_specs=out_specs, check_vma=False
    )
```

```python
import functools

import jax
import jax.numpy as jnp
from jax import lax
from jax.experimental import pallas as pl
from jax.experimental.pallas import tpu as pltpu
from jax.sharding import Mesh
from jax.sharding import PartitionSpec as P

BLOCK = 512
BLOCKS_DEV = 8
REACH = 4
NEIGHBOURS = 6
PAIRED = NEIGHBOURS // 2
SWEEPS = 2
STRIP = 4
COL_DEV = 128
WIDE = ("wide_0", "wide_1")
SIXTEEN = ("sixteen_0", "sixteen_1")

HUBER_EDGE = 1.345
SILL_TERM = 0.02
ROOT_THREE = 1.7320508075688772
SPREAD = 2.0 * STRIP
CUTOFF = 6.0 * STRIP
BAND = 24
GROUP = 16

OWN_TILES = BLOCKS_DEV + PAIRED * BLOCKS_DEV - 6
HALO_TILES = 2 * (2 + 3 + 4)
ROW_TILES, COL_TILES = 9, 13
TILE_SLOTS = 4
OP_SLOTS = 5


def sent_to_all(shard, axis):
    peers = lax.axis_size(axis)
    return lax.all_to_all(
        jnp.broadcast_to(shard[None], (peers, *shard.shape)), axis, 0, 0, tiled=True
    )


def over_copies(shard, axis):
    return jnp.sum(sent_to_all(shard, axis), axis=0)


def beside(shard, width):
    peers, length = lax.axis_size(SIXTEEN), shard.shape[0]
    up = [(i, (i + 1) % peers) for i in range(peers)]
    down = [(j, i) for i, j in up]
    before = lax.ppermute(lax.slice_in_dim(shard, length - width, length, axis=0), SIXTEEN, up)
    after = lax.ppermute(lax.slice_in_dim(shard, 0, width, axis=0), SIXTEEN, down)
    return before, after


def owned_table(group_map, owners, per_owner):
    total_strips = group_map.shape[0]
    member = (group_map[None, :] == jnp.arange(owners, dtype=jnp.int32)[:, None]).astype(jnp.int32)
    ranked = jnp.cumsum(member, axis=1, dtype=jnp.int32) - 1
    slot_hit = (ranked[:, :, None] == jnp.arange(per_owner, dtype=jnp.int32)[None, None, :]).astype(
        jnp.int32
    ) * member[:, :, None]
    numbers = jnp.arange(total_strips, dtype=jnp.int32)
    return jnp.sum(slot_hit * numbers[None, :, None], axis=1, dtype=jnp.int32)


def tile_lists(first_list, total):
    steps = jnp.arange(1, REACH + 1, dtype=jnp.int32)
    held = jnp.any(first_list[None, :] == (steps % total)[:, None], axis=1)
    missing = jnp.min(jnp.where(held, REACH + 1, steps))
    d1, d2, d3 = (k + (missing <= k).astype(jnp.int32) for k in range(1, PAIRED + 1))
    reach = d1 + d2 + d3
    t = jnp.arange(OWN_TILES + HALO_TILES, dtype=jnp.int32)
    n1, n2 = BLOCKS_DEV - d1, 2 * BLOCKS_DEV - d1 - d2
    own_count = (PAIRED + 1) * BLOCKS_DEV - reach
    p = t - BLOCKS_DEV
    pair_a = jnp.where(p < n1, p, jnp.where(p < n2, p - n1, p - n2))
    pair_b = pair_a + jnp.where(p < n1, d1, jnp.where(p < n2, d2, d3))
    q = t - OWN_TILES
    right = q >= reach
    q = jnp.where(right, q - reach, q)
    step = jnp.where(q < d1, d1, jnp.where(q < d1 + d2, d2, d3))
    pos = jnp.where(q < d1, q, jnp.where(q < d1 + d2, q - d1, q - d1 - d2))
    halo_a = jnp.where(right, BLOCKS_DEV - 1 - pos, pos)
    halo_b = jnp.where(right, BLOCKS_DEV - 1 - pos + step, pos - step)
    live = jnp.where(t < OWN_TILES, t < own_count, t < OWN_TILES + 2 * reach)
    one = jnp.where(t < BLOCKS_DEV, t, jnp.where(t < OWN_TILES, pair_a, halo_a))
    other = jnp.where(t < BLOCKS_DEV, t, jnp.where(t < OWN_TILES, pair_b, halo_b))
    one = jnp.where(live, one, 0)
    other = jnp.where(live, other, 0)
    counts = jnp.stack([own_count, 2 * reach])
    return jnp.concatenate([one, other, live.astype(jnp.int32), counts])


LISTED = OWN_TILES + HALO_TILES


def tiles_kernel(first, count, held, table_ref, rows_ref, cols_ref, *refs):
    tiles_ref, buf, sem = refs[held:]
    a, b = ROOT_THREE * CUTOFF / SPREAD, 4.0

    def out_copy(t):
        slot = lax.rem(t - first, TILE_SLOTS)
        return pltpu.make_async_copy(buf.at[slot], tiles_ref.at[t], sem.at[slot])

    def live(t):
        return table_ref[2 * LISTED + t] == 1

    def one_tile(t, carry):
        slot = lax.rem(t - first, TILE_SLOTS)
        past = jnp.maximum(t - TILE_SLOTS, first)

        @pl.when((t >= first + TILE_SLOTS) & live(past))
        def _():
            out_copy(past).wait()

        @pl.when(live(t))
        def _():
            one, other = table_ref[t], table_ref[LISTED + t]
            sill = jnp.where(one == other, (NEIGHBOURS + 1.0) * SILL_TERM, SILL_TERM)
            lane = lax.broadcasted_iota(jnp.int32, (GROUP, COL_DEV), 1)
            to = rows_ref[one + REACH]
            frm = cols_ref[other + REACH]
            for rb in range(STRIP):
                row_b = jnp.broadcast_to(frm[:, rb : rb + 1], (COL_DEV, COL_DEV))
                col_b = jnp.broadcast_to(frm[:, STRIP + rb : STRIP + rb + 1], (COL_DEV, COL_DEV))
                for u in range(COL_DEV // 2 // GROUP):
                    lo_s = slice(GROUP * u, GROUP * (u + 1))
                    hi_s = slice(64 + GROUP * u, 64 + GROUP * (u + 1))
                    near = (lane >= GROUP * u - BAND) & (lane < GROUP * (u + 1) + BAND)
                    one_m = jnp.where(near, 1.0, 0.0).astype(jnp.bfloat16)
                    other_m = jnp.where(near, 0.0, 1.0).astype(jnp.bfloat16)
                    row_s = jnp.where(near, row_b[lo_s], row_b[hi_s])
                    col_s = jnp.where(near, col_b[lo_s], col_b[hi_s])
                    for ra in range(STRIP):
                        dr = row_s - to[ra : ra + 1]
                        dc = col_s - to[STRIP + ra : STRIP + ra + 1]
                        square = dr * dr + dc * dc
                        far = square * lax.rsqrt(jnp.maximum(square, 1e-30))
                        fading = jnp.maximum(1.0 - far, 0.0)
                        fading = fading * fading
                        fading = fading * fading
                        shape = (1.0 + a * far) * (sill + (sill * b) * far)
                        value = shape * fading * jnp.exp(-a * far)
                        hi = value.astype(jnp.bfloat16)
                        lo = (value - hi.astype(jnp.float32)).astype(jnp.bfloat16)
                        lanes = slice(COL_DEV * ra, COL_DEV * (ra + 1))
                        top = rb * COL_DEV + GROUP * u
                        for part, at in ((hi, top), (lo, BLOCK + top)):
                            buf[slot, at : at + GROUP, lanes] = part * one_m
                            buf[slot, at + 64 : at + 64 + GROUP, lanes] = part * other_m
            out_copy(t).start()

        return carry

    lax.fori_loop(first, first + count, one_tile, 0)
    for t in range(max(first, first + count - TILE_SLOTS), first + count):

        @pl.when(live(t))
        def _(t=t):
            out_copy(t).wait()


def covariance_tiles(first, count, table, rows, cols, held):
    vmem, hbm = pl.BlockSpec(memory_space=pltpu.VMEM), pl.BlockSpec(memory_space=pl.ANY)
    extra = [] if held is None else [held]
    return pl.pallas_call(
        functools.partial(tiles_kernel, first, count, len(extra)),
        in_specs=[pl.BlockSpec(memory_space=pltpu.SMEM), vmem, vmem] + [hbm] * len(extra),
        out_specs=hbm,
        scratch_shapes=[
            pltpu.VMEM((TILE_SLOTS, 2 * BLOCK, BLOCK), jnp.bfloat16),
            pltpu.SemaphoreType.DMA((TILE_SLOTS,)),
        ],
        out_shape=jax.ShapeDtypeStruct((LISTED, 2 * BLOCK, BLOCK), jnp.bfloat16),
        input_output_aliases={3: 0} if extra else {},
        compiler_params=pltpu.CompilerParams(vmem_limit_bytes=32 << 20),
        name="tiles",
    )(table, rows, cols, *extra)


def halves(v):
    hi = v.astype(jnp.bfloat16)
    lo = (v - hi.astype(jnp.float32)).astype(jnp.bfloat16)
    return hi, lo


NN = (((1,), (0,)), ((), ()))
NT = (((1,), (1,)), ((), ()))


def product(both, tile_ref, dims):
    fields = both.shape[0] // 2
    main = lax.dot_general(
        both, tile_ref[:BLOCK], dims, preferred_element_type=jnp.float32
    )
    rest = lax.dot_general(
        both[:fields], tile_ref[BLOCK:], dims, preferred_element_type=jnp.float32
    )
    return main[:fields] + (main[fields:] + rest)


def tile_stream(tiles_ref, base, buf, sem):
    def copy(t):
        slot = lax.rem(t, OP_SLOTS)
        return pltpu.make_async_copy(tiles_ref.at[base + t], buf.at[slot], sem.at[slot])

    return copy


def own_kernel(table_ref, v_ref, tiles_ref, out_ref, both_ref, buf, sem):
    fields = v_ref.shape[1]
    count = table_ref[3 * LISTED]
    copy = tile_stream(tiles_ref, 0, buf, sem)
    for t in range(OP_SLOTS - 1):
        copy(t).start()
    for g in range(BLOCKS_DEV):
        hi, lo = halves(v_ref[g])
        both_ref[g, :fields] = hi
        both_ref[g, fields:] = lo

    def arrive(t):
        @pl.when(t + OP_SLOTS - 1 < count)
        def _():
            copy(t + OP_SLOTS - 1).start()

        copy(t).wait()
        return buf.at[lax.rem(t, OP_SLOTS)]

    def with_itself(t, carry):
        tile = arrive(t)
        out_ref[t] = product(both_ref[t], tile, NN)
        return carry

    def with_another(t, carry):
        tile = arrive(t)
        one, other = table_ref[t], table_ref[LISTED + t]
        out_ref[one] += product(both_ref[other], tile, NN)
        out_ref[other] += product(both_ref[one], tile, NT)
        return carry

    lax.fori_loop(0, BLOCKS_DEV, with_itself, 0)
    lax.fori_loop(BLOCKS_DEV, count, with_another, 0)


def halo_kernel(
    table_ref, target_ref, before_ref, after_ref, part_ref, tiles_ref, out_ref, slots_ref,
    both_ref, buf, sem, out_sem,
):
    fields = before_ref.shape[1]
    count = table_ref[3 * LISTED + 1]
    copy = tile_stream(tiles_ref, OWN_TILES, buf, sem)
    for t in range(OP_SLOTS - 1):
        copy(t).start()
    for side, ref in enumerate((before_ref, after_ref)):
        for g in range(REACH):
            hi, lo = halves(ref[g])
            both_ref[side * REACH + g, :fields] = hi
            both_ref[side * REACH + g, fields:] = lo
    out_ref[...] = part_ref[...]

    def with_beside(t, carry):
        @pl.when(t + OP_SLOTS - 1 < count)
        def _():
            copy(t + OP_SLOTS - 1).start()

        copy(t).wait()
        one, other = table_ref[OWN_TILES + t], table_ref[LISTED + OWN_TILES + t]
        side = jnp.where(other < 0, other + REACH, other - BLOCKS_DEV + REACH)
        out_ref[one] += product(both_ref[side], buf.at[lax.rem(t, OP_SLOTS)], NN)
        return carry

    lax.fori_loop(0, count, with_beside, 0)
    out_copies(out_ref, slots_ref, target_ref, out_sem)


def out_copies(values_ref, slots_ref, target_ref, sem):
    copies = [
        pltpu.make_async_copy(values_ref.at[g], slots_ref.at[target_ref[g]], sem.at[g])
        for g in range(BLOCKS_DEV)
    ]
    for copy in copies:
        copy.start()
    for copy in copies:
        copy.wait()


SMEM_SPEC = pl.BlockSpec(memory_space=pltpu.SMEM)
VMEM_SPEC = pl.BlockSpec(memory_space=pltpu.VMEM)
HBM_SPEC = pl.BlockSpec(memory_space=pl.ANY)


def stream_scratch():
    return [
        pltpu.VMEM((OP_SLOTS, 2 * BLOCK, BLOCK), jnp.bfloat16),
        pltpu.SemaphoreType.DMA((OP_SLOTS,)),
    ]


def own_product(table, v, tiles):
    blocks, fields, _ = v.shape
    return pl.pallas_call(
        own_kernel,
        in_specs=[SMEM_SPEC, VMEM_SPEC, HBM_SPEC],
        out_specs=VMEM_SPEC,
        scratch_shapes=[pltpu.VMEM((blocks, 2 * fields, BLOCK), jnp.bfloat16)] + stream_scratch(),
        out_shape=jax.ShapeDtypeStruct(v.shape, jnp.float32),
        compiler_params=pltpu.CompilerParams(vmem_limit_bytes=32 << 20),
        name="own",
    )(table, v, tiles)


def slot_shape(v):
    return jax.ShapeDtypeStruct((lax.axis_size(SIXTEEN), *v.shape[1:]), jnp.float32)


def halo_product(table, targets, before, after, part, tiles):
    blocks, fields, _ = part.shape
    return pl.pallas_call(
        halo_kernel,
        in_specs=[SMEM_SPEC, SMEM_SPEC, VMEM_SPEC, VMEM_SPEC, VMEM_SPEC, HBM_SPEC],
        out_specs=[VMEM_SPEC, HBM_SPEC],
        scratch_shapes=[pltpu.VMEM((2 * REACH, 2 * fields, BLOCK), jnp.bfloat16)]
        + stream_scratch()
        + [pltpu.SemaphoreType.DMA((BLOCKS_DEV,))],
        out_shape=[jax.ShapeDtypeStruct(part.shape, jnp.float32), slot_shape(part)],
        compiler_params=pltpu.CompilerParams(vmem_limit_bytes=32 << 20),
        name="halo",
    )(table, targets, before, after, part, tiles)


def residual_kernel(target_ref, obs_ref, weight_ref, row_ref, col_ref, out_ref, slots_ref, sem):
    col = col_ref[...]
    for g in range(BLOCKS_DEV):
        for ra in range(STRIP):
            r = STRIP * g + ra
            left = obs_ref[:, r, :] - row_ref[:, r : r + 1] - col
            out_ref[g, :, COL_DEV * ra : COL_DEV * (ra + 1)] = weight_ref[r : r + 1, :] * left
    out_copies(out_ref, slots_ref, target_ref, sem)


def residual_of(targets, observations, weight, row_effect, col_effect):
    fields = observations.shape[0]
    out = jax.ShapeDtypeStruct((BLOCKS_DEV, fields, BLOCK), jnp.float32)
    return pl.pallas_call(
        residual_kernel,
        in_specs=[SMEM_SPEC, VMEM_SPEC, VMEM_SPEC, VMEM_SPEC, VMEM_SPEC],
        out_specs=[VMEM_SPEC, HBM_SPEC],
        scratch_shapes=[pltpu.SemaphoreType.DMA((BLOCKS_DEV,))],
        out_shape=[out, slot_shape(out)],
        compiler_params=pltpu.CompilerParams(vmem_limit_bytes=32 << 20),
        name="residual",
    )(targets, observations, weight, row_effect, col_effect)


def combine_kernel(src_ref, scale_ref, *refs):
    ins, (x_ref, r_ref) = refs[:-2], refs[-2:]
    scale = scale_ref[...]
    for j in range(BLOCKS_DEV):
        r0, m1, m2 = (ref[0] for ref in ins[3 * j : 3 * j + 3])
        x_ref[:, j, :] = scale[:, 0:1] * r0 + scale[:, 1:2] * m1
        r_ref[:, j, :] = scale[:, 2:3] * r0 + scale[:, 3:4] * m1 + scale[:, 4:5] * m2


def combined(sources, scale, r0, m1, m2):
    fields = r0.shape[1]
    part = 8
    ins, specs = [], []
    for j in range(BLOCKS_DEV):
        for v in (r0, m1, m2):
            ins.append(v)
            specs.append(
                pl.BlockSpec(
                    (1, part, BLOCK), functools.partial(lambda j, i, s: (s[j], i, 0), j)
                )
            )
    out = pl.BlockSpec((part, BLOCKS_DEV, BLOCK), lambda i, s: (i, 0, 0))
    shape = jax.ShapeDtypeStruct((fields, BLOCKS_DEV, BLOCK), jnp.float32)
    return pl.pallas_call(
        combine_kernel,
        grid_spec=pltpu.PrefetchScalarGridSpec(
            num_scalar_prefetch=1,
            grid=(fields // part,),
            in_specs=[pl.BlockSpec((part, 8), lambda i, s: (i, 0))] + specs,
            out_specs=[out, out],
        ),
        out_shape=[shape, shape],
        compiler_params=pltpu.CompilerParams(vmem_limit_bytes=32 << 20),
        name="combine",
    )(sources, scale, *ins)


def to_owners(slots):
    return lax.all_to_all(slots, SIXTEEN, 0, 0, tiled=True)


def step_scales(h00, h01, h11, h12):
    mu = h01 / h00
    var = (h11 - mu * h01) / h00
    a0 = 1.0 / (1.0 + mu)
    beta = var * a0 * a0
    skew = (h12 - mu * h11 - mu * (h11 - mu * h01)) / h00
    a1 = var / (var + skew - var * var * a0)
    x_r0 = a0 + a1 * beta + a1 * a0 * mu
    x_m1 = -a1 * a0
    r_r0 = a0 * mu * (1.0 - a1) - a1 * beta
    r_m1 = -a0 * (1.0 - a1) - a1 * a0 * mu - a1 * beta
    r_m2 = a1 * a0
    zero = jnp.zeros_like(mu)
    return jnp.stack([x_r0, x_m1, r_r0, r_m1, r_m2, zero, zero, zero], axis=1)


def on_device(observations, huber_scale, observed, jitter, owner_map, neighbours):
    fields, row_dev, col_dev = observations.shape
    sixteen_size = lax.axis_size(SIXTEEN)
    my_place = lax.axis_index(SIXTEEN)
    group_place = lax.axis_index(WIDE)
    total_strips = BLOCKS_DEV * sixteen_size
    group_map = owner_map[0]
    group_lists = neighbours[0]
    owned = owned_table(group_map, sixteen_size, BLOCKS_DEV)
    my_ids = lax.dynamic_index_in_dim(owned, my_place, 0, keepdims=False)
    sources = my_ids // BLOCKS_DEV
    my_targets = lax.dynamic_slice_in_dim(group_map, my_place * BLOCKS_DEV, BLOCKS_DEV)
    table = tile_lists(group_lists[0], total_strips)

    row_place = (my_place * row_dev + jnp.arange(row_dev, dtype=jnp.int32)).astype(jnp.float32)
    col_place = (group_place * col_dev + jnp.arange(col_dev, dtype=jnp.int32)).astype(jnp.float32)
    location = jnp.stack(
        [row_place[:, None] + jitter[0], col_place[None, :] + jitter[1]], axis=0
    ).reshape(2, BLOCKS_DEV, STRIP, col_dev)
    location = location.transpose(1, 0, 2, 3).reshape(BLOCKS_DEV, 2 * STRIP, col_dev)
    location = location * (1.0 / CUTOFF)
    none = jnp.zeros((REACH, 2 * STRIP, col_dev), jnp.float32)
    here = jnp.concatenate([none, location, none], axis=0)
    here = (here, here.transpose(0, 2, 1))
    before, after = beside(location, REACH)
    wider = jnp.concatenate([before, location, after], axis=0)
    wider = (wider, wider.transpose(0, 2, 1))

    weight = observed.astype(jnp.float32)
    spread_scale = huber_scale[:, None, None]
    row_effect = jnp.zeros((fields, row_dev), jnp.float32)
    col_effect = jnp.zeros((fields, col_dev), jnp.float32)
    tiles = None
    first = 0

    def beside_tiles(part, axis, places, count, tiles, first):
        part, table_now, tiles = lax.optimization_barrier((part, table, tiles))
        total = over_copies(part, axis)
        tiles = covariance_tiles(first, count, table_now, *places, tiles)
        total, tiles = lax.optimization_barrier((total, tiles))
        return total, tiles, first + count

    def terms():
        return weight[None] * jnp.clip(
            (observations - row_effect[:, :, None] - col_effect[:, None, :]) / spread_scale,
            -HUBER_EDGE,
            HUBER_EDGE,
        )

    def with_count(part, count):
        rows = jnp.zeros((8, count.shape[0]), jnp.float32).at[0].set(count)
        return jnp.concatenate([part, rows], axis=0)

    for sweep_number in range(SWEEPS):
        part = jnp.sum(terms(), axis=2)
        if sweep_number == 0:
            part = with_count(part, jnp.sum(weight, axis=1))
        total, tiles, first = beside_tiles(
            part, WIDE, (here, wider)[sweep_number], ROW_TILES, tiles, first
        )
        if sweep_number == 0:
            row_count = jnp.maximum(total[fields], 1.0)
        row_effect = row_effect + huber_scale[:, None] * total[:fields] / row_count[None, :]
        part = jnp.sum(terms(), axis=1)
        if sweep_number == 0:
            part = with_count(part, jnp.sum(weight, axis=0))
        total, tiles, first = beside_tiles(
            part, SIXTEEN, (here, wider)[sweep_number], COL_TILES, tiles, first
        )
        if sweep_number == 0:
            col_count = jnp.maximum(total[fields], 1.0)
        col_effect = col_effect + huber_scale[:, None] * total[:fields] / col_count[None, :]

    r0, slots = residual_of(my_targets, observations, weight, row_effect, col_effect)
    owned_r0 = to_owners(slots)
    before, after = beside(r0, REACH)
    part = own_product(table, r0, tiles)
    m1, slots = halo_product(table, my_targets, before, after, part, tiles)
    before, after = beside(m1, REACH)
    part = own_product(table, m1, tiles)
    part, owned_r0 = lax.optimization_barrier((part, owned_r0))
    owned_m1 = to_owners(slots)
    m2, slots = halo_product(table, my_targets, before, after, part, tiles)
    m2, owned_m1, slots = lax.optimization_barrier((m2, owned_m1, slots))
    owned_m2 = to_owners(slots)
    dots = jnp.stack(
        [jnp.sum(p * q, axis=(0, 2)) for p, q in ((r0, r0), (r0, m1), (m1, m1), (m1, m2))]
    )
    dots = over_copies(over_copies(dots, WIDE), SIXTEEN)
    scale = step_scales(*dots)
    solution_now, residual_now = combined(sources, scale, owned_r0, owned_m1, owned_m2)
    return (solution_now[None, None], residual_now[None, None])


def solution(mesh):
    finer = Mesh(mesh.devices.reshape(4, 2, 4, 4), ("wide_0", "wide_1", "sixteen_0", "sixteen_1"))
    in_specs = (
        P(None, SIXTEEN, WIDE),
        P(),
        P(SIXTEEN, WIDE),
        P(None, SIXTEEN, WIDE),
        P(WIDE, None),
        P(WIDE, None, None),
    )
    out_specs = (P(WIDE, SIXTEEN, None, None, None), P(WIDE, SIXTEEN, None, None, None))
    return jax.shard_map(
        on_device, mesh=finer, in_specs=in_specs, out_specs=out_specs, check_vma=False
    )
```

```python
import functools

import jax
import jax.numpy as jnp
from jax import lax
from jax.experimental import pallas as pl
from jax.experimental.pallas import tpu as pltpu
from jax.sharding import Mesh
from jax.sharding import PartitionSpec as P

BLOCK = 512
BLOCKS_DEV = 8
REACH = 4
NEIGHBOURS = 6
PAIRED = NEIGHBOURS // 2
SWEEPS = 2
STRIP = 4
COL_DEV = 128
WIDE = ("wide_0", "wide_1")
SIXTEEN = ("sixteen_0", "sixteen_1")

HUBER_EDGE = 1.345
SILL_TERM = 0.02
ROOT_THREE = 1.7320508075688772
SPREAD = 2.0 * STRIP
CUTOFF = 6.0 * STRIP
BAND = 24
GROUP = 16

OWN_TILES = BLOCKS_DEV + PAIRED * BLOCKS_DEV - 6
HALO_TILES = 2 * (2 + 3 + 4)
ROW_TILES, COL_TILES = 7, 15
TILE_SLOTS = 4
OP_SLOTS = 5


def sent_to_all(shard, axis):
    peers = lax.axis_size(axis)
    return lax.all_to_all(
        jnp.broadcast_to(shard[None], (peers, *shard.shape)), axis, 0, 0, tiled=True
    )


def over_copies(shard, axis):
    return jnp.sum(sent_to_all(shard, axis), axis=0)


def sum_direct(part, axis):
    peers = lax.axis_size(axis)
    moved = [
        lax.ppermute(part, axis, [(i, (i + k) % peers) for i in range(peers)])
        for k in range(1, peers)
    ]
    return functools.reduce(jnp.add, moved, part)


def beside(shard, width):
    peers, length = lax.axis_size(SIXTEEN), shard.shape[0]
    up = [(i, (i + 1) % peers) for i in range(peers)]
    down = [(j, i) for i, j in up]
    last = lax.slice_in_dim(shard, length - width, length, axis=0)
    initial = lax.slice_in_dim(shard, 0, width, axis=0)
    shard, last, initial = lax.optimization_barrier((shard, last, initial))
    return lax.ppermute(last, SIXTEEN, up), lax.ppermute(initial, SIXTEEN, down), shard


def owned_table(group_map, owners, per_owner):
    total_strips = group_map.shape[0]
    member = (group_map[None, :] == jnp.arange(owners, dtype=jnp.int32)[:, None]).astype(jnp.int32)
    ranked = jnp.cumsum(member, axis=1, dtype=jnp.int32) - 1
    slot_hit = (ranked[:, :, None] == jnp.arange(per_owner, dtype=jnp.int32)[None, None, :]).astype(
        jnp.int32
    ) * member[:, :, None]
    numbers = jnp.arange(total_strips, dtype=jnp.int32)
    return jnp.sum(slot_hit * numbers[None, :, None], axis=1, dtype=jnp.int32)


def tile_lists(first_list, total):
    steps = jnp.arange(1, REACH + 1, dtype=jnp.int32)
    held = jnp.any(first_list[None, :] == (steps % total)[:, None], axis=1)
    missing = jnp.min(jnp.where(held, REACH + 1, steps))
    d1, d2, d3 = (k + (missing <= k).astype(jnp.int32) for k in range(1, PAIRED + 1))
    reach = d1 + d2 + d3
    t = jnp.arange(OWN_TILES + HALO_TILES, dtype=jnp.int32)
    n1, n2 = BLOCKS_DEV - d1, 2 * BLOCKS_DEV - d1 - d2
    own_count = (PAIRED + 1) * BLOCKS_DEV - reach
    p = t - BLOCKS_DEV
    pair_a = jnp.where(p < n1, p, jnp.where(p < n2, p - n1, p - n2))
    pair_b = pair_a + jnp.where(p < n1, d1, jnp.where(p < n2, d2, d3))
    q = t - OWN_TILES
    right = q >= reach
    q = jnp.where(right, q - reach, q)
    step = jnp.where(q < d1, d1, jnp.where(q < d1 + d2, d2, d3))
    pos = jnp.where(q < d1, q, jnp.where(q < d1 + d2, q - d1, q - d1 - d2))
    halo_a = jnp.where(right, BLOCKS_DEV - 1 - pos, pos)
    halo_b = jnp.where(right, BLOCKS_DEV - 1 - pos + step, pos - step)
    live = jnp.where(t < OWN_TILES, t < own_count, t < OWN_TILES + 2 * reach)
    one = jnp.where(t < BLOCKS_DEV, t, jnp.where(t < OWN_TILES, pair_a, halo_a))
    other = jnp.where(t < BLOCKS_DEV, t, jnp.where(t < OWN_TILES, pair_b, halo_b))
    one = jnp.where(live, one, 0)
    other = jnp.where(live, other, 0)
    counts = jnp.stack([own_count, 2 * reach])
    return jnp.concatenate([one, other, live.astype(jnp.int32), counts])


LISTED = OWN_TILES + HALO_TILES


def tiles_kernel(first, count, held, table_ref, rows_ref, cols_ref, *refs):
    tiles_ref, buf, sem = refs[held:]
    a, b = ROOT_THREE * CUTOFF / SPREAD, 4.0

    def out_copy(t):
        slot = lax.rem(t - first, TILE_SLOTS)
        return pltpu.make_async_copy(buf.at[slot], tiles_ref.at[t], sem.at[slot])

    def live(t):
        return table_ref[2 * LISTED + t] == 1

    def one_tile(t, carry):
        slot = lax.rem(t - first, TILE_SLOTS)
        past = jnp.maximum(t - TILE_SLOTS, first)

        @pl.when((t >= first + TILE_SLOTS) & live(past))
        def _():
            out_copy(past).wait()

        @pl.when(live(t))
        def _():
            one, other = table_ref[t], table_ref[LISTED + t]
            sill = jnp.where(one == other, (NEIGHBOURS + 1.0) * SILL_TERM, SILL_TERM)
            lane = lax.broadcasted_iota(jnp.int32, (GROUP, COL_DEV), 1)
            to = rows_ref[one + REACH]
            frm = cols_ref[other + REACH]
            for rb in range(STRIP):
                row_b = jnp.broadcast_to(frm[:, rb : rb + 1], (COL_DEV, COL_DEV))
                col_b = jnp.broadcast_to(frm[:, STRIP + rb : STRIP + rb + 1], (COL_DEV, COL_DEV))
                for u in range(COL_DEV // 2 // GROUP):
                    lo_s = slice(GROUP * u, GROUP * (u + 1))
                    hi_s = slice(64 + GROUP * u, 64 + GROUP * (u + 1))
                    near = (lane >= GROUP * u - BAND) & (lane < GROUP * (u + 1) + BAND)
                    one_m = jnp.where(near, 1.0, 0.0).astype(jnp.bfloat16)
                    other_m = jnp.where(near, 0.0, 1.0).astype(jnp.bfloat16)
                    row_s = jnp.where(near, row_b[lo_s], row_b[hi_s])
                    col_s = jnp.where(near, col_b[lo_s], col_b[hi_s])
                    for ra in range(STRIP):
                        dr = row_s - to[ra : ra + 1]
                        dc = col_s - to[STRIP + ra : STRIP + ra + 1]
                        square = dr * dr + dc * dc
                        far = square * lax.rsqrt(jnp.maximum(square, 1e-30))
                        fading = jnp.maximum(1.0 - far, 0.0)
                        fading = fading * fading
                        fading = fading * fading
                        shape = (1.0 + a * far) * (sill + (sill * b) * far)
                        value = shape * fading * jnp.exp(-a * far)
                        hi = value.astype(jnp.bfloat16)
                        lo = (value - hi.astype(jnp.float32)).astype(jnp.bfloat16)
                        lanes = slice(COL_DEV * ra, COL_DEV * (ra + 1))
                        top = rb * COL_DEV + GROUP * u
                        for part, at in ((hi, top), (lo, BLOCK + top)):
                            buf[slot, at : at + GROUP, lanes] = part * one_m
                            buf[slot, at + 64 : at + 64 + GROUP, lanes] = part * other_m
            out_copy(t).start()

        return carry

    lax.fori_loop(first, first + count, one_tile, 0)
    for t in range(max(first, first + count - TILE_SLOTS), first + count):

        @pl.when(live(t))
        def _(t=t):
            out_copy(t).wait()


def covariance_tiles(first, count, table, rows, cols, held):
    vmem, hbm = pl.BlockSpec(memory_space=pltpu.VMEM), pl.BlockSpec(memory_space=pl.ANY)
    extra = [] if held is None else [held]
    return pl.pallas_call(
        functools.partial(tiles_kernel, first, count, len(extra)),
        in_specs=[pl.BlockSpec(memory_space=pltpu.SMEM), vmem, vmem] + [hbm] * len(extra),
        out_specs=hbm,
        scratch_shapes=[
            pltpu.VMEM((TILE_SLOTS, 2 * BLOCK, BLOCK), jnp.bfloat16),
            pltpu.SemaphoreType.DMA((TILE_SLOTS,)),
        ],
        out_shape=jax.ShapeDtypeStruct((LISTED, 2 * BLOCK, BLOCK), jnp.bfloat16),
        input_output_aliases={3: 0} if extra else {},
        compiler_params=pltpu.CompilerParams(vmem_limit_bytes=32 << 20),
        cost_estimate=pl.CostEstimate(
            flops=count * 12 * BLOCK * BLOCK,
            bytes_accessed=count * 4 * BLOCK * BLOCK,
            transcendentals=count * BLOCK * BLOCK,
        ),
        name="tiles",
    )(table, rows, cols, *extra)


def halves(v):
    hi = v.astype(jnp.bfloat16)
    lo = (v - hi.astype(jnp.float32)).astype(jnp.bfloat16)
    return hi, lo


NN = (((1,), (0,)), ((), ()))
NT = (((1,), (1,)), ((), ()))


def product(both, tile_ref, dims):
    fields = both.shape[0] // 2
    main = lax.dot_general(
        both, tile_ref[:BLOCK], dims, preferred_element_type=jnp.float32
    )
    rest = lax.dot_general(
        both[:fields], tile_ref[BLOCK:], dims, preferred_element_type=jnp.float32
    )
    return main[:fields] + (main[fields:] + rest)


def tile_stream(tiles_ref, base, buf, sem):
    def copy(t):
        slot = lax.rem(t, OP_SLOTS)
        return pltpu.make_async_copy(tiles_ref.at[base + t], buf.at[slot], sem.at[slot])

    return copy


def own_kernel(table_ref, v_ref, tiles_ref, out_ref, both_ref, buf, sem):
    fields = v_ref.shape[1]
    count = table_ref[3 * LISTED]
    copy = tile_stream(tiles_ref, 0, buf, sem)
    for t in range(OP_SLOTS - 1):
        copy(t).start()
    for g in range(BLOCKS_DEV):
        hi, lo = halves(v_ref[g])
        both_ref[g, :fields] = hi
        both_ref[g, fields:] = lo

    def arrive(t):
        @pl.when(t + OP_SLOTS - 1 < count)
        def _():
            copy(t + OP_SLOTS - 1).start()

        copy(t).wait()
        return buf.at[lax.rem(t, OP_SLOTS)]

    def with_itself(t, carry):
        tile = arrive(t)
        out_ref[t] = product(both_ref[t], tile, NN)
        return carry

    def with_another(t, carry):
        tile = arrive(t)
        one, other = table_ref[t], table_ref[LISTED + t]
        out_ref[one] += product(both_ref[other], tile, NN)
        out_ref[other] += product(both_ref[one], tile, NT)
        return carry

    lax.fori_loop(0, BLOCKS_DEV, with_itself, 0)
    lax.fori_loop(BLOCKS_DEV, count, with_another, 0)


def halo_kernel(
    table_ref, target_ref, before_ref, after_ref, part_ref, tiles_ref, out_ref, *refs
):
    *slots_ref, both_ref, buf, sem, out_sem = refs
    fields = before_ref.shape[1]
    count = table_ref[3 * LISTED + 1]
    copy = tile_stream(tiles_ref, OWN_TILES, buf, sem)
    for t in range(OP_SLOTS - 1):
        copy(t).start()
    for side, ref in enumerate((before_ref, after_ref)):
        for g in range(REACH):
            hi, lo = halves(ref[g])
            both_ref[side * REACH + g, :fields] = hi
            both_ref[side * REACH + g, fields:] = lo
    out_ref[...] = part_ref[...]

    def with_beside(t, carry):
        @pl.when(t + OP_SLOTS - 1 < count)
        def _():
            copy(t + OP_SLOTS - 1).start()

        copy(t).wait()
        one, other = table_ref[OWN_TILES + t], table_ref[LISTED + OWN_TILES + t]
        side = jnp.where(other < 0, other + REACH, other - BLOCKS_DEV + REACH)
        out_ref[one] += product(both_ref[side], buf.at[lax.rem(t, OP_SLOTS)], NN)
        return carry

    lax.fori_loop(0, count, with_beside, 0)
    if slots_ref:
        sent = out_copies(out_ref, slots_ref[0], target_ref, out_sem)
        for copy_out in sent:
            copy_out.start()
        for copy_out in sent:
            copy_out.wait()


def out_copies(values_ref, slots_ref, target_ref, sem):
    return [
        pltpu.make_async_copy(values_ref.at[g], slots_ref.at[target_ref[g]], sem.at[g])
        for g in range(BLOCKS_DEV)
    ]


SMEM_SPEC = pl.BlockSpec(memory_space=pltpu.SMEM)
VMEM_SPEC = pl.BlockSpec(memory_space=pltpu.VMEM)
HBM_SPEC = pl.BlockSpec(memory_space=pltpu.HBM)


def stream_scratch():
    return [
        pltpu.VMEM((OP_SLOTS, 2 * BLOCK, BLOCK), jnp.bfloat16),
        pltpu.SemaphoreType.DMA((OP_SLOTS,)),
    ]


def slot_shape(v):
    return pltpu.HBM((lax.axis_size(SIXTEEN), *v.shape[1:]), jnp.float32)


def product_cost(tiles, products, fields):
    return pl.CostEstimate(
        flops=products * 3 * 2 * fields * BLOCK * BLOCK,
        bytes_accessed=tiles * 4 * BLOCK * BLOCK,
        transcendentals=0,
    )


def own_product(table, v, tiles):
    blocks, fields, _ = v.shape
    return pl.pallas_call(
        own_kernel,
        in_specs=[SMEM_SPEC, VMEM_SPEC, HBM_SPEC],
        out_specs=VMEM_SPEC,
        scratch_shapes=[pltpu.VMEM((blocks, 2 * fields, BLOCK), jnp.bfloat16)] + stream_scratch(),
        out_shape=jax.ShapeDtypeStruct(v.shape, jnp.float32),
        compiler_params=pltpu.CompilerParams(vmem_limit_bytes=32 << 20),
        cost_estimate=product_cost(OWN_TILES, 42, fields),
        name="own",
    )(table, v, tiles)


def spread_kernel(target_ref, v_ref, *refs):
    slots_ref, sem = refs[-2:]
    sent = out_copies(v_ref, slots_ref, target_ref, sem)
    for copy_out in sent:
        copy_out.start()
    for copy_out in sent:
        copy_out.wait()


def spread(targets, v, *behind):
    return pl.pallas_call(
        spread_kernel,
        in_specs=[SMEM_SPEC] + [VMEM_SPEC] * (1 + len(behind)),
        out_specs=HBM_SPEC,
        scratch_shapes=[pltpu.SemaphoreType.DMA((BLOCKS_DEV,))],
        out_shape=slot_shape(v),
        name="spread",
    )(targets, v, *behind)


def halo_product(table, targets, before, after, part, tiles, send):
    blocks, fields, _ = part.shape
    out = pl.pallas_call(
        halo_kernel,
        in_specs=[SMEM_SPEC, SMEM_SPEC, VMEM_SPEC, VMEM_SPEC, VMEM_SPEC, HBM_SPEC],
        out_specs=[VMEM_SPEC] + [HBM_SPEC] * send,
        scratch_shapes=[pltpu.VMEM((2 * REACH, 2 * fields, BLOCK), jnp.bfloat16)]
        + stream_scratch()
        + [pltpu.SemaphoreType.DMA((BLOCKS_DEV,))],
        out_shape=[jax.ShapeDtypeStruct(part.shape, jnp.float32)] + [slot_shape(part)] * send,
        compiler_params=pltpu.CompilerParams(vmem_limit_bytes=32 << 20),
        cost_estimate=product_cost(HALO_TILES, HALO_TILES, fields),
        name="halo",
    )(table, targets, before, after, part, tiles)
    return out if send else out[0]


def residual_kernel(obs_ref, weight_ref, row_ref, col_ref, out_ref):
    col = col_ref[...]
    for g in range(BLOCKS_DEV):
        for ra in range(STRIP):
            r = STRIP * g + ra
            left = obs_ref[:, r, :] - row_ref[:, r : r + 1] - col
            out_ref[g, :, COL_DEV * ra : COL_DEV * (ra + 1)] = weight_ref[r : r + 1, :] * left


def residual_of(observations, weight, row_effect, col_effect):
    fields = observations.shape[0]
    return pl.pallas_call(
        residual_kernel,
        in_specs=[VMEM_SPEC] * 4,
        out_specs=VMEM_SPEC,
        out_shape=jax.ShapeDtypeStruct((BLOCKS_DEV, fields, BLOCK), jnp.float32),
        compiler_params=pltpu.CompilerParams(vmem_limit_bytes=32 << 20),
        name="residual",
    )(observations, weight, row_effect, col_effect)


def combine_kernel(src_ref, scale_ref, *refs):
    ins, (x_ref, r_ref) = refs[:-2], refs[-2:]
    scale = scale_ref[...]
    for j in range(BLOCKS_DEV):
        r0, m1, m2 = (ref[0] for ref in ins[3 * j : 3 * j + 3])
        x_ref[:, j, :] = scale[:, 0:1] * r0 + scale[:, 1:2] * m1
        r_ref[:, j, :] = scale[:, 2:3] * r0 + scale[:, 3:4] * m1 + scale[:, 4:5] * m2


def combined(sources, scale, r0, m1, m2):
    fields = r0.shape[1]
    part = 16
    ins, specs = [], []
    for j in range(BLOCKS_DEV):
        for v in (r0, m1, m2):
            ins.append(v)
            specs.append(
                pl.BlockSpec(
                    (1, part, BLOCK), functools.partial(lambda j, i, s: (s[j], i, 0), j)
                )
            )
    out = pl.BlockSpec((part, BLOCKS_DEV, BLOCK), lambda i, s: (i, 0, 0))
    shape = jax.ShapeDtypeStruct((fields, BLOCKS_DEV, BLOCK), jnp.float32)
    return pl.pallas_call(
        combine_kernel,
        grid_spec=pltpu.PrefetchScalarGridSpec(
            num_scalar_prefetch=1,
            grid=(fields // part,),
            in_specs=[pl.BlockSpec((part, 8), lambda i, s: (i, 0))] + specs,
            out_specs=[out, out],
        ),
        out_shape=[shape, shape],
        compiler_params=pltpu.CompilerParams(vmem_limit_bytes=32 << 20),
        name="combine",
    )(sources, scale, *ins)


def to_owners(slots):
    return lax.all_to_all(slots, SIXTEEN, 0, 0, tiled=True)


def step_scales(h00, h01, h11, h12):
    mu = h01 / h00
    var = (h11 - mu * h01) / h00
    a0 = 1.0 / (1.0 + mu)
    beta = var * a0 * a0
    skew = (h12 - mu * h11 - mu * (h11 - mu * h01)) / h00
    a1 = var / (var + skew - var * var * a0)
    x_r0 = a0 + a1 * beta + a1 * a0 * mu
    x_m1 = -a1 * a0
    r_r0 = a0 * mu * (1.0 - a1) - a1 * beta
    r_m1 = -a0 * (1.0 - a1) - a1 * a0 * mu - a1 * beta
    r_m2 = a1 * a0
    zero = jnp.zeros_like(mu)
    return jnp.stack([x_r0, x_m1, r_r0, r_m1, r_m2, zero, zero, zero], axis=1)


def on_device(observations, huber_scale, observed, jitter, owner_map, neighbours):
    fields, row_dev, col_dev = observations.shape
    sixteen_size = lax.axis_size(SIXTEEN)
    my_place = lax.axis_index(SIXTEEN)
    group_place = lax.axis_index(WIDE)
    total_strips = BLOCKS_DEV * sixteen_size
    weight = observed.astype(jnp.float32)
    spread_scale = huber_scale[:, None, None]

    def with_count(part, count):
        rows = jnp.zeros((8, count.shape[0]), jnp.float32).at[0].set(count)
        return jnp.concatenate([part, rows], axis=0)

    def terms(row_effect, col_effect):
        return weight[None] * jnp.clip(
            (observations - row_effect[:, :, None] - col_effect[:, None, :]) / spread_scale,
            -HUBER_EDGE,
            HUBER_EDGE,
        )

    row_effect = jnp.zeros((fields, row_dev), jnp.float32)
    col_effect = jnp.zeros((fields, col_dev), jnp.float32)
    part = with_count(jnp.sum(terms(row_effect, col_effect), axis=2), jnp.sum(weight, axis=1))
    part, jitter, owner_map, neighbours = lax.optimization_barrier(
        (part, jitter, owner_map, neighbours)
    )

    group_map = owner_map[0]
    group_lists = neighbours[0]
    owned = owned_table(group_map, sixteen_size, BLOCKS_DEV)
    my_ids = lax.dynamic_index_in_dim(owned, my_place, 0, keepdims=False)
    sources = my_ids // BLOCKS_DEV
    my_targets = lax.dynamic_slice_in_dim(group_map, my_place * BLOCKS_DEV, BLOCKS_DEV)
    table = tile_lists(group_lists[0], total_strips)
    row_place = (my_place * row_dev + jnp.arange(row_dev, dtype=jnp.int32)).astype(jnp.float32)
    col_place = (group_place * col_dev + jnp.arange(col_dev, dtype=jnp.int32)).astype(jnp.float32)
    location = jnp.stack(
        [row_place[:, None] + jitter[0], col_place[None, :] + jitter[1]], axis=0
    ).reshape(2, BLOCKS_DEV, STRIP, col_dev)
    location = location.transpose(1, 0, 2, 3).reshape(BLOCKS_DEV, 2 * STRIP, col_dev)
    location = location * (1.0 / CUTOFF)
    none = jnp.zeros((REACH, 2 * STRIP, col_dev), jnp.float32)
    here = jnp.concatenate([none, location, none], axis=0)
    here = (here, here.transpose(0, 2, 1))

    def beside_tiles(part, axis, places, count, tiles, first):
        if first:
            part, places, tiles = lax.optimization_barrier((part, places, tiles))
        total = over_copies(part, axis)
        tiles = covariance_tiles(first, count, table, *places, tiles)
        total, tiles = lax.optimization_barrier((total, tiles))
        return total, tiles, first + count

    total, tiles, first = beside_tiles(part, WIDE, here, ROW_TILES, None, 0)
    total, table, here = lax.optimization_barrier((total, table, here))
    row_count = jnp.maximum(total[fields], 1.0)
    row_effect = huber_scale[:, None] * total[:fields] / row_count[None, :]
    part = with_count(jnp.sum(terms(row_effect, col_effect), axis=1), jnp.sum(weight, axis=0))
    before, after, location = beside(location, REACH)
    total, tiles, first = beside_tiles(part, SIXTEEN, here, COL_TILES, tiles, first)
    total, before, after = lax.optimization_barrier((total, before, after))
    wider = jnp.concatenate([before, location, after], axis=0)
    wider = (wider, wider.transpose(0, 2, 1))
    col_count = jnp.maximum(total[fields], 1.0)
    col_effect = huber_scale[:, None] * total[:fields] / col_count[None, :]
    part = jnp.sum(terms(row_effect, col_effect), axis=2)
    total, tiles, first = beside_tiles(part, WIDE, wider, ROW_TILES, tiles, first)
    row_effect = row_effect + huber_scale[:, None] * total / row_count[None, :]
    part = jnp.sum(terms(row_effect, col_effect), axis=1)
    total, tiles, first = beside_tiles(part, SIXTEEN, wider, COL_TILES, tiles, first)
    col_effect = col_effect + huber_scale[:, None] * total / col_count[None, :]

    r0 = residual_of(observations, weight, row_effect, col_effect)
    before, after, r0 = beside(r0, REACH)
    part = own_product(table, r0, tiles)
    slots = spread(my_targets, r0, part, before, after)
    owned_r0 = to_owners(slots)
    m1 = halo_product(table, my_targets, before, after, part, tiles, False)
    before, after, m1 = beside(m1, REACH)
    part = own_product(table, m1, tiles)
    slots = spread(my_targets, m1, part, before, after)
    slots, owned_r0 = lax.optimization_barrier((slots, owned_r0))
    owned_m1 = to_owners(slots)
    m2, slots = halo_product(table, my_targets, before, after, part, tiles, True)
    dots = jnp.stack(
        [jnp.sum(p * q, axis=(0, 2)) for p, q in ((r0, r0), (r0, m1), (m1, m1), (m1, m2))]
    )
    slots, owned_m1 = lax.optimization_barrier((slots, owned_m1))
    owned_m2 = to_owners(slots)
    for axis in WIDE[::-1] + SIXTEEN[::-1]:
        dots = sum_direct(dots, axis)
    scale = step_scales(*dots)
    solution_now, residual_now = combined(sources, scale, owned_r0, owned_m1, owned_m2)
    return (solution_now[None, None], residual_now[None, None])


def solution(mesh):
    finer = Mesh(mesh.devices.reshape(4, 2, 4, 4), ("wide_0", "wide_1", "sixteen_0", "sixteen_1"))
    in_specs = (
        P(None, SIXTEEN, WIDE),
        P(),
        P(SIXTEEN, WIDE),
        P(None, SIXTEEN, WIDE),
        P(WIDE, None),
        P(WIDE, None, None),
    )
    out_specs = (P(WIDE, SIXTEEN, None, None, None), P(WIDE, SIXTEEN, None, None, None))
    return jax.shard_map(
        on_device, mesh=finer, in_specs=in_specs, out_specs=out_specs, check_vma=False
    )
```

```python
import functools

import jax
import jax.numpy as jnp
from jax import lax
from jax.experimental import pallas as pl
from jax.experimental.pallas import tpu as pltpu
from jax.sharding import Mesh
from jax.sharding import PartitionSpec as P

BLOCK = 512
BLOCKS_DEV = 8
REACH = 4
NEIGHBOURS = 6
PAIRED = NEIGHBOURS // 2
SWEEPS = 2
STRIP = 4
COL_DEV = 128
WIDE = ("wide_0", "wide_1")
SIXTEEN = ("sixteen_0", "sixteen_1")

HUBER_EDGE = 1.345
SILL_TERM = 0.02
ROOT_THREE = 1.7320508075688772
SPREAD = 2.0 * STRIP
CUTOFF = 6.0 * STRIP
BAND = 24
GROUP = 16

OWN_TILES = BLOCKS_DEV + PAIRED * BLOCKS_DEV - 6
HALO_TILES = 2 * (2 + 3 + 4)
ROW_TILES, COL_TILES = 13, 9
TILE_SLOTS = 4
OP_SLOTS = 5


def sent_to_all(shard, axis):
    peers = lax.axis_size(axis)
    return lax.all_to_all(
        jnp.broadcast_to(shard[None], (peers, *shard.shape)), axis, 0, 0, tiled=True
    )


def over_copies(shard, axis):
    return jnp.sum(sent_to_all(shard, axis), axis=0)


def sum_direct(part, axis):
    peers = lax.axis_size(axis)
    moved = [
        lax.ppermute(part, axis, [(i, (i + k) % peers) for i in range(peers)])
        for k in range(1, peers)
    ]
    return functools.reduce(jnp.add, moved, part)


def beside(shard, width):
    peers, length = lax.axis_size(SIXTEEN), shard.shape[0]
    up = [(i, (i + 1) % peers) for i in range(peers)]
    down = [(j, i) for i, j in up]
    last = lax.slice_in_dim(shard, length - width, length, axis=0)
    initial = lax.slice_in_dim(shard, 0, width, axis=0)
    shard, last, initial = lax.optimization_barrier((shard, last, initial))
    return lax.ppermute(last, SIXTEEN, up), lax.ppermute(initial, SIXTEEN, down), shard


def owned_table(group_map, owners, per_owner):
    total_strips = group_map.shape[0]
    member = (group_map[None, :] == jnp.arange(owners, dtype=jnp.int32)[:, None]).astype(jnp.int32)
    ranked = jnp.cumsum(member, axis=1, dtype=jnp.int32) - 1
    slot_hit = (ranked[:, :, None] == jnp.arange(per_owner, dtype=jnp.int32)[None, None, :]).astype(
        jnp.int32
    ) * member[:, :, None]
    numbers = jnp.arange(total_strips, dtype=jnp.int32)
    return jnp.sum(slot_hit * numbers[None, :, None], axis=1, dtype=jnp.int32)


def tile_lists(first_list, total):
    steps = jnp.arange(1, REACH + 1, dtype=jnp.int32)
    held = jnp.any(first_list[None, :] == (steps % total)[:, None], axis=1)
    missing = jnp.min(jnp.where(held, REACH + 1, steps))
    d1, d2, d3 = (k + (missing <= k).astype(jnp.int32) for k in range(1, PAIRED + 1))
    reach = d1 + d2 + d3
    t = jnp.arange(OWN_TILES + HALO_TILES, dtype=jnp.int32)
    n1, n2 = BLOCKS_DEV - d1, 2 * BLOCKS_DEV - d1 - d2
    own_count = (PAIRED + 1) * BLOCKS_DEV - reach
    p = t - BLOCKS_DEV
    pair_a = jnp.where(p < n1, p, jnp.where(p < n2, p - n1, p - n2))
    pair_b = pair_a + jnp.where(p < n1, d1, jnp.where(p < n2, d2, d3))
    q = t - OWN_TILES
    right = q >= reach
    q = jnp.where(right, q - reach, q)
    step = jnp.where(q < d1, d1, jnp.where(q < d1 + d2, d2, d3))
    pos = jnp.where(q < d1, q, jnp.where(q < d1 + d2, q - d1, q - d1 - d2))
    halo_a = jnp.where(right, BLOCKS_DEV - 1 - pos, pos)
    halo_b = jnp.where(right, BLOCKS_DEV - 1 - pos + step, pos - step)
    live = jnp.where(t < OWN_TILES, t < own_count, t < OWN_TILES + 2 * reach)
    one = jnp.where(t < BLOCKS_DEV, t, jnp.where(t < OWN_TILES, pair_a, halo_a))
    other = jnp.where(t < BLOCKS_DEV, t, jnp.where(t < OWN_TILES, pair_b, halo_b))
    one = jnp.where(live, one, 0)
    other = jnp.where(live, other, 0)
    counts = jnp.stack([own_count, 2 * reach])
    return jnp.concatenate([one, other, live.astype(jnp.int32), counts])


LISTED = OWN_TILES + HALO_TILES


def tiles_kernel(first, count, held, table_ref, rows_ref, cols_ref, *refs):
    tiles_ref, buf, sem = refs[held:]
    a, b = ROOT_THREE * CUTOFF / SPREAD, 4.0

    def out_copy(t):
        slot = lax.rem(t - first, TILE_SLOTS)
        return pltpu.make_async_copy(buf.at[slot], tiles_ref.at[t], sem.at[slot])

    def live(t):
        return table_ref[2 * LISTED + t] == 1

    def one_tile(t, carry):
        slot = lax.rem(t - first, TILE_SLOTS)
        past = jnp.maximum(t - TILE_SLOTS, first)

        @pl.when((t >= first + TILE_SLOTS) & live(past))
        def _():
            out_copy(past).wait()

        @pl.when(live(t))
        def _():
            one, other = table_ref[t], table_ref[LISTED + t]
            sill = jnp.where(one == other, (NEIGHBOURS + 1.0) * SILL_TERM, SILL_TERM)
            lane = lax.broadcasted_iota(jnp.int32, (GROUP, COL_DEV), 1)
            to = rows_ref[one + REACH]
            frm = cols_ref[other + REACH]
            for rb in range(STRIP):
                row_b = jnp.broadcast_to(frm[:, rb : rb + 1], (COL_DEV, COL_DEV))
                col_b = jnp.broadcast_to(frm[:, STRIP + rb : STRIP + rb + 1], (COL_DEV, COL_DEV))
                for u in range(COL_DEV // 2 // GROUP):
                    lo_s = slice(GROUP * u, GROUP * (u + 1))
                    hi_s = slice(64 + GROUP * u, 64 + GROUP * (u + 1))
                    near = (lane >= GROUP * u - BAND) & (lane < GROUP * (u + 1) + BAND)
                    one_m = jnp.where(near, 1.0, 0.0).astype(jnp.bfloat16)
                    other_m = jnp.where(near, 0.0, 1.0).astype(jnp.bfloat16)
                    row_s = jnp.where(near, row_b[lo_s], row_b[hi_s])
                    col_s = jnp.where(near, col_b[lo_s], col_b[hi_s])
                    for ra in range(STRIP):
                        dr = row_s - to[ra : ra + 1]
                        dc = col_s - to[STRIP + ra : STRIP + ra + 1]
                        square = dr * dr + dc * dc
                        far = square * lax.rsqrt(jnp.maximum(square, 1e-30))
                        fading = jnp.maximum(1.0 - far, 0.0)
                        fading = fading * fading
                        fading = fading * fading
                        shape = (1.0 + a * far) * (sill + (sill * b) * far)
                        value = shape * fading * jnp.exp(-a * far)
                        hi = value.astype(jnp.bfloat16)
                        lo = (value - hi.astype(jnp.float32)).astype(jnp.bfloat16)
                        lanes = slice(COL_DEV * ra, COL_DEV * (ra + 1))
                        top = rb * COL_DEV + GROUP * u
                        for part, at in ((hi, top), (lo, BLOCK + top)):
                            buf[slot, at : at + GROUP, lanes] = part * one_m
                            buf[slot, at + 64 : at + 64 + GROUP, lanes] = part * other_m
            out_copy(t).start()

        return carry

    lax.fori_loop(first, first + count, one_tile, 0)
    for t in range(max(first, first + count - TILE_SLOTS), first + count):

        @pl.when(live(t))
        def _(t=t):
            out_copy(t).wait()


def covariance_tiles(first, count, table, rows, cols, held):
    vmem, hbm = pl.BlockSpec(memory_space=pltpu.VMEM), pl.BlockSpec(memory_space=pl.ANY)
    extra = [] if held is None else [held]
    return pl.pallas_call(
        functools.partial(tiles_kernel, first, count, len(extra)),
        in_specs=[pl.BlockSpec(memory_space=pltpu.SMEM), vmem, vmem] + [hbm] * len(extra),
        out_specs=hbm,
        scratch_shapes=[
            pltpu.VMEM((TILE_SLOTS, 2 * BLOCK, BLOCK), jnp.bfloat16),
            pltpu.SemaphoreType.DMA((TILE_SLOTS,)),
        ],
        out_shape=jax.ShapeDtypeStruct((LISTED, 2 * BLOCK, BLOCK), jnp.bfloat16),
        input_output_aliases={3: 0} if extra else {},
        compiler_params=pltpu.CompilerParams(vmem_limit_bytes=12 << 20),
        cost_estimate=pl.CostEstimate(
            flops=count * 12 * BLOCK * BLOCK,
            bytes_accessed=count * 4 * BLOCK * BLOCK,
            transcendentals=count * BLOCK * BLOCK,
        ),
        name="tiles",
    )(table, rows, cols, *extra)


def halves(v):
    hi = v.astype(jnp.bfloat16)
    lo = (v - hi.astype(jnp.float32)).astype(jnp.bfloat16)
    return hi, lo


NN = (((1,), (0,)), ((), ()))
NT = (((1,), (1,)), ((), ()))


def product(both, tile_ref, dims):
    fields = both.shape[0] // 2
    main = lax.dot_general(
        both, tile_ref[:BLOCK], dims, preferred_element_type=jnp.float32
    )
    rest = lax.dot_general(
        both[:fields], tile_ref[BLOCK:], dims, preferred_element_type=jnp.float32
    )
    return main[:fields] + (main[fields:] + rest)


def tile_stream(tiles_ref, base, buf, sem):
    def copy(t):
        slot = lax.rem(t, OP_SLOTS)
        return pltpu.make_async_copy(tiles_ref.at[base + t], buf.at[slot], sem.at[slot])

    return copy


def own_kernel(table_ref, v_ref, tiles_ref, out_ref, both_ref, buf, sem):
    fields = v_ref.shape[1]
    count = table_ref[3 * LISTED]
    copy = tile_stream(tiles_ref, 0, buf, sem)
    for t in range(OP_SLOTS - 1):
        copy(t).start()
    for g in range(BLOCKS_DEV):
        hi, lo = halves(v_ref[g])
        both_ref[g, :fields] = hi
        both_ref[g, fields:] = lo

    def arrive(t):
        @pl.when(t + OP_SLOTS - 1 < count)
        def _():
            copy(t + OP_SLOTS - 1).start()

        copy(t).wait()
        return buf.at[lax.rem(t, OP_SLOTS)]

    def with_itself(t, carry):
        tile = arrive(t)
        out_ref[t] = product(both_ref[t], tile, NN)
        return carry

    def with_another(t, carry):
        tile = arrive(t)
        one, other = table_ref[t], table_ref[LISTED + t]
        out_ref[one] += product(both_ref[other], tile, NN)
        out_ref[other] += product(both_ref[one], tile, NT)
        return carry

    lax.fori_loop(0, BLOCKS_DEV, with_itself, 0)
    lax.fori_loop(BLOCKS_DEV, count, with_another, 0)


def halo_kernel(
    table_ref, target_ref, before_ref, after_ref, part_ref, tiles_ref, out_ref, *refs
):
    *slots_ref, both_ref, buf, sem, out_sem = refs
    fields = before_ref.shape[1]
    count = table_ref[3 * LISTED + 1]
    copy = tile_stream(tiles_ref, OWN_TILES, buf, sem)
    for t in range(OP_SLOTS - 1):
        copy(t).start()
    for side, ref in enumerate((before_ref, after_ref)):
        for g in range(REACH):
            hi, lo = halves(ref[g])
            both_ref[side * REACH + g, :fields] = hi
            both_ref[side * REACH + g, fields:] = lo
    out_ref[...] = part_ref[...]

    def with_beside(t, carry):
        @pl.when(t + OP_SLOTS - 1 < count)
        def _():
            copy(t + OP_SLOTS - 1).start()

        copy(t).wait()
        one, other = table_ref[OWN_TILES + t], table_ref[LISTED + OWN_TILES + t]
        side = jnp.where(other < 0, other + REACH, other - BLOCKS_DEV + REACH)
        out_ref[one] += product(both_ref[side], buf.at[lax.rem(t, OP_SLOTS)], NN)
        return carry

    lax.fori_loop(0, count, with_beside, 0)
    if slots_ref:
        sent = out_copies(out_ref, slots_ref[0], target_ref, out_sem)
        for copy_out in sent:
            copy_out.start()
        for copy_out in sent:
            copy_out.wait()


def out_copies(values_ref, slots_ref, target_ref, sem):
    return [
        pltpu.make_async_copy(values_ref.at[g], slots_ref.at[target_ref[g]], sem.at[g])
        for g in range(BLOCKS_DEV)
    ]


SMEM_SPEC = pl.BlockSpec(memory_space=pltpu.SMEM)
VMEM_SPEC = pl.BlockSpec(memory_space=pltpu.VMEM)
HBM_SPEC = pl.BlockSpec(memory_space=pltpu.HBM)


def stream_scratch():
    return [
        pltpu.VMEM((OP_SLOTS, 2 * BLOCK, BLOCK), jnp.bfloat16),
        pltpu.SemaphoreType.DMA((OP_SLOTS,)),
    ]


def slot_shape(v):
    return pltpu.HBM((lax.axis_size(SIXTEEN), *v.shape[1:]), jnp.float32)


def product_cost(tiles, products, fields):
    return pl.CostEstimate(
        flops=products * 3 * 2 * fields * BLOCK * BLOCK,
        bytes_accessed=tiles * 4 * BLOCK * BLOCK,
        transcendentals=0,
    )


def own_product(table, v, tiles):
    blocks, fields, _ = v.shape
    return pl.pallas_call(
        own_kernel,
        in_specs=[SMEM_SPEC, VMEM_SPEC, HBM_SPEC],
        out_specs=VMEM_SPEC,
        scratch_shapes=[pltpu.VMEM((blocks, 2 * fields, BLOCK), jnp.bfloat16)] + stream_scratch(),
        out_shape=jax.ShapeDtypeStruct(v.shape, jnp.float32),
        compiler_params=pltpu.CompilerParams(vmem_limit_bytes=12 << 20),
        cost_estimate=product_cost(OWN_TILES, 42, fields),
        name="own",
    )(table, v, tiles)


def spread_kernel(target_ref, v_ref, *refs):
    slots_ref, sem = refs[-2:]
    sent = out_copies(v_ref, slots_ref, target_ref, sem)
    for copy_out in sent:
        copy_out.start()
    for copy_out in sent:
        copy_out.wait()


def spread(targets, v, *others):
    behind = [functools.reduce(jnp.add, [other[0, :8, :COL_DEV] for other in others])]
    return pl.pallas_call(
        spread_kernel,
        in_specs=[SMEM_SPEC] + [VMEM_SPEC] * (1 + len(behind)),
        out_specs=HBM_SPEC,
        scratch_shapes=[pltpu.SemaphoreType.DMA((BLOCKS_DEV,))],
        out_shape=slot_shape(v),
        compiler_params=pltpu.CompilerParams(vmem_limit_bytes=1 << 20),
        name="spread",
    )(targets, v, *behind)


def halo_product(table, targets, before, after, part, tiles, send):
    blocks, fields, _ = part.shape
    out = pl.pallas_call(
        halo_kernel,
        in_specs=[SMEM_SPEC, SMEM_SPEC, VMEM_SPEC, VMEM_SPEC, VMEM_SPEC, HBM_SPEC],
        out_specs=[VMEM_SPEC] + [HBM_SPEC] * send,
        scratch_shapes=[pltpu.VMEM((2 * REACH, 2 * fields, BLOCK), jnp.bfloat16)]
        + stream_scratch()
        + [pltpu.SemaphoreType.DMA((BLOCKS_DEV,))],
        out_shape=[jax.ShapeDtypeStruct(part.shape, jnp.float32)] + [slot_shape(part)] * send,
        compiler_params=pltpu.CompilerParams(vmem_limit_bytes=12 << 20),
        cost_estimate=product_cost(HALO_TILES, HALO_TILES, fields),
        name="halo",
    )(table, targets, before, after, part, tiles)
    return out if send else out[0]


def residual_kernel(obs_ref, weight_ref, row_ref, col_ref, out_ref):
    col = col_ref[...]
    for g in range(BLOCKS_DEV):
        for ra in range(STRIP):
            r = STRIP * g + ra
            left = obs_ref[:, r, :] - row_ref[:, r : r + 1] - col
            out_ref[g, :, COL_DEV * ra : COL_DEV * (ra + 1)] = weight_ref[r : r + 1, :] * left


def residual_of(observations, weight, row_effect, col_effect):
    fields = observations.shape[0]
    return pl.pallas_call(
        residual_kernel,
        in_specs=[VMEM_SPEC] * 4,
        out_specs=VMEM_SPEC,
        out_shape=jax.ShapeDtypeStruct((BLOCKS_DEV, fields, BLOCK), jnp.float32),
        compiler_params=pltpu.CompilerParams(vmem_limit_bytes=8 << 20),
        name="residual",
    )(observations, weight, row_effect, col_effect)


def observed_kernel(target_ref, obs_ref, one_ref, two_ref, buf, sem):
    half = obs_ref.shape[0] // 2
    for g in range(BLOCKS_DEV):
        for ra in range(STRIP):
            lanes = slice(COL_DEV * ra, COL_DEV * (ra + 1))
            buf[g, :, lanes] = obs_ref[:, STRIP * g + ra, :]
        for side, slots_ref in enumerate((one_ref, two_ref)):
            pltpu.make_async_copy(
                buf.at[g, pl.ds(half * side, half)], slots_ref.at[target_ref[g]], sem.at[side, g]
            ).start()
    for g in range(BLOCKS_DEV):
        for side, slots_ref in enumerate((one_ref, two_ref)):
            pltpu.make_async_copy(
                buf.at[g, pl.ds(half * side, half)], slots_ref.at[target_ref[g]], sem.at[side, g]
            ).wait()


def observed_slots(targets, observations):
    fields = observations.shape[0]
    shape = pltpu.HBM((lax.axis_size(SIXTEEN), fields // 2, BLOCK), jnp.float32)
    return pl.pallas_call(
        observed_kernel,
        in_specs=[SMEM_SPEC, VMEM_SPEC],
        out_specs=[HBM_SPEC] * 2,
        scratch_shapes=[
            pltpu.VMEM((BLOCKS_DEV, fields, BLOCK), jnp.float32),
            pltpu.SemaphoreType.DMA((2, BLOCKS_DEV)),
        ],
        out_shape=[shape] * 2,
        compiler_params=pltpu.CompilerParams(vmem_limit_bytes=12 << 20),
        name="observed",
    )(targets, observations)


def combine_kernel(src_ref, scale_ref, col_ref, weight_ref, row_ref, *refs):
    ins, (x_ref, r_ref) = refs[:-2], refs[-2:]

    def with_half(half):
        for j in range(BLOCKS_DEV):
            obs_ref, m1_ref, m2_ref = ins[4 * j + half], ins[4 * j + 2], ins[4 * j + 3]
            for ra in range(STRIP):
                lanes = slice(COL_DEV * ra, COL_DEV * (ra + 1))
                left = obs_ref[0, :, lanes] - row_ref[j, :, ra : ra + 1] - col_ref[...]
                r0 = weight_ref[j : j + 1, lanes] * left
                m1, m2 = m1_ref[0, :, lanes], m2_ref[0, :, lanes]
                x_ref[:, j, lanes] = scale_ref[:, 0:1] * r0 + scale_ref[:, 1:2] * m1
                r_ref[:, j, lanes] = (
                    scale_ref[:, 2:3] * r0 + scale_ref[:, 3:4] * m1 + scale_ref[:, 4:5] * m2
                )

    for half in range(2):
        pl.when(pl.program_id(0) == half)(functools.partial(with_half, half))


def combined(sources, scale, col_effect, weight, rows, obs_one, obs_two, m1, m2):
    fields = m2.shape[1]
    part = fields // 2
    ins, specs = [], []

    def chosen(j, at):
        return pl.BlockSpec((1, part, BLOCK), lambda i, s: (s[j], at(i), 0))

    for j in range(BLOCKS_DEV):
        ins += [obs_one, obs_two, m1, m2]
        specs += [chosen(j, lambda i: 0)] * 2 + [chosen(j, lambda i: i)] * 2
    out = pl.BlockSpec((part, BLOCKS_DEV, BLOCK), lambda i, s: (i, 0, 0))
    shape = jax.ShapeDtypeStruct((fields, BLOCKS_DEV, BLOCK), jnp.float32)
    by_field = lambda lanes: pl.BlockSpec((part, lanes), lambda i, s: (i, 0))
    return pl.pallas_call(
        combine_kernel,
        grid_spec=pltpu.PrefetchScalarGridSpec(
            num_scalar_prefetch=1,
            grid=(2,),
            in_specs=[
                by_field(8),
                by_field(COL_DEV),
                pl.BlockSpec(weight.shape, lambda i, s: (0, 0)),
                pl.BlockSpec((BLOCKS_DEV, part, STRIP), lambda i, s: (0, i, 0)),
            ]
            + specs,
            out_specs=[out, out],
        ),
        out_shape=[shape, shape],
        compiler_params=pltpu.CompilerParams(vmem_limit_bytes=20 << 20),
        name="combine",
    )(sources, scale, col_effect, weight, rows, *ins)


def to_owners(slots):
    return lax.all_to_all(slots, SIXTEEN, 0, 0, tiled=True)


def step_scales(h00, h01, h11, h12):
    mu = h01 / h00
    var = (h11 - mu * h01) / h00
    a0 = 1.0 / (1.0 + mu)
    beta = var * a0 * a0
    skew = (h12 - mu * h11 - mu * (h11 - mu * h01)) / h00
    a1 = var / (var + skew - var * var * a0)
    x_r0 = a0 + a1 * beta + a1 * a0 * mu
    x_m1 = -a1 * a0
    r_r0 = a0 * mu * (1.0 - a1) - a1 * beta
    r_m1 = -a0 * (1.0 - a1) - a1 * a0 * mu - a1 * beta
    r_m2 = a1 * a0
    zero = jnp.zeros_like(mu)
    return jnp.stack([x_r0, x_m1, r_r0, r_m1, r_m2, zero, zero, zero], axis=1)


def on_device(observations, huber_scale, observed, jitter, owner_map, neighbours):
    fields, row_dev, col_dev = observations.shape
    sixteen_size = lax.axis_size(SIXTEEN)
    my_place = lax.axis_index(SIXTEEN)
    group_place = lax.axis_index(WIDE)
    total_strips = BLOCKS_DEV * sixteen_size
    weight = observed.astype(jnp.float32)
    spread_scale = huber_scale[:, None, None]

    def with_count(part, count):
        rows = jnp.zeros((8, count.shape[0]), jnp.float32).at[0].set(count)
        return jnp.concatenate([part, rows], axis=0)

    def terms(row_effect, col_effect):
        return weight[None] * jnp.clip(
            (observations - row_effect[:, :, None] - col_effect[:, None, :]) / spread_scale,
            -HUBER_EDGE,
            HUBER_EDGE,
        )

    def sum_wide(part):
        for axis in WIDE[::-1]:
            part = sum_direct(part, axis)
        return part

    row_effect = jnp.zeros((fields, row_dev), jnp.float32)
    col_effect = jnp.zeros((fields, col_dev), jnp.float32)
    part = with_count(jnp.sum(terms(row_effect, col_effect), axis=2), jnp.sum(weight, axis=1))
    part, jitter, owner_map, neighbours = lax.optimization_barrier(
        (part, jitter, owner_map, neighbours)
    )

    group_map = owner_map[0]
    group_lists = neighbours[0]
    my_targets = lax.dynamic_slice_in_dim(group_map, my_place * BLOCKS_DEV, BLOCKS_DEV)
    sent_one, sent_two = observed_slots(my_targets, observations)
    owned = owned_table(group_map, sixteen_size, BLOCKS_DEV)
    my_ids = lax.dynamic_index_in_dim(owned, my_place, 0, keepdims=False)
    sources = my_ids // BLOCKS_DEV
    table = tile_lists(group_lists[0], total_strips)
    row_place = (my_place * row_dev + jnp.arange(row_dev, dtype=jnp.int32)).astype(jnp.float32)
    col_place = (group_place * col_dev + jnp.arange(col_dev, dtype=jnp.int32)).astype(jnp.float32)
    location = jnp.stack(
        [row_place[:, None] + jitter[0], col_place[None, :] + jitter[1]], axis=0
    ).reshape(2, BLOCKS_DEV, STRIP, col_dev)
    location = location.transpose(1, 0, 2, 3).reshape(BLOCKS_DEV, 2 * STRIP, col_dev)
    location = location * (1.0 / CUTOFF)
    none = jnp.zeros((REACH, 2 * STRIP, col_dev), jnp.float32)
    here = jnp.concatenate([none, location, none], axis=0)
    here = (here, here.transpose(0, 2, 1))

    owned_one = to_owners(sent_one)
    total = sum_wide(part)
    tiles = covariance_tiles(0, ROW_TILES, table, *here, None)
    total, tiles, owned_one = lax.optimization_barrier((total, tiles, owned_one))
    row_count = jnp.maximum(total[fields], 1.0)
    row_effect = huber_scale[:, None] * total[:fields] / row_count[None, :]
    part = with_count(jnp.sum(terms(row_effect, col_effect), axis=1), jnp.sum(weight, axis=0))
    before, after, location = beside(location, REACH)
    part, here, tiles = lax.optimization_barrier((part, here, tiles))
    total = over_copies(part, SIXTEEN)
    tiles = covariance_tiles(ROW_TILES, COL_TILES, table, *here, tiles)
    total, tiles, before, after = lax.optimization_barrier((total, tiles, before, after))
    wider = jnp.concatenate([before, location, after], axis=0)
    wider = (wider, wider.transpose(0, 2, 1))
    col_count = jnp.maximum(total[fields], 1.0)
    col_effect = huber_scale[:, None] * total[:fields] / col_count[None, :]
    part = jnp.sum(terms(row_effect, col_effect), axis=2)
    part, wider, tiles, sent_two = lax.optimization_barrier((part, wider, tiles, sent_two))
    owned_two = to_owners(sent_two)
    total = sum_wide(part)
    tiles = covariance_tiles(ROW_TILES + COL_TILES, ROW_TILES, table, *wider, tiles)
    total, tiles, owned_two = lax.optimization_barrier((total, tiles, owned_two))
    row_effect = row_effect + huber_scale[:, None] * total / row_count[None, :]
    part = jnp.sum(terms(row_effect, col_effect), axis=1)
    part, tiles = lax.optimization_barrier((part, tiles))
    total = over_copies(part, SIXTEEN)
    tiles = covariance_tiles(2 * ROW_TILES + COL_TILES, COL_TILES, table, *wider, tiles)
    total, tiles = lax.optimization_barrier((total, tiles))
    col_effect = col_effect + huber_scale[:, None] * total / col_count[None, :]
    all_rows = lax.all_gather(
        row_effect.T.reshape(BLOCKS_DEV, STRIP, fields), SIXTEEN, axis=0, tiled=True
    )
    all_weights = lax.all_gather(weight.reshape(BLOCKS_DEV, BLOCK), SIXTEEN, axis=0, tiled=True)

    r0 = residual_of(observations, weight, row_effect, col_effect)
    before, after, r0 = beside(r0, REACH)
    part = own_product(table, r0, tiles)
    m1 = halo_product(table, my_targets, before, after, part, tiles, False)
    before, after, m1 = beside(m1, REACH)
    part = own_product(table, m1, tiles)
    slots = spread(my_targets, m1, part, before, after)
    owned_m1 = to_owners(slots)
    m2, slots = halo_product(table, my_targets, before, after, part, tiles, True)
    dots = jnp.stack(
        [jnp.sum(p * q, axis=(0, 2)) for p, q in ((r0, r0), (r0, m1), (m1, m1), (m1, m2))]
    )
    dots = sum_wide(dots)
    slots, owned_m1, dots = lax.optimization_barrier((slots, owned_m1, dots))
    owned_m2 = to_owners(slots)
    for axis in SIXTEEN[::-1]:
        dots = sum_direct(dots, axis)
    scale = step_scales(*dots)
    rows = jnp.take(all_rows, my_ids, axis=0).transpose(0, 2, 1)
    weights = jnp.take(all_weights, my_ids, axis=0)
    solution_now, residual_now = combined(
        sources, scale, col_effect, weights, rows, owned_one, owned_two, owned_m1, owned_m2
    )
    return (solution_now[None, None], residual_now[None, None])


def solution(mesh):
    finer = Mesh(mesh.devices.reshape(4, 2, 4, 4), ("wide_0", "wide_1", "sixteen_0", "sixteen_1"))
    in_specs = (
        P(None, SIXTEEN, WIDE),
        P(),
        P(SIXTEEN, WIDE),
        P(None, SIXTEEN, WIDE),
        P(WIDE, None),
        P(WIDE, None, None),
    )
    out_specs = (P(WIDE, SIXTEEN, None, None, None), P(WIDE, SIXTEEN, None, None, None))
    return jax.shard_map(
        on_device, mesh=finer, in_specs=in_specs, out_specs=out_specs, check_vma=False
    )
```

```python
import functools

import jax
import jax.numpy as jnp
from jax import lax
from jax.experimental import pallas as pl
from jax.experimental.pallas import tpu as pltpu
from jax.sharding import Mesh
from jax.sharding import PartitionSpec as P

BLOCK = 512
BLOCKS_DEV = 8
REACH = 4
NEIGHBOURS = 6
PAIRED = NEIGHBOURS // 2
SWEEPS = 2
STRIP = 4
COL_DEV = 128
WIDE = ("wide_0", "wide_1")
SIXTEEN = ("sixteen_0", "sixteen_1")

HUBER_EDGE = 1.345
SILL_TERM = 0.02
ROOT_THREE = 1.7320508075688772
SPREAD = 2.0 * STRIP
CUTOFF = 6.0 * STRIP
BAND = 24
GROUP = 16

OWN_TILES = BLOCKS_DEV + PAIRED * BLOCKS_DEV - 6
HALO_TILES = 2 * (2 + 3 + 4)
ROW_TILES, COL_TILES = 7, 15
TILE_SLOTS = 4
OP_SLOTS = 5


def sent_to_all(shard, axis):
    peers = lax.axis_size(axis)
    return lax.all_to_all(
        jnp.broadcast_to(shard[None], (peers, *shard.shape)), axis, 0, 0, tiled=True
    )


def over_copies(shard, axis):
    return jnp.sum(sent_to_all(shard, axis), axis=0)


def sum_direct(part, axis):
    peers = lax.axis_size(axis)
    moved = [
        lax.ppermute(part, axis, [(i, (i + k) % peers) for i in range(peers)])
        for k in range(1, peers)
    ]
    return functools.reduce(jnp.add, moved, part)


def beside(shard, width, dim=0):
    peers, length = lax.axis_size(SIXTEEN), shard.shape[dim]
    up = [(i, (i + 1) % peers) for i in range(peers)]
    down = [(j, i) for i, j in up]
    last = lax.slice_in_dim(shard, length - width, length, axis=dim)
    initial = lax.slice_in_dim(shard, 0, width, axis=dim)
    shard, last, initial = lax.optimization_barrier((shard, last, initial))
    return lax.ppermute(last, SIXTEEN, up), lax.ppermute(initial, SIXTEEN, down), shard


def owned_table(group_map, owners, per_owner):
    total_strips = group_map.shape[0]
    member = (group_map[None, :] == jnp.arange(owners, dtype=jnp.int32)[:, None]).astype(jnp.int32)
    ranked = jnp.cumsum(member, axis=1, dtype=jnp.int32) - 1
    slot_hit = (ranked[:, :, None] == jnp.arange(per_owner, dtype=jnp.int32)[None, None, :]).astype(
        jnp.int32
    ) * member[:, :, None]
    numbers = jnp.arange(total_strips, dtype=jnp.int32)
    return jnp.sum(slot_hit * numbers[None, :, None], axis=1, dtype=jnp.int32)


def offsets_of(list_ref):
    held = [
        functools.reduce(jnp.logical_or, [list_ref[n] == d for n in range(NEIGHBOURS)])
        for d in range(1, REACH)
    ]
    missing = jnp.where(held[0], jnp.where(held[1], jnp.where(held[2], 4, 3), 2), 1)
    return [k + jnp.where(missing <= k, 1, 0) for k in range(1, PAIRED + 1)]


def own_count(offsets):
    return (PAIRED + 1) * BLOCKS_DEV - (offsets[0] + offsets[1] + offsets[2])


def halo_count(offsets):
    return 2 * (offsets[0] + offsets[1] + offsets[2])


def own_pair(t, offsets):
    d1, d2, d3 = offsets
    p = t - BLOCKS_DEV
    n1, n2 = BLOCKS_DEV - d1, 2 * BLOCKS_DEV - d1 - d2
    one = jnp.where(p < n1, p, jnp.where(p < n2, p - n1, p - n2))
    return one, one + jnp.where(p < n1, d1, jnp.where(p < n2, d2, d3))


def halo_pair(q, offsets):
    d1, d2, d3 = offsets
    reach = d1 + d2 + d3
    right = q >= reach
    q = jnp.where(right, q - reach, q)
    step = jnp.where(q < d1, d1, jnp.where(q < d1 + d2, d2, d3))
    pos = jnp.where(q < d1, q, jnp.where(q < d1 + d2, q - d1, q - d1 - d2))
    one = jnp.where(right, BLOCKS_DEV - 1 - pos, pos)
    return one, jnp.where(right, one + step, one - step)


LISTED = OWN_TILES + HALO_TILES


def tiles_kernel(first, count, beside, held, scalar_ref, jitter_ref, *refs):
    beside_refs, refs = refs[:beside], refs[beside + held :]
    tiles_ref, buf, sem = refs
    a, b = ROOT_THREE * CUTOFF / SPREAD, 4.0
    offsets = offsets_of(scalar_ref)
    place, group = scalar_ref[NEIGHBOURS], scalar_ref[NEIGHBOURS + 1]
    total_rows = scalar_ref[NEIGHBOURS + 2]
    row_dev = STRIP * BLOCKS_DEV
    lane = lax.broadcasted_iota(jnp.int32, (GROUP, COL_DEV), 1)
    within = lax.broadcasted_iota(jnp.int32, (STRIP, COL_DEV), 0)
    across = lax.broadcasted_iota(jnp.int32, (STRIP, COL_DEV), 1)
    col_place = (group * COL_DEV + across).astype(jnp.float32)

    def out_copy(t):
        slot = lax.rem(t - first, TILE_SLOTS)
        return pltpu.make_async_copy(buf.at[slot], tiles_ref.at[t], sem.at[slot])

    def live(t):
        mine = (t < OWN_TILES) & (t < own_count(offsets))
        return mine | ((t >= OWN_TILES) & (t < OWN_TILES + halo_count(offsets)))

    def places(block, ref, at):
        row = lax.rem(place * row_dev + STRIP * block + total_rows, total_rows)
        rows = (row + within).astype(jnp.float32) + ref[0, pl.ds(at, STRIP), :]
        cols = col_place + ref[1, pl.ds(at, STRIP), :]
        return jnp.concatenate([rows, cols], axis=0) * (1.0 / CUTOFF)

    def pair_of(t):
        q = t - OWN_TILES
        one, other = own_pair(t, offsets)
        one_q, other_q = halo_pair(q, offsets)
        same = t < BLOCKS_DEV
        mine = t < OWN_TILES
        one = jnp.where(same, t, jnp.where(mine, one, one_q))
        return one, jnp.where(same, t, jnp.where(mine, other, other_q))

    def evaluate(slot, to, frm, sill):
        for rb in range(STRIP):
            row_b = jnp.broadcast_to(frm[:, rb : rb + 1], (COL_DEV, COL_DEV))
            col_b = jnp.broadcast_to(frm[:, STRIP + rb : STRIP + rb + 1], (COL_DEV, COL_DEV))
            for u in range(COL_DEV // 2 // GROUP):
                lo_s = slice(GROUP * u, GROUP * (u + 1))
                hi_s = slice(64 + GROUP * u, 64 + GROUP * (u + 1))
                near = (lane >= GROUP * u - BAND) & (lane < GROUP * (u + 1) + BAND)
                one_m = jnp.where(near, 1.0, 0.0).astype(jnp.bfloat16)
                other_m = jnp.where(near, 0.0, 1.0).astype(jnp.bfloat16)
                row_s = jnp.where(near, row_b[lo_s], row_b[hi_s])
                col_s = jnp.where(near, col_b[lo_s], col_b[hi_s])
                for ra in range(STRIP):
                    dr = row_s - to[ra : ra + 1]
                    dc = col_s - to[STRIP + ra : STRIP + ra + 1]
                    square = dr * dr + dc * dc
                    far = square * lax.rsqrt(jnp.maximum(square, 1e-30))
                    fading = jnp.maximum(1.0 - far, 0.0)
                    fading = fading * fading
                    fading = fading * fading
                    shape = (1.0 + a * far) * (sill + (sill * b) * far)
                    value = shape * fading * jnp.exp(-a * far)
                    hi = value.astype(jnp.bfloat16)
                    lo = (value - hi.astype(jnp.float32)).astype(jnp.bfloat16)
                    lanes = slice(COL_DEV * ra, COL_DEV * (ra + 1))
                    top = rb * COL_DEV + GROUP * u
                    for part, at in ((hi, top), (lo, BLOCK + top)):
                        buf[slot, at : at + GROUP, lanes] = part * one_m
                        buf[slot, at + 64 : at + 64 + GROUP, lanes] = part * other_m

    def one_tile(t, carry):
        slot = lax.rem(t - first, TILE_SLOTS)
        past = jnp.maximum(t - TILE_SLOTS, first)

        @pl.when((t >= first + TILE_SLOTS) & live(past))
        def _():
            out_copy(past).wait()

        @pl.when(live(t))
        def _():
            one, other = pair_of(t)
            sill = jnp.where(one == other, (NEIGHBOURS + 1.0) * SILL_TERM, SILL_TERM)
            inside = jnp.clip(other, 0, BLOCKS_DEV - 1)
            to = places(one, jitter_ref, STRIP * one)
            frm = places(other, jitter_ref, STRIP * inside)
            if beside_refs:
                left = places(other, beside_refs[0], STRIP * jnp.clip(other + REACH, 0, REACH - 1))
                right = places(
                    other, beside_refs[1], STRIP * jnp.clip(other - BLOCKS_DEV, 0, REACH - 1)
                )
                frm = jnp.where(other < 0, left, jnp.where(other < BLOCKS_DEV, frm, right))
            evaluate(slot, to, frm.T, sill)
            out_copy(t).start()

        return carry

    lax.fori_loop(first, first + count, one_tile, 0)
    for t in range(max(first, first + count - TILE_SLOTS), first + count):

        @pl.when(live(t))
        def _(t=t):
            out_copy(t).wait()


def covariance_tiles(first, count, scalars, jitter, beside_jitter, held):
    extra = [] if held is None else [held]
    ins = [scalars, jitter, *beside_jitter, *extra]
    return pl.pallas_call(
        functools.partial(tiles_kernel, first, count, len(beside_jitter), len(extra)),
        in_specs=[SMEM_SPEC] + [VMEM_SPEC] * (1 + len(beside_jitter)) + [HBM_SPEC] * len(extra),
        out_specs=HBM_SPEC,
        scratch_shapes=[
            pltpu.VMEM((TILE_SLOTS, 2 * BLOCK, BLOCK), jnp.bfloat16),
            pltpu.SemaphoreType.DMA((TILE_SLOTS,)),
        ],
        out_shape=jax.ShapeDtypeStruct((LISTED, 2 * BLOCK, BLOCK), jnp.bfloat16),
        input_output_aliases={len(ins) - 1: 0} if extra else {},
        compiler_params=pltpu.CompilerParams(vmem_limit_bytes=12 << 20),
        cost_estimate=pl.CostEstimate(
            flops=count * 12 * BLOCK * BLOCK,
            bytes_accessed=count * 4 * BLOCK * BLOCK,
            transcendentals=count * BLOCK * BLOCK,
        ),
        name="tiles",
    )(*ins)


def halves(v):
    hi = v.astype(jnp.bfloat16)
    lo = (v - hi.astype(jnp.float32)).astype(jnp.bfloat16)
    return hi, lo


NN = (((1,), (0,)), ((), ()))
NT = (((1,), (1,)), ((), ()))


def product(both, tile_ref, dims):
    fields = both.shape[0] // 2
    main = lax.dot_general(
        both, tile_ref[:BLOCK], dims, preferred_element_type=jnp.float32
    )
    rest = lax.dot_general(
        both[:fields], tile_ref[BLOCK:], dims, preferred_element_type=jnp.float32
    )
    return main[:fields] + (main[fields:] + rest)


def op_kernel(own, halo, send, scalar_ref, target_ref, *refs):
    refs = list(refs)
    v_ref = refs.pop(0) if own else None
    beside_refs = [refs.pop(0), refs.pop(0)] if halo else []
    held_ref = None if own else refs.pop(0)
    tiles_ref, out_ref = refs.pop(0), refs.pop(0)
    slots_ref = refs.pop(0) if send else None
    values, both_ref, total, buf, sem, in_sem, out_sem = refs
    fields = total.shape[1]
    offsets = offsets_of(scalar_ref)
    mine = own_count(offsets) if own else 0
    base = 0 if own else OWN_TILES
    count = mine + (halo_count(offsets) if halo else 0)

    def copy(t):
        slot = lax.rem(t, OP_SLOTS)
        at = jnp.where(t < mine, t, t - mine + OWN_TILES) if own else t + OWN_TILES
        return pltpu.make_async_copy(tiles_ref.at[at], buf.at[slot], sem.at[slot])

    loads = []
    if own:
        loads.append((v_ref, 0, BLOCKS_DEV))
    for side, ref in enumerate(beside_refs):
        loads.append((ref, BLOCKS_DEV + REACH * side, REACH))
    arriving = [
        pltpu.make_async_copy(ref, values.at[pl.ds(at, size)], in_sem.at[i])
        for i, (ref, at, size) in enumerate(loads)
    ]
    if held_ref is not None:
        arriving.append(pltpu.make_async_copy(held_ref, total, in_sem.at[3]))
    for load in arriving:
        load.start()
    for t in range(OP_SLOTS - 1):
        copy(t).start()
    for load in arriving:
        load.wait()
    for _, at, size in loads:
        for g in range(at, at + size):
            hi, lo = halves(values[g])
            both_ref[g, :fields] = hi
            both_ref[g, fields:] = lo

    def arrive(t):
        @pl.when(t + OP_SLOTS - 1 < count)
        def _():
            copy(t + OP_SLOTS - 1).start()

        copy(t).wait()
        return buf.at[lax.rem(t, OP_SLOTS)]

    def with_itself(t, carry):
        tile = arrive(t)
        total[t] = product(both_ref[t], tile, NN)
        return carry

    def with_another(t, carry):
        tile = arrive(t)
        one, other = own_pair(t, offsets)
        total[one] += product(both_ref[other], tile, NN)
        total[other] += product(both_ref[one], tile, NT)
        return carry

    def with_beside(t, carry):
        tile = arrive(t)
        one, other = halo_pair(t - mine, offsets)
        side = BLOCKS_DEV + jnp.where(other < 0, other + REACH, other - BLOCKS_DEV + REACH)
        total[one] += product(both_ref[side], tile, NN)
        return carry

    if own:
        lax.fori_loop(0, BLOCKS_DEV, with_itself, 0)
        lax.fori_loop(BLOCKS_DEV, mine, with_another, 0)
    if halo:
        lax.fori_loop(mine, count, with_beside, 0)
    leaving = [pltpu.make_async_copy(total, out_ref, out_sem.at[BLOCKS_DEV])]
    if send:
        leaving += out_copies(total, slots_ref, target_ref, out_sem)
    for out in leaving:
        out.start()
    for out in leaving:
        out.wait()


def out_copies(values_ref, slots_ref, target_ref, sem):
    return [
        pltpu.make_async_copy(values_ref.at[g], slots_ref.at[target_ref[g]], sem.at[g])
        for g in range(BLOCKS_DEV)
    ]


SMEM_SPEC = pl.BlockSpec(memory_space=pltpu.SMEM)
VMEM_SPEC = pl.BlockSpec(memory_space=pltpu.VMEM)
HBM_SPEC = pl.BlockSpec(memory_space=pltpu.HBM)


def in_hbm(x):
    return pltpu.with_memory_space_constraint(x, pltpu.HBM)


def slot_shape(v):
    return pltpu.HBM((lax.axis_size(SIXTEEN), *v.shape[1:]), jnp.float32)


def applied(scalars, targets, tiles, v=None, beside=(), held=None, send=False):
    shape = (held if v is None else v).shape
    blocks, fields, _ = shape
    out = pltpu.HBM(shape, jnp.float32)
    ins = [in_hbm(x) for x in (v, *beside, held) if x is not None] + [tiles]
    number = OWN_TILES * (v is not None) + HALO_TILES * bool(beside)
    out = pl.pallas_call(
        functools.partial(op_kernel, v is not None, bool(beside), send),
        in_specs=[SMEM_SPEC] * 2 + [HBM_SPEC] * len(ins),
        out_specs=[HBM_SPEC] * (1 + send),
        scratch_shapes=[
            pltpu.VMEM((blocks + 2 * REACH, fields, BLOCK), jnp.float32),
            pltpu.VMEM((blocks + 2 * REACH, 2 * fields, BLOCK), jnp.bfloat16),
            pltpu.VMEM(shape, jnp.float32),
            pltpu.VMEM((OP_SLOTS, 2 * BLOCK, BLOCK), jnp.bfloat16),
            pltpu.SemaphoreType.DMA((OP_SLOTS,)),
            pltpu.SemaphoreType.DMA((4,)),
            pltpu.SemaphoreType.DMA((BLOCKS_DEV + 1,)),
        ],
        out_shape=[out] + [slot_shape(out)] * send,
        compiler_params=pltpu.CompilerParams(vmem_limit_bytes=24 << 20),
        cost_estimate=pl.CostEstimate(
            flops=3 * number * 3 * fields * BLOCK * BLOCK,
            bytes_accessed=number * 4 * BLOCK * BLOCK,
            transcendentals=0,
        ),
        name="applied",
    )(scalars, targets, *ins)
    return out if send else out[0]


def spread_kernel(target_ref, v_ref, *refs):
    slots_ref, sem = refs[-2:]
    sent = out_copies(v_ref, slots_ref, target_ref, sem)
    for copy_out in sent:
        copy_out.start()
    for copy_out in sent:
        copy_out.wait()


def spread(targets, v, *others):
    return pl.pallas_call(
        spread_kernel,
        in_specs=[SMEM_SPEC] + [HBM_SPEC] * (1 + len(others)),
        out_specs=HBM_SPEC,
        scratch_shapes=[pltpu.SemaphoreType.DMA((BLOCKS_DEV,))],
        out_shape=slot_shape(v),
        compiler_params=pltpu.CompilerParams(vmem_limit_bytes=1 << 20),
        name="spread",
    )(targets, *map(in_hbm, (v, *others)))


def residual_kernel(
    target_ref, obs_ref, weight_ref, row_ref, before_ref, before_row_ref, after_ref,
    after_row_ref, col_ref, out_ref, before_out_ref, after_out_ref, slots_ref, buf, sem,
):
    fields = obs_ref.shape[0]
    col = col_ref[...]

    def block(at, obs, weight, row, g):
        for ra in range(STRIP):
            r = STRIP * g + ra
            left = obs[:fields, r, :] - row[:, r : r + 1] - col
            weighted = weight[r : r + 1, :] * left
            buf[at, :, COL_DEV * ra : COL_DEV * (ra + 1)] = weighted

    copies = []
    for g in range(BLOCKS_DEV):
        block(g, obs_ref, weight_ref, row_ref, g)
        copies.append(
            pltpu.make_async_copy(buf.at[g], slots_ref.at[target_ref[g]], sem.at[g])
        )
        copies[-1].start()
    copies.append(
        pltpu.make_async_copy(buf.at[pl.ds(0, BLOCKS_DEV)], out_ref, sem.at[BLOCKS_DEV])
    )
    copies[-1].start()
    sides = ((before_ref, before_row_ref, before_out_ref), (after_ref, after_row_ref, after_out_ref))
    for side, (obs, row, out) in enumerate(sides):
        first = BLOCKS_DEV + REACH * side
        for g in range(REACH):
            block(first + g, obs, obs.at[fields], row, g)
        copies.append(
            pltpu.make_async_copy(
                buf.at[pl.ds(first, REACH)], out, sem.at[BLOCKS_DEV + 1 + side]
            )
        )
        copies[-1].start()
    for copy in copies:
        copy.wait()


def residual_of(targets, observations, weight, row_effect, before, before_row, after, after_row, col):
    fields = observations.shape[0]
    own = pltpu.HBM((BLOCKS_DEV, fields, BLOCK), jnp.float32)
    side = pltpu.HBM((REACH, fields, BLOCK), jnp.float32)
    return pl.pallas_call(
        residual_kernel,
        in_specs=[SMEM_SPEC] + [VMEM_SPEC] * 8,
        out_specs=[HBM_SPEC] * 4,
        scratch_shapes=[
            pltpu.VMEM((BLOCKS_DEV + 2 * REACH, fields, BLOCK), jnp.float32),
            pltpu.SemaphoreType.DMA((BLOCKS_DEV + 3,)),
        ],
        out_shape=[own, side, side, slot_shape(own)],
        compiler_params=pltpu.CompilerParams(vmem_limit_bytes=12 << 20),
        name="residual",
    )(targets, observations, weight, row_effect, before, before_row, after, after_row, col)


def combine_kernel(src_ref, scale_ref, *refs):
    ins, (x_ref, r_ref) = refs[:-2], refs[-2:]
    scale = scale_ref[...]
    for j in range(BLOCKS_DEV):
        r0, m1, m2 = (ref[0] for ref in ins[3 * j : 3 * j + 3])
        x_ref[:, j, :] = scale[:, 0:1] * r0 + scale[:, 1:2] * m1
        r_ref[:, j, :] = scale[:, 2:3] * r0 + scale[:, 3:4] * m1 + scale[:, 4:5] * m2


def combined(sources, scale, r0, m1, m2):
    fields = r0.shape[1]
    part = 16
    ins, specs = [], []
    for j in range(BLOCKS_DEV):
        for v in (r0, m1, m2):
            ins.append(v)
            specs.append(
                pl.BlockSpec(
                    (1, part, BLOCK), functools.partial(lambda j, i, s: (s[j], i, 0), j)
                )
            )
    out = pl.BlockSpec((part, BLOCKS_DEV, BLOCK), lambda i, s: (i, 0, 0))
    shape = jax.ShapeDtypeStruct((fields, BLOCKS_DEV, BLOCK), jnp.float32)
    return pl.pallas_call(
        combine_kernel,
        grid_spec=pltpu.PrefetchScalarGridSpec(
            num_scalar_prefetch=1,
            grid=(fields // part,),
            in_specs=[pl.BlockSpec((part, 8), lambda i, s: (i, 0))] + specs,
            out_specs=[out, out],
        ),
        out_shape=[shape, shape],
        compiler_params=pltpu.CompilerParams(vmem_limit_bytes=20 << 20),
        name="combine",
    )(sources, scale, *ins)


def to_owners(slots):
    return lax.all_to_all(slots, SIXTEEN, 0, 0, tiled=True)


def step_scales(h00, h01, h11, h12):
    mu = h01 / h00
    var = (h11 - mu * h01) / h00
    a0 = 1.0 / (1.0 + mu)
    beta = var * a0 * a0
    skew = (h12 - mu * h11 - mu * (h11 - mu * h01)) / h00
    a1 = var / (var + skew - var * var * a0)
    x_r0 = a0 + a1 * beta + a1 * a0 * mu
    x_m1 = -a1 * a0
    r_r0 = a0 * mu * (1.0 - a1) - a1 * beta
    r_m1 = -a0 * (1.0 - a1) - a1 * a0 * mu - a1 * beta
    r_m2 = a1 * a0
    zero = jnp.zeros_like(mu)
    return jnp.stack([x_r0, x_m1, r_r0, r_m1, r_m2, zero, zero, zero], axis=1)


def on_device(observations, huber_scale, observed, jitter, owner_map, neighbours):
    fields, row_dev, col_dev = observations.shape
    sixteen_size = lax.axis_size(SIXTEEN)
    my_place = lax.axis_index(SIXTEEN)
    group_place = lax.axis_index(WIDE)
    total_strips = BLOCKS_DEV * sixteen_size
    weight = observed.astype(jnp.float32)
    spread_scale = huber_scale[:, None, None]

    def with_count(part, count):
        rows = jnp.zeros((8, count.shape[0]), jnp.float32).at[0].set(count)
        return jnp.concatenate([part, rows], axis=0)

    def terms(row_effect, col_effect):
        return weight[None] * jnp.clip(
            (observations - row_effect[:, :, None] - col_effect[:, None, :]) / spread_scale,
            -HUBER_EDGE,
            HUBER_EDGE,
        )

    def sum_wide(part):
        for axis in WIDE[::-1]:
            part = sum_direct(part, axis)
        return part

    row_effect = jnp.zeros((fields, row_dev), jnp.float32)
    col_effect = jnp.zeros((fields, col_dev), jnp.float32)
    part = with_count(jnp.sum(terms(row_effect, col_effect), axis=2), jnp.sum(weight, axis=1))
    part, jitter, owner_map, neighbours = lax.optimization_barrier(
        (part, jitter, owner_map, neighbours)
    )
    group_map = owner_map[0]
    scalars = jnp.concatenate(
        [neighbours[0, 0], jnp.stack([my_place, group_place, total_strips * STRIP])]
    ).astype(jnp.int32)

    def beside_tiles(part, axis, count, tiles, first, near):
        if first:
            part, tiles = lax.optimization_barrier((part, tiles))
        total = over_copies(part, axis)
        tiles = covariance_tiles(first, count, scalars, jitter, near, tiles)
        total, tiles = lax.optimization_barrier((total, tiles))
        return total, tiles, first + count

    edges = jnp.concatenate([observations, weight[None], jitter], axis=0)
    before, after, _ = beside(edges, REACH * STRIP, 1)
    total, tiles, first = beside_tiles(part, WIDE, ROW_TILES, None, 0, ())
    row_count = jnp.maximum(total[fields], 1.0)
    row_effect = huber_scale[:, None] * total[:fields] / row_count[None, :]
    part = with_count(jnp.sum(terms(row_effect, col_effect), axis=1), jnp.sum(weight, axis=0))
    total, tiles, first = beside_tiles(part, SIXTEEN, COL_TILES, tiles, first, ())
    total, before, after = lax.optimization_barrier((total, before, after))
    near = (before[fields + 1 :], after[fields + 1 :])
    col_count = jnp.maximum(total[fields], 1.0)
    col_effect = huber_scale[:, None] * total[:fields] / col_count[None, :]
    part = jnp.sum(terms(row_effect, col_effect), axis=2)
    total, tiles, first = beside_tiles(part, WIDE, ROW_TILES, tiles, first, near)
    row_effect = row_effect + huber_scale[:, None] * total / row_count[None, :]
    part = jnp.sum(terms(row_effect, col_effect), axis=1)
    row_before, row_after, _ = beside(row_effect, REACH * STRIP, 1)
    total, tiles, first = beside_tiles(part, SIXTEEN, COL_TILES, tiles, first, near)
    col_effect = col_effect + huber_scale[:, None] * total / col_count[None, :]

    my_targets = lax.dynamic_slice_in_dim(group_map, my_place * BLOCKS_DEV, BLOCKS_DEV)
    r0, r0_before, r0_after, slots = residual_of(
        my_targets, observations, weight, row_effect, before, row_before, after, row_after, col_effect
    )
    owned_r0 = to_owners(slots)
    m1 = applied(scalars, my_targets, tiles, r0, (r0_before, r0_after))
    before, after, m1 = beside(m1, REACH)
    part = applied(scalars, my_targets, tiles, m1)
    slots = spread(my_targets, m1, part, before, after)
    slots, owned_r0 = lax.optimization_barrier((slots, owned_r0))
    owned_m1 = to_owners(slots)
    m2, slots = applied(scalars, my_targets, tiles, None, (before, after), part, True)
    dots = jnp.stack(
        [jnp.sum(p * q, axis=(0, 2)) for p, q in ((r0, r0), (r0, m1), (m1, m1), (m1, m2))]
    )
    dots = sum_wide(dots)
    slots, owned_m1, dots = lax.optimization_barrier((slots, owned_m1, dots))
    owned_m2 = to_owners(slots)
    for axis in SIXTEEN[::-1]:
        dots = sum_direct(dots, axis)
    scale = step_scales(*dots)
    owned = owned_table(group_map, sixteen_size, BLOCKS_DEV)
    my_ids = lax.dynamic_index_in_dim(owned, my_place, 0, keepdims=False)
    solution_now, residual_now = combined(
        my_ids // BLOCKS_DEV, scale, owned_r0, owned_m1, owned_m2
    )
    return (solution_now[None, None], residual_now[None, None])


def solution(mesh):
    finer = Mesh(mesh.devices.reshape(4, 2, 4, 4), ("wide_0", "wide_1", "sixteen_0", "sixteen_1"))
    in_specs = (
        P(None, SIXTEEN, WIDE),
        P(),
        P(SIXTEEN, WIDE),
        P(None, SIXTEEN, WIDE),
        P(WIDE, None),
        P(WIDE, None, None),
    )
    out_specs = (P(WIDE, SIXTEEN, None, None, None), P(WIDE, SIXTEEN, None, None, None))
    return jax.shard_map(
        on_device, mesh=finer, in_specs=in_specs, out_specs=out_specs, check_vma=False
    )
```

```python
import functools

import jax
import jax.numpy as jnp
from jax import lax
from jax.experimental import pallas as pl
from jax.experimental.pallas import tpu as pltpu
from jax.sharding import Mesh
from jax.sharding import PartitionSpec as P

BLOCK = 512
BLOCKS_DEV = 8
REACH = 4
NEIGHBOURS = 6
PAIRED = NEIGHBOURS // 2
SWEEPS = 2
STRIP = 4
COL_DEV = 128
WIDE = ("wide_0", "wide_1")
SIXTEEN = ("sixteen_0", "sixteen_1")

HUBER_EDGE = 1.345
SILL_TERM = 0.02
ROOT_THREE = 1.7320508075688772
SPREAD = 2.0 * STRIP
CUTOFF = 6.0 * STRIP
BAND = 24
GROUP = 16

OWN_TILES = BLOCKS_DEV + PAIRED * BLOCKS_DEV - 6
HALO_TILES = 2 * (2 + 3 + 4)
ROW_TILES, COL_TILES = 7, 15
TILE_SLOTS = 4
OP_SLOTS = 5
EXTRA = 8
EARLY_TILES = 12


def sent_to_all(shard, axis):
    peers = lax.axis_size(axis)
    return lax.all_to_all(
        jnp.broadcast_to(shard[None], (peers, *shard.shape)), axis, 0, 0, tiled=True
    )


def over_copies(shard, axis):
    return jnp.sum(sent_to_all(shard, axis), axis=0)


def sum_direct(part, axis):
    peers = lax.axis_size(axis)
    moved = [
        lax.ppermute(part, axis, [(i, (i + k) % peers) for i in range(peers)])
        for k in range(1, peers)
    ]
    return functools.reduce(jnp.add, moved, part)


def beside(shard, width, dim=0):
    peers, length = lax.axis_size(SIXTEEN), shard.shape[dim]
    up = [(i, (i + 1) % peers) for i in range(peers)]
    down = [(j, i) for i, j in up]
    last = lax.slice_in_dim(shard, length - width, length, axis=dim)
    initial = lax.slice_in_dim(shard, 0, width, axis=dim)
    shard, last, initial = lax.optimization_barrier((shard, last, initial))
    return lax.ppermute(last, SIXTEEN, up), lax.ppermute(initial, SIXTEEN, down), shard


def owned_table(group_map, owners, per_owner):
    total_strips = group_map.shape[0]
    member = (group_map[None, :] == jnp.arange(owners, dtype=jnp.int32)[:, None]).astype(jnp.int32)
    ranked = jnp.cumsum(member, axis=1, dtype=jnp.int32) - 1
    slot_hit = (ranked[:, :, None] == jnp.arange(per_owner, dtype=jnp.int32)[None, None, :]).astype(
        jnp.int32
    ) * member[:, :, None]
    numbers = jnp.arange(total_strips, dtype=jnp.int32)
    return jnp.sum(slot_hit * numbers[None, :, None], axis=1, dtype=jnp.int32)


def offsets_of(list_ref):
    held = [
        functools.reduce(jnp.logical_or, [list_ref[n] == d for n in range(NEIGHBOURS)])
        for d in range(1, REACH)
    ]
    missing = jnp.where(held[0], jnp.where(held[1], jnp.where(held[2], 4, 3), 2), 1)
    return [k + jnp.where(missing <= k, 1, 0) for k in range(1, PAIRED + 1)]


def own_count(offsets):
    return (PAIRED + 1) * BLOCKS_DEV - (offsets[0] + offsets[1] + offsets[2])


def halo_count(offsets):
    return 2 * (offsets[0] + offsets[1] + offsets[2])


def own_pair(t, offsets):
    d1, d2, d3 = offsets
    p = t - BLOCKS_DEV
    n1, n2 = BLOCKS_DEV - d1, 2 * BLOCKS_DEV - d1 - d2
    one = jnp.where(p < n1, p, jnp.where(p < n2, p - n1, p - n2))
    return one, one + jnp.where(p < n1, d1, jnp.where(p < n2, d2, d3))


def halo_pair(q, offsets):
    d1, d2, d3 = offsets
    reach = d1 + d2 + d3
    right = q >= reach
    q = jnp.where(right, q - reach, q)
    step = jnp.where(q < d1, d1, jnp.where(q < d1 + d2, d2, d3))
    pos = jnp.where(q < d1, q, jnp.where(q < d1 + d2, q - d1, q - d1 - d2))
    one = jnp.where(right, BLOCKS_DEV - 1 - pos, pos)
    return one, jnp.where(right, one + step, one - step)


LISTED = OWN_TILES + HALO_TILES


def tiles_kernel(first, count, beside, held, scalar_ref, jitter_ref, *refs):
    beside_refs, refs = refs[:beside], refs[beside + held :]
    tiles_ref, buf, sem = refs
    a, b = ROOT_THREE * CUTOFF / SPREAD, 4.0
    offsets = offsets_of(scalar_ref)
    place, group = scalar_ref[NEIGHBOURS], scalar_ref[NEIGHBOURS + 1]
    total_rows = scalar_ref[NEIGHBOURS + 2]
    row_dev = STRIP * BLOCKS_DEV
    lane = lax.broadcasted_iota(jnp.int32, (GROUP, COL_DEV), 1)
    within = lax.broadcasted_iota(jnp.int32, (STRIP, COL_DEV), 0)
    across = lax.broadcasted_iota(jnp.int32, (STRIP, COL_DEV), 1)
    col_place = (group * COL_DEV + across).astype(jnp.float32)

    def out_copy(t):
        slot = lax.rem(t - first, TILE_SLOTS)
        return pltpu.make_async_copy(buf.at[slot], tiles_ref.at[t], sem.at[slot])

    def live(t):
        mine = (t < OWN_TILES) & (t < own_count(offsets))
        return mine | ((t >= OWN_TILES) & (t < OWN_TILES + halo_count(offsets)))

    def places(block, ref, at):
        row = lax.rem(place * row_dev + STRIP * block + total_rows, total_rows)
        rows = (row + within).astype(jnp.float32) + ref[0, pl.ds(at, STRIP), :]
        cols = col_place + ref[1, pl.ds(at, STRIP), :]
        return jnp.concatenate([rows, cols], axis=0) * (1.0 / CUTOFF)

    def pair_of(t):
        q = t - OWN_TILES
        one, other = own_pair(t, offsets)
        one_q, other_q = halo_pair(q, offsets)
        same = t < BLOCKS_DEV
        mine = t < OWN_TILES
        one = jnp.where(same, t, jnp.where(mine, one, one_q))
        return one, jnp.where(same, t, jnp.where(mine, other, other_q))

    def evaluate(slot, to, frm, sill):
        for rb in range(STRIP):
            row_b = jnp.broadcast_to(frm[:, rb : rb + 1], (COL_DEV, COL_DEV))
            col_b = jnp.broadcast_to(frm[:, STRIP + rb : STRIP + rb + 1], (COL_DEV, COL_DEV))
            for u in range(COL_DEV // 2 // GROUP):
                lo_s = slice(GROUP * u, GROUP * (u + 1))
                hi_s = slice(64 + GROUP * u, 64 + GROUP * (u + 1))
                near = (lane >= GROUP * u - BAND) & (lane < GROUP * (u + 1) + BAND)
                one_m = jnp.where(near, 1.0, 0.0).astype(jnp.bfloat16)
                other_m = jnp.where(near, 0.0, 1.0).astype(jnp.bfloat16)
                row_s = jnp.where(near, row_b[lo_s], row_b[hi_s])
                col_s = jnp.where(near, col_b[lo_s], col_b[hi_s])
                for ra in range(STRIP):
                    dr = row_s - to[ra : ra + 1]
                    dc = col_s - to[STRIP + ra : STRIP + ra + 1]
                    square = dr * dr + dc * dc
                    far = square * lax.rsqrt(jnp.maximum(square, 1e-30))
                    fading = jnp.maximum(1.0 - far, 0.0)
                    fading = fading * fading
                    fading = fading * fading
                    shape = (1.0 + a * far) * (sill + (sill * b) * far)
                    value = shape * fading * jnp.exp(-a * far)
                    hi = value.astype(jnp.bfloat16)
                    lo = (value - hi.astype(jnp.float32)).astype(jnp.bfloat16)
                    lanes = slice(COL_DEV * ra, COL_DEV * (ra + 1))
                    top = rb * COL_DEV + GROUP * u
                    for part, at in ((hi, top), (lo, BLOCK + top)):
                        buf[slot, at : at + GROUP, lanes] = part * one_m
                        buf[slot, at + 64 : at + 64 + GROUP, lanes] = part * other_m

    def one_tile(t, carry):
        slot = lax.rem(t - first, TILE_SLOTS)
        past = jnp.maximum(t - TILE_SLOTS, first)

        @pl.when((t >= first + TILE_SLOTS) & live(past))
        def _():
            out_copy(past).wait()

        @pl.when(live(t))
        def _():
            one, other = pair_of(t)
            sill = jnp.where(one == other, (NEIGHBOURS + 1.0) * SILL_TERM, SILL_TERM)
            inside = jnp.clip(other, 0, BLOCKS_DEV - 1)
            to = places(one, jitter_ref, STRIP * one)
            frm = places(other, jitter_ref, STRIP * inside)
            if beside_refs:
                left = places(other, beside_refs[0], STRIP * jnp.clip(other + REACH, 0, REACH - 1))
                right = places(
                    other, beside_refs[1], STRIP * jnp.clip(other - BLOCKS_DEV, 0, REACH - 1)
                )
                frm = jnp.where(other < 0, left, jnp.where(other < BLOCKS_DEV, frm, right))
            evaluate(slot, to, frm.T, sill)
            out_copy(t).start()

        return carry

    lax.fori_loop(first, first + count, one_tile, 0)
    for t in range(max(first, first + count - TILE_SLOTS), first + count):

        @pl.when(live(t))
        def _(t=t):
            out_copy(t).wait()


def covariance_tiles(first, count, scalars, jitter, beside_jitter, held):
    extra = [] if held is None else [held]
    ins = [scalars, jitter, *beside_jitter, *extra]
    return pl.pallas_call(
        functools.partial(tiles_kernel, first, count, len(beside_jitter), len(extra)),
        in_specs=[SMEM_SPEC] + [VMEM_SPEC] * (1 + len(beside_jitter)) + [HBM_SPEC] * len(extra),
        out_specs=HBM_SPEC,
        scratch_shapes=[
            pltpu.VMEM((TILE_SLOTS, 2 * BLOCK, BLOCK), jnp.bfloat16),
            pltpu.SemaphoreType.DMA((TILE_SLOTS,)),
        ],
        out_shape=jax.ShapeDtypeStruct((LISTED, 2 * BLOCK, BLOCK), jnp.bfloat16),
        input_output_aliases={len(ins) - 1: 0} if extra else {},
        compiler_params=pltpu.CompilerParams(vmem_limit_bytes=12 << 20),
        cost_estimate=pl.CostEstimate(
            flops=count * 12 * BLOCK * BLOCK,
            bytes_accessed=count * 4 * BLOCK * BLOCK,
            transcendentals=count * BLOCK * BLOCK,
        ),
        name="tiles",
    )(*ins)


def halves(v):
    hi = v.astype(jnp.bfloat16)
    lo = (v - hi.astype(jnp.float32)).astype(jnp.bfloat16)
    return hi, lo


NN = (((1,), (0,)), ((), ()))
NT = (((1,), (1,)), ((), ()))


def product(both, tile_ref, dims):
    fields = both.shape[0] // 2
    main = lax.dot_general(
        both, tile_ref[:BLOCK], dims, preferred_element_type=jnp.float32
    )
    rest = lax.dot_general(
        both[:fields], tile_ref[BLOCK:], dims, preferred_element_type=jnp.float32
    )
    return main[:fields] + (main[fields:] + rest)


def op_kernel(first, last, halo, held, send, scalar_ref, target_ref, *refs):
    refs = list(refs)
    v_ref = refs.pop(0)
    beside_refs = [refs.pop(0), refs.pop(0)] if halo else []
    held_ref = refs.pop(0) if held else None
    tiles_ref, out_ref = refs.pop(0), refs.pop(0)
    slots_ref = refs.pop(0) if send else None
    values, both_ref, total, buf, sem, in_sem, out_sem = refs
    fields = total.shape[1]
    offsets = offsets_of(scalar_ref)
    mine = (own_count(offsets) if last is None else last) - first
    count = mine + (halo_count(offsets) if halo else 0)

    def copy(t):
        slot = lax.rem(t, OP_SLOTS)
        at = jnp.where(t < mine, t + first, t - mine + OWN_TILES)
        return pltpu.make_async_copy(tiles_ref.at[at], buf.at[slot], sem.at[slot])

    loads = [(v_ref, 0, BLOCKS_DEV)]
    for side, ref in enumerate(beside_refs):
        loads.append((ref, BLOCKS_DEV + REACH * side, REACH))
    arriving = [
        pltpu.make_async_copy(ref, values.at[pl.ds(at, size)], in_sem.at[i])
        for i, (ref, at, size) in enumerate(loads)
    ]
    if held_ref is not None:
        arriving.append(pltpu.make_async_copy(held_ref, total, in_sem.at[3]))
    for load in arriving:
        load.start()
    for t in range(OP_SLOTS - 1):
        copy(t).start()
    for load in arriving:
        load.wait()
    for _, at, size in loads:
        for g in range(at, at + size):
            hi, lo = halves(values[g])
            both_ref[g, :fields] = hi
            both_ref[g, fields:] = lo

    def arrive(t):
        @pl.when(t + OP_SLOTS - 1 < count)
        def _():
            copy(t + OP_SLOTS - 1).start()

        copy(t).wait()
        return buf.at[lax.rem(t, OP_SLOTS)]

    def with_itself(t, carry):
        tile = arrive(t)
        total[t] = product(both_ref[t], tile, NN)
        return carry

    def with_another(t, carry):
        tile = arrive(t)
        one, other = own_pair(t + first, offsets)
        total[one] += product(both_ref[other], tile, NN)
        total[other] += product(both_ref[one], tile, NT)
        return carry

    def with_beside(t, carry):
        tile = arrive(t)
        one, other = halo_pair(t - mine, offsets)
        side = BLOCKS_DEV + jnp.where(other < 0, other + REACH, other - BLOCKS_DEV + REACH)
        total[one] += product(both_ref[side], tile, NN)
        return carry

    if first == 0:
        lax.fori_loop(0, BLOCKS_DEV, with_itself, 0)
    lax.fori_loop(max(BLOCKS_DEV - first, 0), mine, with_another, 0)
    if halo:
        lax.fori_loop(mine, count, with_beside, 0)
    leaving = [pltpu.make_async_copy(total, out_ref, out_sem.at[BLOCKS_DEV])]
    if send:
        leaving += out_copies(total, slots_ref, target_ref, out_sem)
    for out in leaving:
        out.start()
    for out in leaving:
        out.wait()


def out_copies(values_ref, slots_ref, target_ref, sem):
    fields = values_ref.shape[1]
    return [
        pltpu.make_async_copy(
            values_ref.at[g], slots_ref.at[target_ref[g], pl.ds(0, fields)], sem.at[g]
        )
        for g in range(BLOCKS_DEV)
    ]


SMEM_SPEC = pl.BlockSpec(memory_space=pltpu.SMEM)
VMEM_SPEC = pl.BlockSpec(memory_space=pltpu.VMEM)
HBM_SPEC = pl.BlockSpec(memory_space=pltpu.HBM)


def in_hbm(x):
    return pltpu.with_memory_space_constraint(x, pltpu.HBM)


def slot_shape(v, extra=0):
    _, fields, points = v.shape
    return pltpu.HBM((lax.axis_size(SIXTEEN), fields + extra, points), jnp.float32)


def applied(scalars, targets, tiles, v, tiles_of=(0, None), beside=(), held=None, extra=None):
    blocks, fields, _ = v.shape
    send = extra is not None
    out = pltpu.HBM(v.shape, jnp.float32)
    ins = [in_hbm(x) for x in (v, *beside, held) if x is not None] + [tiles]
    number = (tiles_of[1] or OWN_TILES) - tiles_of[0] + HALO_TILES * bool(beside)
    out = pl.pallas_call(
        functools.partial(op_kernel, *tiles_of, bool(beside), held is not None, send),
        in_specs=[SMEM_SPEC] * 2 + [HBM_SPEC] * len(ins),
        out_specs=[HBM_SPEC] * (1 + send),
        scratch_shapes=[
            pltpu.VMEM((blocks + 2 * REACH, fields, BLOCK), jnp.float32),
            pltpu.VMEM((blocks + 2 * REACH, 2 * fields, BLOCK), jnp.bfloat16),
            pltpu.VMEM(v.shape, jnp.float32),
            pltpu.VMEM((OP_SLOTS, 2 * BLOCK, BLOCK), jnp.bfloat16),
            pltpu.SemaphoreType.DMA((OP_SLOTS,)),
            pltpu.SemaphoreType.DMA((4,)),
            pltpu.SemaphoreType.DMA((BLOCKS_DEV + 1,)),
        ],
        out_shape=[out] + [slot_shape(v, extra or 0)] * send,
        compiler_params=pltpu.CompilerParams(vmem_limit_bytes=24 << 20),
        cost_estimate=pl.CostEstimate(
            flops=3 * number * 3 * fields * BLOCK * BLOCK,
            bytes_accessed=number * 4 * BLOCK * BLOCK,
            transcendentals=0,
        ),
        name="applied",
    )(scalars, targets, *ins)
    return out if send else out[0]


def gate_kernel(*refs):
    pass


def gate(slots, *others):
    return pl.pallas_call(
        gate_kernel,
        in_specs=[HBM_SPEC] + [VMEM_SPEC] * len(others),
        out_specs=HBM_SPEC,
        out_shape=pltpu.HBM(slots.shape, jnp.float32),
        input_output_aliases={0: 0},
        compiler_params=pltpu.CompilerParams(vmem_limit_bytes=1 << 20),
        name="gate",
    )(slots, *(other[0, :8, :COL_DEV] for other in others))


def attach_kernel(rows_ref, slots_ref, out_ref, sem):
    rows = rows_ref.shape[0]
    copies = [
        pltpu.make_async_copy(
            rows_ref, out_ref.at[o, pl.ds(out_ref.shape[1] - rows, rows)], sem.at[o]
        )
        for o in range(out_ref.shape[0])
    ]
    for copy in copies:
        copy.start()
    for copy in copies:
        copy.wait()


def attach(slots, rows):
    return pl.pallas_call(
        attach_kernel,
        in_specs=[VMEM_SPEC, HBM_SPEC],
        out_specs=HBM_SPEC,
        scratch_shapes=[pltpu.SemaphoreType.DMA((slots.shape[0],))],
        out_shape=pltpu.HBM(slots.shape, jnp.float32),
        input_output_aliases={1: 0},
        compiler_params=pltpu.CompilerParams(vmem_limit_bytes=1 << 20),
        name="attach",
    )(rows, slots)


def residual_kernel(
    target_ref, obs_ref, weight_ref, row_ref, before_ref, before_row_ref, after_ref,
    after_row_ref, col_ref, out_ref, before_out_ref, after_out_ref, slots_ref, buf, sem,
):
    fields = obs_ref.shape[0]
    col = col_ref[...]

    def block(at, obs, weight, row, g):
        for ra in range(STRIP):
            r = STRIP * g + ra
            left = obs[:fields, r, :] - row[:, r : r + 1] - col
            weighted = weight[r : r + 1, :] * left
            buf[at, :, COL_DEV * ra : COL_DEV * (ra + 1)] = weighted

    copies = []
    for g in range(BLOCKS_DEV):
        block(g, obs_ref, weight_ref, row_ref, g)
        copies.append(
            pltpu.make_async_copy(buf.at[g], slots_ref.at[target_ref[g]], sem.at[g])
        )
        copies[-1].start()
    copies.append(
        pltpu.make_async_copy(buf.at[pl.ds(0, BLOCKS_DEV)], out_ref, sem.at[BLOCKS_DEV])
    )
    copies[-1].start()
    sides = ((before_ref, before_row_ref, before_out_ref), (after_ref, after_row_ref, after_out_ref))
    for side, (obs, row, out) in enumerate(sides):
        first = BLOCKS_DEV + REACH * side
        for g in range(REACH):
            block(first + g, obs, obs.at[fields], row, g)
        copies.append(
            pltpu.make_async_copy(
                buf.at[pl.ds(first, REACH)], out, sem.at[BLOCKS_DEV + 1 + side]
            )
        )
        copies[-1].start()
    for copy in copies:
        copy.wait()


def residual_of(targets, observations, weight, row_effect, before, before_row, after, after_row, col):
    fields = observations.shape[0]
    own = pltpu.HBM((BLOCKS_DEV, fields, BLOCK), jnp.float32)
    side = pltpu.HBM((REACH, fields, BLOCK), jnp.float32)
    return pl.pallas_call(
        residual_kernel,
        in_specs=[SMEM_SPEC] + [VMEM_SPEC] * 8,
        out_specs=[HBM_SPEC] * 4,
        scratch_shapes=[
            pltpu.VMEM((BLOCKS_DEV + 2 * REACH, fields, BLOCK), jnp.float32),
            pltpu.SemaphoreType.DMA((BLOCKS_DEV + 3,)),
        ],
        out_shape=[own, side, side, slot_shape(own)],
        compiler_params=pltpu.CompilerParams(vmem_limit_bytes=12 << 20),
        name="residual",
    )(targets, observations, weight, row_effect, before, before_row, after, after_row, col)


def combine_kernel(src_ref, sums_ref, *refs):
    ins, (x_ref, r_ref, scale_ref) = refs[:-3], refs[-3:]
    part = x_ref.shape[0]

    @pl.when(pl.program_id(0) == 0)
    def _():
        sums = sums_ref[0, :, :COL_DEV]
        for o in range(1, sums_ref.shape[0]):
            sums = sums + sums_ref[o, :, :COL_DEV]
        scale_ref[...] = step_scales(*(sums[k : k + 1] for k in range(4))).T

    scale = scale_ref[pl.ds(pl.multiple_of(pl.program_id(0) * part, part), part), :]
    for j in range(BLOCKS_DEV):
        r0, m1, m2 = (ref[0] for ref in ins[3 * j : 3 * j + 3])
        x_ref[:, j, :] = scale[:, 0:1] * r0 + scale[:, 1:2] * m1
        r_ref[:, j, :] = scale[:, 2:3] * r0 + scale[:, 3:4] * m1 + scale[:, 4:5] * m2


def combined(sources, r0, m1, m2):
    owners, fields, _ = r0.shape
    part = 16
    ins, specs = [], []
    for j in range(BLOCKS_DEV):
        for v in (r0, m1, m2):
            ins.append(v)
            specs.append(
                pl.BlockSpec(
                    (1, part, BLOCK), functools.partial(lambda j, i, s: (s[j], i, 0), j)
                )
            )
    out = pl.BlockSpec((part, BLOCKS_DEV, BLOCK), lambda i, s: (i, 0, 0))
    shape = jax.ShapeDtypeStruct((fields, BLOCKS_DEV, BLOCK), jnp.float32)
    return pl.pallas_call(
        combine_kernel,
        grid_spec=pltpu.PrefetchScalarGridSpec(
            num_scalar_prefetch=1,
            grid=(fields // part,),
            in_specs=[pl.BlockSpec((owners, EXTRA, COL_DEV), lambda i, s: (0, fields // EXTRA, 0))]
            + specs,
            out_specs=[out, out],
            scratch_shapes=[pltpu.VMEM((COL_DEV, 8), jnp.float32)],
        ),
        out_shape=[shape, shape],
        compiler_params=pltpu.CompilerParams(vmem_limit_bytes=20 << 20),
        name="combine",
    )(sources, m2, *ins)


def to_owners(slots):
    return lax.all_to_all(slots, SIXTEEN, 0, 0, tiled=True)


def step_scales(h00, h01, h11, h12):
    mu = h01 / h00
    var = (h11 - mu * h01) / h00
    a0 = 1.0 / (1.0 + mu)
    beta = var * a0 * a0
    skew = (h12 - mu * h11 - mu * (h11 - mu * h01)) / h00
    a1 = var / (var + skew - var * var * a0)
    x_r0 = a0 + a1 * beta + a1 * a0 * mu
    x_m1 = -a1 * a0
    r_r0 = a0 * mu * (1.0 - a1) - a1 * beta
    r_m1 = -a0 * (1.0 - a1) - a1 * a0 * mu - a1 * beta
    r_m2 = a1 * a0
    zero = jnp.zeros_like(mu)
    return jnp.concatenate([x_r0, x_m1, r_r0, r_m1, r_m2, zero, zero, zero], axis=0)


def on_device(observations, huber_scale, observed, jitter, owner_map, neighbours):
    fields, row_dev, col_dev = observations.shape
    sixteen_size = lax.axis_size(SIXTEEN)
    my_place = lax.axis_index(SIXTEEN)
    group_place = lax.axis_index(WIDE)
    total_strips = BLOCKS_DEV * sixteen_size
    weight = observed.astype(jnp.float32)
    spread_scale = huber_scale[:, None, None]

    def with_count(part, count):
        rows = jnp.zeros((8, count.shape[0]), jnp.float32).at[0].set(count)
        return jnp.concatenate([part, rows], axis=0)

    def terms(row_effect, col_effect):
        return weight[None] * jnp.clip(
            (observations - row_effect[:, :, None] - col_effect[:, None, :]) / spread_scale,
            -HUBER_EDGE,
            HUBER_EDGE,
        )

    def sum_wide(part):
        for axis in WIDE[::-1]:
            part = sum_direct(part, axis)
        return part

    row_effect = jnp.zeros((fields, row_dev), jnp.float32)
    col_effect = jnp.zeros((fields, col_dev), jnp.float32)
    part = with_count(jnp.sum(terms(row_effect, col_effect), axis=2), jnp.sum(weight, axis=1))
    part, jitter, owner_map, neighbours = lax.optimization_barrier(
        (part, jitter, owner_map, neighbours)
    )
    group_map = owner_map[0]
    scalars = jnp.concatenate(
        [neighbours[0, 0], jnp.stack([my_place, group_place, total_strips * STRIP])]
    ).astype(jnp.int32)

    def beside_tiles(part, axis, count, tiles, first, near):
        if first:
            part, tiles = lax.optimization_barrier((part, tiles))
        total = over_copies(part, axis)
        tiles = covariance_tiles(first, count, scalars, jitter, near, tiles)
        total, tiles = lax.optimization_barrier((total, tiles))
        return total, tiles, first + count

    edges = jnp.concatenate([observations, weight[None], jitter], axis=0)
    before, after, _ = beside(edges, REACH * STRIP, 1)
    total, tiles, first = beside_tiles(part, WIDE, ROW_TILES, None, 0, ())
    row_count = jnp.maximum(total[fields], 1.0)
    row_effect = huber_scale[:, None] * total[:fields] / row_count[None, :]
    part = with_count(jnp.sum(terms(row_effect, col_effect), axis=1), jnp.sum(weight, axis=0))
    total, tiles, first = beside_tiles(part, SIXTEEN, COL_TILES, tiles, first, ())
    total, before, after = lax.optimization_barrier((total, before, after))
    near = (before[fields + 1 :], after[fields + 1 :])
    col_count = jnp.maximum(total[fields], 1.0)
    col_effect = huber_scale[:, None] * total[:fields] / col_count[None, :]
    part = jnp.sum(terms(row_effect, col_effect), axis=2)
    total, tiles, first = beside_tiles(part, WIDE, ROW_TILES, tiles, first, near)
    row_effect = row_effect + huber_scale[:, None] * total / row_count[None, :]
    part = jnp.sum(terms(row_effect, col_effect), axis=1)
    row_before, row_after, _ = beside(row_effect, REACH * STRIP, 1)
    total, tiles, first = beside_tiles(part, SIXTEEN, COL_TILES, tiles, first, near)
    col_effect = col_effect + huber_scale[:, None] * total / col_count[None, :]

    my_targets = lax.dynamic_slice_in_dim(group_map, my_place * BLOCKS_DEV, BLOCKS_DEV)
    r0, r0_before, r0_after, slots = residual_of(
        my_targets, observations, weight, row_effect, before, row_before, after, row_after, col_effect
    )
    owned_r0 = to_owners(slots)
    m1, slots = applied(
        scalars, my_targets, tiles, r0, beside=(r0_before, r0_after), extra=0
    )
    before, after, m1 = beside(m1, REACH)
    part = applied(scalars, my_targets, tiles, m1, (0, EARLY_TILES))
    slots = gate(slots, part, before, after, owned_r0)
    owned_m1 = to_owners(slots)
    m2, slots = applied(
        scalars, my_targets, tiles, m1, (EARLY_TILES, None), (before, after), part, EXTRA
    )
    dots = jnp.stack(
        [jnp.sum(p * q, axis=(0, 2)) for p, q in ((r0, r0), (r0, m1), (m1, m1), (m1, m2))]
    )
    dots = sum_direct(dots, WIDE)
    slots = attach(slots, jnp.pad(dots, ((0, EXTRA - 4), (0, BLOCK - fields))))
    slots = gate(slots, owned_m1)
    owned_m2 = to_owners(slots)
    owned = owned_table(group_map, sixteen_size, BLOCKS_DEV)
    my_ids = lax.dynamic_index_in_dim(owned, my_place, 0, keepdims=False)
    solution_now, residual_now = combined(my_ids // BLOCKS_DEV, owned_r0, owned_m1, owned_m2)
    return (solution_now[None, None], residual_now[None, None])


def solution(mesh):
    finer = Mesh(mesh.devices.reshape(4, 2, 4, 4), ("wide_0", "wide_1", "sixteen_0", "sixteen_1"))
    in_specs = (
        P(None, SIXTEEN, WIDE),
        P(),
        P(SIXTEEN, WIDE),
        P(None, SIXTEEN, WIDE),
        P(WIDE, None),
        P(WIDE, None, None),
    )
    out_specs = (P(WIDE, SIXTEEN, None, None, None), P(WIDE, SIXTEEN, None, None, None))
    return jax.shard_map(
        on_device, mesh=finer, in_specs=in_specs, out_specs=out_specs, check_vma=False
    )
```

```python
import functools

import jax
import jax.numpy as jnp
from jax import lax
from jax.experimental import pallas as pl
from jax.experimental.pallas import tpu as pltpu
from jax.sharding import Mesh
from jax.sharding import PartitionSpec as P

BLOCK = 512
BLOCKS_DEV = 8
REACH = 4
NEIGHBOURS = 6
PAIRED = NEIGHBOURS // 2
SWEEPS = 2
STRIP = 4
COL_DEV = 128
WIDE = ("wide_0", "wide_1")
SIXTEEN = ("sixteen_0", "sixteen_1")

HUBER_EDGE = 1.345
SILL_TERM = 0.02
ROOT_THREE = 1.7320508075688772
LOG2_E = 1.4426950408889634
SPREAD = 2.0 * STRIP
CUTOFF = 6.0 * STRIP
BAND = 24
GROUP = 16

OWN_TILES = BLOCKS_DEV + PAIRED * BLOCKS_DEV - 6
HALO_TILES = 2 * (2 + 3 + 4)
CHUNKS = (5, 9, 12, 18)
TILE_SLOTS = 4
OP_SLOTS = 5
EXTRA = 8
EARLY_TILES = 12


def sent_to_all(shard, axis):
    peers = lax.axis_size(axis)
    return lax.all_to_all(
        jnp.broadcast_to(shard[None], (peers, *shard.shape)), axis, 0, 0, tiled=True
    )


def over_copies(shard, axis):
    return jnp.sum(sent_to_all(shard, axis), axis=0)


def sum_direct(part, axis):
    peers = lax.axis_size(axis)
    moved = [
        lax.ppermute(part, axis, [(i, (i + k) % peers) for i in range(peers)])
        for k in range(1, peers)
    ]
    return functools.reduce(jnp.add, moved, part)


def beside(shard, width, dim=0):
    peers, length = lax.axis_size(SIXTEEN), shard.shape[dim]
    up = [(i, (i + 1) % peers) for i in range(peers)]
    down = [(j, i) for i, j in up]
    last = lax.slice_in_dim(shard, length - width, length, axis=dim)
    initial = lax.slice_in_dim(shard, 0, width, axis=dim)
    shard, last, initial = lax.optimization_barrier((shard, last, initial))
    return lax.ppermute(last, SIXTEEN, up), lax.ppermute(initial, SIXTEEN, down), shard


def owned_table(group_map, owners, per_owner):
    total_strips = group_map.shape[0]
    member = (group_map[None, :] == jnp.arange(owners, dtype=jnp.int32)[:, None]).astype(jnp.int32)
    ranked = jnp.cumsum(member, axis=1, dtype=jnp.int32) - 1
    slot_hit = (ranked[:, :, None] == jnp.arange(per_owner, dtype=jnp.int32)[None, None, :]).astype(
        jnp.int32
    ) * member[:, :, None]
    numbers = jnp.arange(total_strips, dtype=jnp.int32)
    return jnp.sum(slot_hit * numbers[None, :, None], axis=1, dtype=jnp.int32)


def offsets_of(list_ref):
    held = [
        functools.reduce(jnp.logical_or, [list_ref[n] == d for n in range(NEIGHBOURS)])
        for d in range(1, REACH)
    ]
    missing = jnp.where(held[0], jnp.where(held[1], jnp.where(held[2], 4, 3), 2), 1)
    return [k + jnp.where(missing <= k, 1, 0) for k in range(1, PAIRED + 1)]


def own_count(offsets):
    return (PAIRED + 1) * BLOCKS_DEV - (offsets[0] + offsets[1] + offsets[2])


def halo_count(offsets):
    return 2 * (offsets[0] + offsets[1] + offsets[2])


def own_pair(t, offsets):
    d1, d2, d3 = offsets
    p = t - BLOCKS_DEV
    n1, n2 = BLOCKS_DEV - d1, 2 * BLOCKS_DEV - d1 - d2
    one = jnp.where(p < n1, p, jnp.where(p < n2, p - n1, p - n2))
    return one, one + jnp.where(p < n1, d1, jnp.where(p < n2, d2, d3))


def halo_pair(q, offsets):
    d1, d2, d3 = offsets
    reach = d1 + d2 + d3
    right = q >= reach
    q = jnp.where(right, q - reach, q)
    step = jnp.where(q < d1, d1, jnp.where(q < d1 + d2, d2, d3))
    pos = jnp.where(q < d1, q, jnp.where(q < d1 + d2, q - d1, q - d1 - d2))
    one = jnp.where(right, BLOCKS_DEV - 1 - pos, pos)
    return one, jnp.where(right, one + step, one - step)


LISTED = OWN_TILES + HALO_TILES


def tiles_kernel(first, count, beside, held, scalar_ref, jitter_ref, *refs):
    beside_refs, refs = refs[:beside], refs[beside + held :]
    tiles_ref, buf, sem = refs
    a, b = ROOT_THREE * CUTOFF / SPREAD, 4.0
    offsets = offsets_of(scalar_ref)
    place, group = scalar_ref[NEIGHBOURS], scalar_ref[NEIGHBOURS + 1]
    total_rows = scalar_ref[NEIGHBOURS + 2]
    row_dev = STRIP * BLOCKS_DEV
    lane = lax.broadcasted_iota(jnp.int32, (GROUP, COL_DEV), 1)
    within = lax.broadcasted_iota(jnp.int32, (STRIP, COL_DEV), 0)
    across = lax.broadcasted_iota(jnp.int32, (STRIP, COL_DEV), 1)
    col_place = (group * COL_DEV + across).astype(jnp.float32)

    def out_copy(t):
        slot = lax.rem(t - first, TILE_SLOTS)
        return pltpu.make_async_copy(buf.at[slot], tiles_ref.at[t], sem.at[slot])

    def live(t):
        mine = (t < OWN_TILES) & (t < own_count(offsets))
        return mine | ((t >= OWN_TILES) & (t < OWN_TILES + halo_count(offsets)))

    def places(block, ref, at):
        row = lax.rem(place * row_dev + STRIP * block + total_rows, total_rows)
        rows = (row + within).astype(jnp.float32) + ref[0, pl.ds(at, STRIP), :]
        cols = col_place + ref[1, pl.ds(at, STRIP), :]
        return jnp.concatenate([rows, cols], axis=0) * (1.0 / CUTOFF)

    def pair_of(t):
        q = t - OWN_TILES
        one, other = own_pair(t, offsets)
        one_q, other_q = halo_pair(q, offsets)
        same = t < BLOCKS_DEV
        mine = t < OWN_TILES
        one = jnp.where(same, t, jnp.where(mine, one, one_q))
        return one, jnp.where(same, t, jnp.where(mine, other, other_q))

    def evaluate(slot, to, frm, sill):
        for rb in range(STRIP):
            row_b = jnp.broadcast_to(frm[rb : rb + 1], (COL_DEV, COL_DEV)).T
            col_b = jnp.broadcast_to(frm[STRIP + rb : STRIP + rb + 1], (COL_DEV, COL_DEV)).T
            for u in range(COL_DEV // 2 // GROUP):
                lo_s = slice(GROUP * u, GROUP * (u + 1))
                hi_s = slice(64 + GROUP * u, 64 + GROUP * (u + 1))
                near = (lane >= GROUP * u - BAND) & (lane < GROUP * (u + 1) + BAND)
                one_m = jnp.where(near, 1.0, 0.0).astype(jnp.bfloat16)
                other_m = jnp.where(near, 0.0, 1.0).astype(jnp.bfloat16)
                row_s = jnp.where(near, row_b[lo_s], row_b[hi_s])
                col_s = jnp.where(near, col_b[lo_s], col_b[hi_s])
                for ra in range(STRIP):
                    dr = row_s - to[ra : ra + 1]
                    dc = col_s - to[STRIP + ra : STRIP + ra + 1]
                    square = dr * dr + dc * dc
                    far = square * lax.rsqrt(jnp.maximum(square, 1e-30))
                    fading = jnp.maximum(1.0 - far, 0.0)
                    fading = fading * fading
                    fading = fading * fading
                    shape = (sill + (sill * (a + b)) * far) + (sill * (a * b)) * square
                    value = shape * fading * jnp.exp2((-a * LOG2_E) * far)
                    hi = value.astype(jnp.bfloat16)
                    lo = (value - hi.astype(jnp.float32)).astype(jnp.bfloat16)
                    lanes = slice(COL_DEV * ra, COL_DEV * (ra + 1))
                    top = rb * COL_DEV + GROUP * u
                    for part, at in ((hi, top), (lo, BLOCK + top)):
                        buf[slot, at : at + GROUP, lanes] = part * one_m
                        buf[slot, at + 64 : at + 64 + GROUP, lanes] = part * other_m

    def one_tile(t, carry):
        slot = lax.rem(t - first, TILE_SLOTS)
        past = jnp.maximum(t - TILE_SLOTS, first)

        @pl.when((t >= first + TILE_SLOTS) & live(past))
        def _():
            out_copy(past).wait()

        @pl.when(live(t))
        def _():
            one, other = pair_of(t)
            sill = jnp.where(one == other, (NEIGHBOURS + 1.0) * SILL_TERM, SILL_TERM)
            inside = jnp.clip(other, 0, BLOCKS_DEV - 1)
            to = places(one, jitter_ref, STRIP * one)
            frm = places(other, jitter_ref, STRIP * inside)
            if beside_refs:
                left = places(other, beside_refs[0], STRIP * jnp.clip(other + REACH, 0, REACH - 1))
                right = places(
                    other, beside_refs[1], STRIP * jnp.clip(other - BLOCKS_DEV, 0, REACH - 1)
                )
                frm = jnp.where(other < 0, left, jnp.where(other < BLOCKS_DEV, frm, right))
            evaluate(slot, to, frm, sill)
            out_copy(t).start()

        return carry

    lax.fori_loop(first, first + count, one_tile, 0)
    for t in range(max(first, first + count - TILE_SLOTS), first + count):

        @pl.when(live(t))
        def _(t=t):
            out_copy(t).wait()


def covariance_tiles(first, count, scalars, jitter, beside_jitter, held):
    extra = [] if held is None else [held]
    ins = [scalars, jitter, *beside_jitter, *extra]
    return pl.pallas_call(
        functools.partial(tiles_kernel, first, count, len(beside_jitter), len(extra)),
        in_specs=[SMEM_SPEC] + [VMEM_SPEC] * (1 + len(beside_jitter)) + [HBM_SPEC] * len(extra),
        out_specs=HBM_SPEC,
        scratch_shapes=[
            pltpu.VMEM((TILE_SLOTS, 2 * BLOCK, BLOCK), jnp.bfloat16),
            pltpu.SemaphoreType.DMA((TILE_SLOTS,)),
        ],
        out_shape=jax.ShapeDtypeStruct((LISTED, 2 * BLOCK, BLOCK), jnp.bfloat16),
        input_output_aliases={len(ins) - 1: 0} if extra else {},
        compiler_params=pltpu.CompilerParams(vmem_limit_bytes=12 << 20),
        cost_estimate=pl.CostEstimate(
            flops=count * 12 * BLOCK * BLOCK,
            bytes_accessed=count * 4 * BLOCK * BLOCK,
            transcendentals=count * BLOCK * BLOCK,
        ),
        name="tiles",
    )(*ins)


def halves(v):
    hi = v.astype(jnp.bfloat16)
    lo = (v - hi.astype(jnp.float32)).astype(jnp.bfloat16)
    return hi, lo


NN = (((1,), (0,)), ((), ()))
NT = (((1,), (1,)), ((), ()))


def product(both, tile_ref, dims):
    fields = both.shape[0] // 2
    main = lax.dot_general(
        both, tile_ref[:BLOCK], dims, preferred_element_type=jnp.float32
    )
    rest = lax.dot_general(
        both[:fields], tile_ref[BLOCK:], dims, preferred_element_type=jnp.float32
    )
    return main[:fields] + (main[fields:] + rest)


def op_kernel(first, last, halo, held, send, scalar_ref, target_ref, *refs):
    refs = list(refs)
    v_ref = refs.pop(0)
    beside_refs = [refs.pop(0), refs.pop(0)] if halo else []
    held_ref = refs.pop(0) if held else None
    tiles_ref, out_ref = refs.pop(0), refs.pop(0)
    slots_ref, dots_ref = (refs.pop(0), refs.pop(0)) if send else (None, None)
    values, both_ref, total, buf, sem, in_sem, out_sem = refs
    fields = total.shape[1]
    offsets = offsets_of(scalar_ref)
    mine = (own_count(offsets) if last is None else last) - first
    count = mine + (halo_count(offsets) if halo else 0)

    def copy(t):
        slot = lax.rem(t, OP_SLOTS)
        at = jnp.where(t < mine, t + first, t - mine + OWN_TILES)
        return pltpu.make_async_copy(tiles_ref.at[at], buf.at[slot], sem.at[slot])

    loads = [(v_ref, 0, BLOCKS_DEV)]
    for side, ref in enumerate(beside_refs):
        loads.append((ref, BLOCKS_DEV + REACH * side, REACH))
    arriving = [
        pltpu.make_async_copy(ref, values.at[pl.ds(at, size)], in_sem.at[i])
        for i, (ref, at, size) in enumerate(loads)
    ]
    if held_ref is not None:
        arriving.append(pltpu.make_async_copy(held_ref, total, in_sem.at[3]))
    for load in arriving:
        load.start()
    for t in range(OP_SLOTS - 1):
        copy(t).start()
    for load in arriving:
        load.wait()
    for _, at, size in loads:
        for g in range(at, at + size):
            hi, lo = halves(values[g])
            both_ref[g, :fields] = hi
            both_ref[g, fields:] = lo

    def arrive(t):
        @pl.when(t + OP_SLOTS - 1 < count)
        def _():
            copy(t + OP_SLOTS - 1).start()

        copy(t).wait()
        return buf.at[lax.rem(t, OP_SLOTS)]

    def with_itself(t, carry):
        tile = arrive(t)
        total[t] = product(both_ref[t], tile, NN)
        return carry

    def with_another(t, carry):
        tile = arrive(t)
        one, other = own_pair(t + first, offsets)
        total[one] += product(both_ref[other], tile, NN)
        total[other] += product(both_ref[one], tile, NT)
        return carry

    def with_beside(t, carry):
        tile = arrive(t)
        one, other = halo_pair(t - mine, offsets)
        side = BLOCKS_DEV + jnp.where(other < 0, other + REACH, other - BLOCKS_DEV + REACH)
        total[one] += product(both_ref[side], tile, NN)
        return carry

    if first == 0:
        lax.fori_loop(0, BLOCKS_DEV, with_itself, 0)
    lax.fori_loop(max(BLOCKS_DEV - first, 0), mine, with_another, 0)
    if halo:
        lax.fori_loop(mine, count, with_beside, 0)
    leaving = [pltpu.make_async_copy(total, out_ref, out_sem.at[STRIP * BLOCKS_DEV])]
    if send:
        leaving += out_copies(total, slots_ref, target_ref, out_sem)
    for out in leaving:
        out.start()
    if send:
        lane = lax.broadcasted_iota(jnp.int32, (fields, COL_DEV), 1)
        dots = jnp.zeros((fields, COL_DEV), jnp.float32)
        for at, one, other in products_of(values, total, held):
            summed = functools.reduce(jnp.add, [one[g] * other[g] for g in range(BLOCKS_DEV)])
            dots = jnp.where(lane == at, jnp.sum(summed, axis=1, keepdims=True), dots)
        dots = jnp.concatenate([dots, jnp.zeros((COL_DEV - fields, COL_DEV), jnp.float32)], axis=0)
        dots_ref[...] = dots.T[:EXTRA]
    for out in leaving:
        out.wait()


def products_of(v, image, second):
    if second:
        return [(3, v, image)]
    return [(0, v, v), (1, v, image), (2, image, image)]


def out_copies(values_ref, slots_ref, target_ref, sem):
    fields = values_ref.shape[1]
    if slots_ref.shape[2] == BLOCK:
        return [
            pltpu.make_async_copy(values_ref.at[g], slots_ref.at[target_ref[g]], sem.at[g])
            for g in range(BLOCKS_DEV)
        ]
    return [
        pltpu.make_async_copy(
            values_ref.at[g, :, pl.ds(COL_DEV * ra, COL_DEV)],
            slots_ref.at[target_ref[g], pl.ds(fields * ra, fields)],
            sem.at[STRIP * g + ra],
        )
        for g in range(BLOCKS_DEV)
        for ra in range(STRIP)
    ]


SMEM_SPEC = pl.BlockSpec(memory_space=pltpu.SMEM)
VMEM_SPEC = pl.BlockSpec(memory_space=pltpu.VMEM)
HBM_SPEC = pl.BlockSpec(memory_space=pltpu.HBM)


def in_hbm(x):
    return pltpu.with_memory_space_constraint(x, pltpu.HBM)


def slot_shape(v, extra=0):
    _, fields, points = v.shape
    block = (STRIP * fields + extra, points // STRIP) if extra else (fields, points)
    return pltpu.HBM((lax.axis_size(SIXTEEN), *block), jnp.float32)


def applied(scalars, targets, tiles, v, tiles_of=(0, None), beside=(), held=None, extra=None):
    blocks, fields, _ = v.shape
    send = extra is not None
    out = pltpu.HBM(v.shape, jnp.float32)
    ins = [in_hbm(x) for x in (v, *beside, held) if x is not None] + [tiles]
    number = (tiles_of[1] or OWN_TILES) - tiles_of[0] + HALO_TILES * bool(beside)
    out = pl.pallas_call(
        functools.partial(op_kernel, *tiles_of, bool(beside), held is not None, send),
        in_specs=[SMEM_SPEC] * 2 + [HBM_SPEC] * len(ins),
        out_specs=[HBM_SPEC] + [HBM_SPEC, VMEM_SPEC] * send,
        scratch_shapes=[
            pltpu.VMEM((blocks + 2 * REACH, fields, BLOCK), jnp.float32),
            pltpu.VMEM((blocks + 2 * REACH, 2 * fields, BLOCK), jnp.bfloat16),
            pltpu.VMEM(v.shape, jnp.float32),
            pltpu.VMEM((OP_SLOTS, 2 * BLOCK, BLOCK), jnp.bfloat16),
            pltpu.SemaphoreType.DMA((OP_SLOTS,)),
            pltpu.SemaphoreType.DMA((4,)),
            pltpu.SemaphoreType.DMA((STRIP * BLOCKS_DEV + 1,)),
        ],
        out_shape=[out]
        + [slot_shape(v, extra or 0), jax.ShapeDtypeStruct((EXTRA, COL_DEV), jnp.float32)] * send,
        compiler_params=pltpu.CompilerParams(vmem_limit_bytes=24 << 20),
        cost_estimate=pl.CostEstimate(
            flops=3 * number * 3 * fields * BLOCK * BLOCK,
            bytes_accessed=number * 4 * BLOCK * BLOCK,
            transcendentals=0,
        ),
        name="applied",
    )(scalars, targets, *ins)
    return out if send else out[0]


def gate_kernel(*refs):
    pass


def gate(slots, *others):
    return pl.pallas_call(
        gate_kernel,
        in_specs=[HBM_SPEC] + [VMEM_SPEC] * len(others),
        out_specs=HBM_SPEC,
        out_shape=pltpu.HBM(slots.shape, jnp.float32),
        input_output_aliases={0: 0},
        compiler_params=pltpu.CompilerParams(vmem_limit_bytes=1 << 20),
        name="gate",
    )(slots, *(other[0, :8, :COL_DEV] for other in others))


def attach_kernel(rows_ref, slots_ref, out_ref, sem):
    rows = rows_ref.shape[0]
    copies = [
        pltpu.make_async_copy(
            rows_ref, out_ref.at[o, pl.ds(out_ref.shape[1] - rows, rows)], sem.at[o]
        )
        for o in range(out_ref.shape[0])
    ]
    for copy in copies:
        copy.start()
    for copy in copies:
        copy.wait()


def attach(slots, rows):
    return pl.pallas_call(
        attach_kernel,
        in_specs=[VMEM_SPEC, HBM_SPEC],
        out_specs=HBM_SPEC,
        scratch_shapes=[pltpu.SemaphoreType.DMA((slots.shape[0],))],
        out_shape=pltpu.HBM(slots.shape, jnp.float32),
        input_output_aliases={1: 0},
        compiler_params=pltpu.CompilerParams(vmem_limit_bytes=1 << 20),
        name="attach",
    )(rows, slots)


def residual_kernel(
    target_ref, obs_ref, weight_ref, row_ref, before_ref, before_row_ref, after_ref,
    after_row_ref, col_ref, out_ref, before_out_ref, after_out_ref, slots_ref, buf, sem,
):
    fields = obs_ref.shape[0]
    col = col_ref[...]

    def block(at, obs, weight, row, g):
        for ra in range(STRIP):
            r = STRIP * g + ra
            left = obs[:fields, r, :] - row[:, r : r + 1] - col
            weighted = weight[r : r + 1, :] * left
            buf[at, :, COL_DEV * ra : COL_DEV * (ra + 1)] = weighted

    copies = []
    for g in range(BLOCKS_DEV):
        block(g, obs_ref, weight_ref, row_ref, g)
        copies.append(
            pltpu.make_async_copy(buf.at[g], slots_ref.at[target_ref[g]], sem.at[g])
        )
        copies[-1].start()
    copies.append(
        pltpu.make_async_copy(buf.at[pl.ds(0, BLOCKS_DEV)], out_ref, sem.at[BLOCKS_DEV])
    )
    copies[-1].start()
    sides = ((before_ref, before_row_ref, before_out_ref), (after_ref, after_row_ref, after_out_ref))
    for side, (obs, row, out) in enumerate(sides):
        first = BLOCKS_DEV + REACH * side
        for g in range(REACH):
            block(first + g, obs, obs.at[fields], row, g)
        copies.append(
            pltpu.make_async_copy(
                buf.at[pl.ds(first, REACH)], out, sem.at[BLOCKS_DEV + 1 + side]
            )
        )
        copies[-1].start()
    for copy in copies:
        copy.wait()


def residual_of(targets, observations, weight, row_effect, before, before_row, after, after_row, col):
    fields = observations.shape[0]
    own = pltpu.HBM((BLOCKS_DEV, fields, BLOCK), jnp.float32)
    side = pltpu.HBM((REACH, fields, BLOCK), jnp.float32)
    return pl.pallas_call(
        residual_kernel,
        in_specs=[SMEM_SPEC] + [VMEM_SPEC] * 8,
        out_specs=[HBM_SPEC] * 4,
        scratch_shapes=[
            pltpu.VMEM((BLOCKS_DEV + 2 * REACH, fields, BLOCK), jnp.float32),
            pltpu.SemaphoreType.DMA((BLOCKS_DEV + 3,)),
        ],
        out_shape=[own, side, side, slot_shape(own)],
        compiler_params=pltpu.CompilerParams(vmem_limit_bytes=12 << 20),
        name="residual",
    )(targets, observations, weight, row_effect, before, before_row, after, after_row, col)


def combine_kernel(src_ref, sums_ref, *refs):
    ins, (x_ref, r_ref, scale_ref) = refs[:-3], refs[-3:]
    part = x_ref.shape[0]

    @pl.when(pl.program_id(0) == 0)
    def _():
        sums = functools.reduce(jnp.add, [sums_ref[o] for o in range(sums_ref.shape[0])])
        scale_ref[...] = step_scales(*(sums[k : k + 1] for k in range(4))).T

    scale = scale_ref[pl.ds(pl.multiple_of(pl.program_id(0) * part, part), part), :]
    for j in range(BLOCKS_DEV):
        r0_ref, m1_ref, *m2_refs = ins[(2 + STRIP) * j : (2 + STRIP) * (j + 1)]
        for ra in range(STRIP):
            lanes = slice(COL_DEV * ra, COL_DEV * (ra + 1))
            r0, m1, m2 = r0_ref[0, :, lanes], m1_ref[0, :, lanes], m2_refs[ra][0]
            x_ref[:, j, lanes] = scale[:, 0:1] * r0 + scale[:, 1:2] * m1
            r_ref[:, j, lanes] = scale[:, 2:3] * r0 + scale[:, 3:4] * m1 + scale[:, 4:5] * m2


def combined(sources, r0, m1, m2):
    owners, fields, _ = r0.shape
    part = 16
    ins, specs = [], []
    r0, m1 = in_hbm(r0), in_hbm(m1)

    def chosen(j, points, at):
        return pl.BlockSpec((1, part, points), lambda i, s: (s[j], at // part + i, 0))

    for j in range(BLOCKS_DEV):
        ins += [r0, m1] + [m2] * STRIP
        specs += [chosen(j, BLOCK, 0)] * 2
        specs += [chosen(j, COL_DEV, fields * ra) for ra in range(STRIP)]
    out = pl.BlockSpec((part, BLOCKS_DEV, BLOCK), lambda i, s: (i, 0, 0))
    shape = jax.ShapeDtypeStruct((fields, BLOCKS_DEV, BLOCK), jnp.float32)
    return pl.pallas_call(
        combine_kernel,
        grid_spec=pltpu.PrefetchScalarGridSpec(
            num_scalar_prefetch=1,
            grid=(fields // part,),
            in_specs=[
                pl.BlockSpec((owners, EXTRA, COL_DEV), lambda i, s: (0, STRIP * fields // EXTRA, 0))
            ]
            + specs,
            out_specs=[out, out],
            scratch_shapes=[pltpu.VMEM((COL_DEV, 8), jnp.float32)],
        ),
        out_shape=[shape, shape],
        compiler_params=pltpu.CompilerParams(vmem_limit_bytes=20 << 20),
        name="combine",
    )(sources, m2, *ins)


def to_owners(slots):
    return lax.all_to_all(slots, SIXTEEN, 0, 0, tiled=True)


def step_scales(h00, h01, h11, h12):
    mu = h01 / h00
    var = (h11 - mu * h01) / h00
    a0 = 1.0 / (1.0 + mu)
    beta = var * a0 * a0
    skew = (h12 - mu * h11 - mu * (h11 - mu * h01)) / h00
    a1 = var / (var + skew - var * var * a0)
    x_r0 = a0 + a1 * beta + a1 * a0 * mu
    x_m1 = -a1 * a0
    r_r0 = a0 * mu * (1.0 - a1) - a1 * beta
    r_m1 = -a0 * (1.0 - a1) - a1 * a0 * mu - a1 * beta
    r_m2 = a1 * a0
    zero = jnp.zeros_like(mu)
    return jnp.concatenate([x_r0, x_m1, r_r0, r_m1, r_m2, zero, zero, zero], axis=0)


def on_device(observations, huber_scale, observed, jitter, owner_map, neighbours):
    fields, row_dev, col_dev = observations.shape
    sixteen_size = lax.axis_size(SIXTEEN)
    my_place = lax.axis_index(SIXTEEN)
    group_place = lax.axis_index(WIDE)
    total_strips = BLOCKS_DEV * sixteen_size
    weight = observed.astype(jnp.float32)
    spread_scale = huber_scale[:, None, None]

    def with_count(part, count):
        rows = jnp.zeros((8, count.shape[0]), jnp.float32).at[0].set(count)
        return jnp.concatenate([part, rows], axis=0)

    def terms(row_effect, col_effect):
        return weight[None] * jnp.clip(
            (observations - row_effect[:, :, None] - col_effect[:, None, :]) / spread_scale,
            -HUBER_EDGE,
            HUBER_EDGE,
        )

    def sum_wide(part):
        for axis in WIDE[::-1]:
            part = sum_direct(part, axis)
        return part

    row_effect = jnp.zeros((fields, row_dev), jnp.float32)
    col_effect = jnp.zeros((fields, col_dev), jnp.float32)
    part = with_count(jnp.sum(terms(row_effect, col_effect), axis=2), jnp.sum(weight, axis=1))
    part, jitter, owner_map, neighbours = lax.optimization_barrier(
        (part, jitter, owner_map, neighbours)
    )
    group_map = owner_map[0]
    scalars = jnp.concatenate(
        [neighbours[0, 0], jnp.stack([my_place, group_place, total_strips * STRIP])]
    ).astype(jnp.int32)

    def beside_tiles(part, axis, chunk, tiles, near=()):
        first = sum(CHUNKS[:chunk])
        if chunk:
            part, tiles = lax.optimization_barrier((part, tiles))
        received = sent_to_all(part, axis)
        tiles = covariance_tiles(first, CHUNKS[chunk], scalars, jitter, near, tiles)
        return lax.optimization_barrier((received, tiles))

    edges = jnp.concatenate([observations, weight[None], jitter], axis=0)
    before, after, _ = beside(edges, REACH * STRIP, 1)
    received, tiles = beside_tiles(part, WIDE, 0, None)
    total = jnp.sum(received, axis=0)
    row_count = jnp.maximum(total[fields], 1.0)
    row_effect = huber_scale[:, None] * total[:fields] / row_count[None, :]
    part = with_count(jnp.sum(terms(row_effect, col_effect), axis=1), jnp.sum(weight, axis=0))
    received, tiles = beside_tiles(part, SIXTEEN, 1, tiles)
    total = jnp.sum(received, axis=0)
    col_count = jnp.maximum(total[fields], 1.0)
    col_effect = huber_scale[:, None] * total[:fields] / col_count[None, :]
    part = jnp.sum(terms(row_effect, col_effect), axis=2)
    received, tiles = beside_tiles(part, WIDE, 2, tiles)
    received, before, after = lax.optimization_barrier((received, before, after))
    near = (before[fields + 1 :], after[fields + 1 :])
    row_effect = row_effect + huber_scale[:, None] * jnp.sum(received, axis=0) / row_count[None, :]
    part = jnp.sum(terms(row_effect, col_effect), axis=1)
    part = jnp.concatenate([part, row_effect.reshape(-1, col_dev)], axis=0)
    received, tiles = beside_tiles(part, SIXTEEN, 3, tiles, near)
    total = jnp.sum(received[:, :fields], axis=0)
    col_effect = col_effect + huber_scale[:, None] * total / col_count[None, :]

    def rows_of(place, first):
        rows = lax.dynamic_index_in_dim(received[:, fields:], place % sixteen_size, 0, False)
        return rows.reshape(fields, row_dev)[:, first : first + REACH * STRIP]

    row_before = rows_of(my_place + sixteen_size - 1, row_dev - REACH * STRIP)
    row_after = rows_of(my_place + 1, 0)

    my_targets = lax.dynamic_slice_in_dim(group_map, my_place * BLOCKS_DEV, BLOCKS_DEV)
    r0, r0_before, r0_after, slots = residual_of(
        my_targets, observations, weight, row_effect, before, row_before, after, row_after, col_effect
    )
    owned_r0 = to_owners(slots)
    m1, slots, dots = applied(
        scalars, my_targets, tiles, r0, beside=(r0_before, r0_after), extra=0
    )
    before, after, m1 = beside(m1, REACH)
    part = applied(scalars, my_targets, tiles, m1, (0, EARLY_TILES))
    slots = gate(slots, part, before, after, owned_r0)
    owned_m1 = to_owners(slots)
    m2, slots, last = applied(
        scalars, my_targets, tiles, m1, (EARLY_TILES, None), (before, after), part, EXTRA
    )
    slots = attach(slots, sum_direct(dots + last, WIDE))
    slots = gate(slots, owned_m1)
    owned_m2 = to_owners(slots)
    owned = owned_table(group_map, sixteen_size, BLOCKS_DEV)
    my_ids = lax.dynamic_index_in_dim(owned, my_place, 0, keepdims=False)
    solution_now, residual_now = combined(my_ids // BLOCKS_DEV, owned_r0, owned_m1, owned_m2)
    return (solution_now[None, None], residual_now[None, None])


def solution(mesh):
    finer = Mesh(mesh.devices.reshape(4, 2, 4, 4), ("wide_0", "wide_1", "sixteen_0", "sixteen_1"))
    in_specs = (
        P(None, SIXTEEN, WIDE),
        P(),
        P(SIXTEEN, WIDE),
        P(None, SIXTEEN, WIDE),
        P(WIDE, None),
        P(WIDE, None, None),
    )
    out_specs = (P(WIDE, SIXTEEN, None, None, None), P(WIDE, SIXTEEN, None, None, None))
    return jax.shard_map(
        on_device, mesh=finer, in_specs=in_specs, out_specs=out_specs, check_vma=False
    )
```

```python
import functools

import jax
import jax.numpy as jnp
from jax import lax
from jax.experimental import pallas as pl
from jax.experimental.pallas import tpu as pltpu
from jax.sharding import Mesh
from jax.sharding import PartitionSpec as P

BLOCK = 512
BLOCKS_DEV = 8
REACH = 4
NEIGHBOURS = 6
PAIRED = NEIGHBOURS // 2
SWEEPS = 2
STRIP = 4
COL_DEV = 128
WIDE = ("wide_0", "wide_1")
SIXTEEN = ("sixteen_0", "sixteen_1")

HUBER_EDGE = 1.345
SILL_TERM = 0.02
ROOT_THREE = 1.7320508075688772
LOG2_E = 1.4426950408889634
SPREAD = 2.0 * STRIP
CUTOFF = 6.0 * STRIP
BAND = 24
GROUP = 16

OWN_TILES = BLOCKS_DEV + PAIRED * BLOCKS_DEV - 6
HALO_TILES = 2 * (2 + 3 + 4)
CHUNKS = (5, 9, 12, 18)
TILE_SLOTS = 4
OP_SLOTS = 5
EXTRA = 8
EARLY_TILES = 18


def sent_to_all(shard, axis):
    peers = lax.axis_size(axis)
    return lax.all_to_all(
        jnp.broadcast_to(shard[None], (peers, *shard.shape)), axis, 0, 0, tiled=True
    )


def over_copies(shard, axis):
    return jnp.sum(sent_to_all(shard, axis), axis=0)


def sum_direct(part, axis):
    peers = lax.axis_size(axis)
    moved = [
        lax.ppermute(part, axis, [(i, (i + k) % peers) for i in range(peers)])
        for k in range(1, peers)
    ]
    return functools.reduce(jnp.add, moved, part)


def beside(shard, width, dim=0):
    peers, length = lax.axis_size(SIXTEEN), shard.shape[dim]
    up = [(i, (i + 1) % peers) for i in range(peers)]
    down = [(j, i) for i, j in up]
    last = lax.slice_in_dim(shard, length - width, length, axis=dim)
    initial = lax.slice_in_dim(shard, 0, width, axis=dim)
    shard, last, initial = lax.optimization_barrier((shard, last, initial))
    return lax.ppermute(last, SIXTEEN, up), lax.ppermute(initial, SIXTEEN, down), shard


def owned_table(group_map, owners, per_owner):
    total_strips = group_map.shape[0]
    member = (group_map[None, :] == jnp.arange(owners, dtype=jnp.int32)[:, None]).astype(jnp.int32)
    ranked = jnp.cumsum(member, axis=1, dtype=jnp.int32) - 1
    slot_hit = (ranked[:, :, None] == jnp.arange(per_owner, dtype=jnp.int32)[None, None, :]).astype(
        jnp.int32
    ) * member[:, :, None]
    numbers = jnp.arange(total_strips, dtype=jnp.int32)
    return jnp.sum(slot_hit * numbers[None, :, None], axis=1, dtype=jnp.int32)


def offsets_of(list_ref):
    held = [
        functools.reduce(jnp.logical_or, [list_ref[n] == d for n in range(NEIGHBOURS)])
        for d in range(1, REACH)
    ]
    missing = jnp.where(held[0], jnp.where(held[1], jnp.where(held[2], 4, 3), 2), 1)
    return [k + jnp.where(missing <= k, 1, 0) for k in range(1, PAIRED + 1)]


def own_count(offsets):
    return (PAIRED + 1) * BLOCKS_DEV - (offsets[0] + offsets[1] + offsets[2])


def halo_count(offsets):
    return 2 * (offsets[0] + offsets[1] + offsets[2])


def own_pair(t, offsets):
    d1, d2, d3 = offsets
    p = t - BLOCKS_DEV
    n1, n2 = BLOCKS_DEV - d1, 2 * BLOCKS_DEV - d1 - d2
    one = jnp.where(p < n1, p, jnp.where(p < n2, p - n1, p - n2))
    return one, one + jnp.where(p < n1, d1, jnp.where(p < n2, d2, d3))


def halo_pair(q, offsets):
    d1, d2, d3 = offsets
    reach = d1 + d2 + d3
    right = q >= reach
    q = jnp.where(right, q - reach, q)
    step = jnp.where(q < d1, d1, jnp.where(q < d1 + d2, d2, d3))
    pos = jnp.where(q < d1, q, jnp.where(q < d1 + d2, q - d1, q - d1 - d2))
    one = jnp.where(right, BLOCKS_DEV - 1 - pos, pos)
    return one, jnp.where(right, one + step, one - step)


LISTED = OWN_TILES + HALO_TILES


def tiles_kernel(first, count, beside, held, scalar_ref, jitter_ref, *refs):
    beside_refs, refs = refs[:beside], refs[beside + held :]
    tiles_ref, buf, sem = refs
    a, b = ROOT_THREE * CUTOFF / SPREAD, 4.0
    offsets = offsets_of(scalar_ref)
    place, group = scalar_ref[NEIGHBOURS], scalar_ref[NEIGHBOURS + 1]
    total_rows = scalar_ref[NEIGHBOURS + 2]
    row_dev = STRIP * BLOCKS_DEV
    lane = lax.broadcasted_iota(jnp.int32, (GROUP, COL_DEV), 1)
    within = lax.broadcasted_iota(jnp.int32, (STRIP, COL_DEV), 0)
    across = lax.broadcasted_iota(jnp.int32, (STRIP, COL_DEV), 1)
    col_place = (group * COL_DEV + across).astype(jnp.float32)

    def out_copy(t):
        slot = lax.rem(t - first, TILE_SLOTS)
        return pltpu.make_async_copy(buf.at[slot], tiles_ref.at[t], sem.at[slot])

    def live(t):
        mine = (t < OWN_TILES) & (t < own_count(offsets))
        return mine | ((t >= OWN_TILES) & (t < OWN_TILES + halo_count(offsets)))

    def places(block, ref, at):
        row = lax.rem(place * row_dev + STRIP * block + total_rows, total_rows)
        rows = (row + within).astype(jnp.float32) + ref[0, pl.ds(at, STRIP), :]
        cols = col_place + ref[1, pl.ds(at, STRIP), :]
        return jnp.concatenate([rows, cols], axis=0) * (1.0 / CUTOFF)

    def pair_of(t):
        q = t - OWN_TILES
        one, other = own_pair(t, offsets)
        one_q, other_q = halo_pair(q, offsets)
        same = t < BLOCKS_DEV
        mine = t < OWN_TILES
        one = jnp.where(same, t, jnp.where(mine, one, one_q))
        return one, jnp.where(same, t, jnp.where(mine, other, other_q))

    def evaluate(slot, to, frm, sill):
        for rb in range(STRIP):
            row_b = jnp.broadcast_to(frm[rb : rb + 1], (COL_DEV, COL_DEV)).T
            col_b = jnp.broadcast_to(frm[STRIP + rb : STRIP + rb + 1], (COL_DEV, COL_DEV)).T
            for u in range(COL_DEV // 2 // GROUP):
                lo_s = slice(GROUP * u, GROUP * (u + 1))
                hi_s = slice(64 + GROUP * u, 64 + GROUP * (u + 1))
                near = (lane >= GROUP * u - BAND) & (lane < GROUP * (u + 1) + BAND)
                one_m = jnp.where(near, 1.0, 0.0).astype(jnp.bfloat16)
                other_m = jnp.where(near, 0.0, 1.0).astype(jnp.bfloat16)
                row_s = jnp.where(near, row_b[lo_s], row_b[hi_s])
                col_s = jnp.where(near, col_b[lo_s], col_b[hi_s])
                for ra in range(STRIP):
                    dr = row_s - to[ra : ra + 1]
                    dc = col_s - to[STRIP + ra : STRIP + ra + 1]
                    square = dr * dr + dc * dc
                    far = square * lax.rsqrt(jnp.maximum(square, 1e-30))
                    fading = jnp.maximum(1.0 - far, 0.0)
                    fading = fading * fading
                    fading = fading * fading
                    shape = (sill + (sill * (a + b)) * far) + (sill * (a * b)) * square
                    value = shape * fading * jnp.exp2((-a * LOG2_E) * far)
                    hi = value.astype(jnp.bfloat16)
                    lo = (value - hi.astype(jnp.float32)).astype(jnp.bfloat16)
                    lanes = slice(COL_DEV * ra, COL_DEV * (ra + 1))
                    top = rb * COL_DEV + GROUP * u
                    for part, at in ((hi, top), (lo, BLOCK + top)):
                        buf[slot, at : at + GROUP, lanes] = part * one_m
                        buf[slot, at + 64 : at + 64 + GROUP, lanes] = part * other_m

    def one_tile(t, carry):
        slot = lax.rem(t - first, TILE_SLOTS)
        past = jnp.maximum(t - TILE_SLOTS, first)

        @pl.when((t >= first + TILE_SLOTS) & live(past))
        def _():
            out_copy(past).wait()

        @pl.when(live(t))
        def _():
            one, other = pair_of(t)
            sill = jnp.where(one == other, (NEIGHBOURS + 1.0) * SILL_TERM, SILL_TERM)
            inside = jnp.clip(other, 0, BLOCKS_DEV - 1)
            to = places(one, jitter_ref, STRIP * one)
            frm = places(other, jitter_ref, STRIP * inside)
            if beside_refs:
                left = places(other, beside_refs[0], STRIP * jnp.clip(other + REACH, 0, REACH - 1))
                right = places(
                    other, beside_refs[1], STRIP * jnp.clip(other - BLOCKS_DEV, 0, REACH - 1)
                )
                frm = jnp.where(other < 0, left, jnp.where(other < BLOCKS_DEV, frm, right))
            evaluate(slot, to, frm, sill)
            out_copy(t).start()

        return carry

    lax.fori_loop(first, first + count, one_tile, 0)
    for t in range(max(first, first + count - TILE_SLOTS), first + count):

        @pl.when(live(t))
        def _(t=t):
            out_copy(t).wait()


def covariance_tiles(first, count, scalars, jitter, beside_jitter, held):
    extra = [] if held is None else [held]
    ins = [scalars, jitter, *beside_jitter, *extra]
    return pl.pallas_call(
        functools.partial(tiles_kernel, first, count, len(beside_jitter), len(extra)),
        in_specs=[SMEM_SPEC] + [VMEM_SPEC] * (1 + len(beside_jitter)) + [HBM_SPEC] * len(extra),
        out_specs=HBM_SPEC,
        scratch_shapes=[
            pltpu.VMEM((TILE_SLOTS, 2 * BLOCK, BLOCK), jnp.bfloat16),
            pltpu.SemaphoreType.DMA((TILE_SLOTS,)),
        ],
        out_shape=jax.ShapeDtypeStruct((LISTED, 2 * BLOCK, BLOCK), jnp.bfloat16),
        input_output_aliases={len(ins) - 1: 0} if extra else {},
        compiler_params=pltpu.CompilerParams(vmem_limit_bytes=12 << 20),
        cost_estimate=pl.CostEstimate(
            flops=count * 12 * BLOCK * BLOCK,
            bytes_accessed=count * 4 * BLOCK * BLOCK,
            transcendentals=count * BLOCK * BLOCK,
        ),
        name="tiles",
    )(*ins)


def halves(v):
    hi = v.astype(jnp.bfloat16)
    lo = (v - hi.astype(jnp.float32)).astype(jnp.bfloat16)
    return hi, lo


NN = (((1,), (0,)), ((), ()))
NT = (((1,), (1,)), ((), ()))


def product(both, tile_ref, dims):
    fields = both.shape[0] // 2
    main = lax.dot_general(
        both, tile_ref[:BLOCK], dims, preferred_element_type=jnp.float32
    )
    rest = lax.dot_general(
        both[:fields], tile_ref[BLOCK:], dims, preferred_element_type=jnp.float32
    )
    return main[:fields] + (main[fields:] + rest)


def op_kernel(first, last, halo, held, send, scalar_ref, target_ref, *refs):
    refs = list(refs)
    v_ref = refs.pop(0)
    beside_refs = [refs.pop(0), refs.pop(0)] if halo else []
    held_ref = refs.pop(0) if held else None
    tiles_ref, out_ref = refs.pop(0), refs.pop(0)
    slots_ref, dots_ref = (refs.pop(0), refs.pop(0)) if send else (None, None)
    values, both_ref, total, buf, sem, in_sem, out_sem = refs
    fields = total.shape[1]
    offsets = offsets_of(scalar_ref)
    mine = (own_count(offsets) if last is None else last) - first
    count = mine + (halo_count(offsets) if halo else 0)

    def copy(t):
        slot = lax.rem(t, OP_SLOTS)
        at = jnp.where(t < mine, t + first, t - mine + OWN_TILES)
        return pltpu.make_async_copy(tiles_ref.at[at], buf.at[slot], sem.at[slot])

    loads = [(v_ref, 0, BLOCKS_DEV)]
    for side, ref in enumerate(beside_refs):
        loads.append((ref, BLOCKS_DEV + REACH * side, REACH))
    arriving = [
        pltpu.make_async_copy(ref, values.at[pl.ds(at, size)], in_sem.at[i])
        for i, (ref, at, size) in enumerate(loads)
    ]
    if held_ref is not None:
        arriving.append(pltpu.make_async_copy(held_ref, total, in_sem.at[3]))
    for load in arriving:
        load.start()
    for t in range(OP_SLOTS - 1):
        copy(t).start()
    for load in arriving:
        load.wait()
    for _, at, size in loads:
        for g in range(at, at + size):
            hi, lo = halves(values[g])
            both_ref[g, :fields] = hi
            both_ref[g, fields:] = lo

    def arrive(t):
        @pl.when(t + OP_SLOTS - 1 < count)
        def _():
            copy(t + OP_SLOTS - 1).start()

        copy(t).wait()
        return buf.at[lax.rem(t, OP_SLOTS)]

    def with_itself(t, carry):
        tile = arrive(t)
        total[t] = product(both_ref[t], tile, NN)
        return carry

    def with_another(t, carry):
        tile = arrive(t)
        one, other = own_pair(t + first, offsets)
        total[one] += product(both_ref[other], tile, NN)
        total[other] += product(both_ref[one], tile, NT)
        return carry

    def with_beside(t, carry):
        tile = arrive(t)
        one, other = halo_pair(t - mine, offsets)
        side = BLOCKS_DEV + jnp.where(other < 0, other + REACH, other - BLOCKS_DEV + REACH)
        total[one] += product(both_ref[side], tile, NN)
        return carry

    if first == 0:
        lax.fori_loop(0, BLOCKS_DEV, with_itself, 0)
    lax.fori_loop(max(BLOCKS_DEV - first, 0), mine, with_another, 0)
    if halo:
        lax.fori_loop(mine, count, with_beside, 0)
    leaving = [pltpu.make_async_copy(total, out_ref, out_sem.at[BLOCKS_DEV])]
    if send:
        leaving += out_copies(total, slots_ref, target_ref, out_sem)
    for out in leaving:
        out.start()
    if send:
        lane = lax.broadcasted_iota(jnp.int32, (fields, COL_DEV), 1)
        dots = jnp.zeros((fields, COL_DEV), jnp.float32)
        for at, one, other in products_of(values, total, held):
            summed = functools.reduce(jnp.add, [one[g] * other[g] for g in range(BLOCKS_DEV)])
            dots = jnp.where(lane == at, jnp.sum(summed, axis=1, keepdims=True), dots)
        dots = jnp.concatenate([dots, jnp.zeros((COL_DEV - fields, COL_DEV), jnp.float32)], axis=0)
        dots_ref[...] = dots.T[:EXTRA]
    for out in leaving:
        out.wait()


def products_of(v, image, second):
    if second:
        return [(3, v, image)]
    return [(0, v, v), (1, v, image), (2, image, image)]


def out_copies(values_ref, slots_ref, target_ref, sem):
    return [
        pltpu.make_async_copy(values_ref.at[g], slots_ref.at[target_ref[g]], sem.at[g])
        for g in range(BLOCKS_DEV)
    ]


SMEM_SPEC = pl.BlockSpec(memory_space=pltpu.SMEM)
VMEM_SPEC = pl.BlockSpec(memory_space=pltpu.VMEM)
HBM_SPEC = pl.BlockSpec(memory_space=pltpu.HBM)


def in_hbm(x):
    return pltpu.with_memory_space_constraint(x, pltpu.HBM)


def slot_shape(v):
    return pltpu.HBM((lax.axis_size(SIXTEEN), *v.shape[1:]), jnp.float32)


def applied(scalars, targets, tiles, v, tiles_of=(0, None), beside=(), held=None, send=False):
    blocks, fields, _ = v.shape
    out = pltpu.HBM(v.shape, jnp.float32)
    ins = [in_hbm(x) for x in (v, *beside, held) if x is not None] + [tiles]
    number = (tiles_of[1] or OWN_TILES) - tiles_of[0] + HALO_TILES * bool(beside)
    out = pl.pallas_call(
        functools.partial(op_kernel, *tiles_of, bool(beside), held is not None, send),
        in_specs=[SMEM_SPEC] * 2 + [HBM_SPEC] * len(ins),
        out_specs=[HBM_SPEC] + [HBM_SPEC, VMEM_SPEC] * send,
        scratch_shapes=[
            pltpu.VMEM((blocks + 2 * REACH, fields, BLOCK), jnp.float32),
            pltpu.VMEM((blocks + 2 * REACH, 2 * fields, BLOCK), jnp.bfloat16),
            pltpu.VMEM(v.shape, jnp.float32),
            pltpu.VMEM((OP_SLOTS, 2 * BLOCK, BLOCK), jnp.bfloat16),
            pltpu.SemaphoreType.DMA((OP_SLOTS,)),
            pltpu.SemaphoreType.DMA((4,)),
            pltpu.SemaphoreType.DMA((BLOCKS_DEV + 1,)),
        ],
        out_shape=[out]
        + [slot_shape(v), jax.ShapeDtypeStruct((EXTRA, COL_DEV), jnp.float32)] * send,
        compiler_params=pltpu.CompilerParams(vmem_limit_bytes=24 << 20),
        cost_estimate=pl.CostEstimate(
            flops=3 * number * 3 * fields * BLOCK * BLOCK,
            bytes_accessed=number * 4 * BLOCK * BLOCK,
            transcendentals=0,
        ),
        name="applied",
    )(scalars, targets, *ins)
    return out if send else out[0]


def gate_kernel(*refs):
    pass


def gate(slots, *others):
    return pl.pallas_call(
        gate_kernel,
        in_specs=[HBM_SPEC] + [VMEM_SPEC] * len(others),
        out_specs=HBM_SPEC,
        out_shape=pltpu.HBM(slots.shape, jnp.float32),
        input_output_aliases={0: 0},
        compiler_params=pltpu.CompilerParams(vmem_limit_bytes=1 << 20),
        name="gate",
    )(slots, *(other[0, :8, :COL_DEV] for other in others))


def residual_kernel(
    target_ref, obs_ref, weight_ref, row_ref, before_ref, before_row_ref, after_ref,
    after_row_ref, col_ref, out_ref, before_out_ref, after_out_ref, slots_ref, buf, sem,
):
    fields = obs_ref.shape[0]
    col = col_ref[...]

    def block(at, obs, weight, row, g):
        for ra in range(STRIP):
            r = STRIP * g + ra
            left = obs[:fields, r, :] - row[:, r : r + 1] - col
            weighted = weight[r : r + 1, :] * left
            buf[at, :, COL_DEV * ra : COL_DEV * (ra + 1)] = weighted

    copies = []
    for g in range(BLOCKS_DEV):
        block(g, obs_ref, weight_ref, row_ref, g)
        copies.append(
            pltpu.make_async_copy(buf.at[g], slots_ref.at[target_ref[g]], sem.at[g])
        )
        copies[-1].start()
    copies.append(
        pltpu.make_async_copy(buf.at[pl.ds(0, BLOCKS_DEV)], out_ref, sem.at[BLOCKS_DEV])
    )
    copies[-1].start()
    sides = ((before_ref, before_row_ref, before_out_ref), (after_ref, after_row_ref, after_out_ref))
    for side, (obs, row, out) in enumerate(sides):
        first = BLOCKS_DEV + REACH * side
        for g in range(REACH):
            block(first + g, obs, obs.at[fields], row, g)
        copies.append(
            pltpu.make_async_copy(
                buf.at[pl.ds(first, REACH)], out, sem.at[BLOCKS_DEV + 1 + side]
            )
        )
        copies[-1].start()
    for copy in copies:
        copy.wait()


def residual_of(targets, observations, weight, row_effect, before, before_row, after, after_row, col):
    fields = observations.shape[0]
    own = pltpu.HBM((BLOCKS_DEV, fields, BLOCK), jnp.float32)
    side = pltpu.HBM((REACH, fields, BLOCK), jnp.float32)
    return pl.pallas_call(
        residual_kernel,
        in_specs=[SMEM_SPEC] + [VMEM_SPEC] * 8,
        out_specs=[HBM_SPEC] * 4,
        scratch_shapes=[
            pltpu.VMEM((BLOCKS_DEV + 2 * REACH, fields, BLOCK), jnp.float32),
            pltpu.SemaphoreType.DMA((BLOCKS_DEV + 3,)),
        ],
        out_shape=[own, side, side, slot_shape(own)],
        compiler_params=pltpu.CompilerParams(vmem_limit_bytes=12 << 20),
        name="residual",
    )(targets, observations, weight, row_effect, before, before_row, after, after_row, col)


def scales_of(dots_ref, scale_ref, part):
    @pl.when(pl.program_id(0) == 0)
    def _():
        scale_ref[...] = step_scales(*(dots_ref[k : k + 1] for k in range(4))).T

    return scale_ref[pl.ds(pl.multiple_of(pl.program_id(0) * part, part), part), :]


def first_kernel(src_ref, dots_ref, *refs):
    ins, (x_ref, r_ref, scale_ref) = refs[:-3], refs[-3:]
    scale = scales_of(dots_ref, scale_ref, x_ref.shape[0])
    for j in range(BLOCKS_DEV):
        r0, m1 = (ref[0] for ref in ins[2 * j : 2 * j + 2])
        x_ref[:, j, :] = scale[:, 0:1] * r0 + scale[:, 1:2] * m1
        r_ref[:, j, :] = scale[:, 2:3] * r0 + scale[:, 3:4] * m1


def second_kernel(src_ref, dots_ref, part_ref, *refs):
    ins, (r_ref, scale_ref) = refs[:-2], refs[-2:]
    scale = scales_of(dots_ref, scale_ref, r_ref.shape[0])
    for j in range(BLOCKS_DEV):
        r_ref[:, j, :] = part_ref[:, j, :] + scale[:, 4:5] * ins[j][0]


def combined(kernel, name, outs, sources, dots, held, *owned):
    _, fields, _ = owned[0].shape
    part = 16
    by_field = pl.BlockSpec((part, BLOCKS_DEV, BLOCK), lambda i, s: (i, 0, 0))
    ins, specs = list(held), [by_field] * len(held)
    for j in range(BLOCKS_DEV):
        for v in owned:
            ins.append(v)
            specs.append(
                pl.BlockSpec(
                    (1, part, BLOCK), functools.partial(lambda j, i, s: (s[j], i, 0), j)
                )
            )
    shape = jax.ShapeDtypeStruct((fields, BLOCKS_DEV, BLOCK), jnp.float32)
    return pl.pallas_call(
        kernel,
        grid_spec=pltpu.PrefetchScalarGridSpec(
            num_scalar_prefetch=1,
            grid=(fields // part,),
            in_specs=[pl.BlockSpec(dots.shape, lambda i, s: (0, 0))] + specs,
            out_specs=[by_field] * outs,
            scratch_shapes=[pltpu.VMEM((COL_DEV, 8), jnp.float32)],
        ),
        out_shape=[shape] * outs,
        compiler_params=pltpu.CompilerParams(vmem_limit_bytes=20 << 20),
        name=name,
    )(sources, dots, *ins)


def to_owners(slots):
    return lax.all_to_all(slots, SIXTEEN, 0, 0, tiled=True)


def step_scales(h00, h01, h11, h12):
    mu = h01 / h00
    var = (h11 - mu * h01) / h00
    a0 = 1.0 / (1.0 + mu)
    beta = var * a0 * a0
    skew = (h12 - mu * h11 - mu * (h11 - mu * h01)) / h00
    a1 = var / (var + skew - var * var * a0)
    x_r0 = a0 + a1 * beta + a1 * a0 * mu
    x_m1 = -a1 * a0
    r_r0 = a0 * mu * (1.0 - a1) - a1 * beta
    r_m1 = -a0 * (1.0 - a1) - a1 * a0 * mu - a1 * beta
    r_m2 = a1 * a0
    zero = jnp.zeros_like(mu)
    return jnp.concatenate([x_r0, x_m1, r_r0, r_m1, r_m2, zero, zero, zero], axis=0)


def on_device(observations, huber_scale, observed, jitter, owner_map, neighbours):
    fields, row_dev, col_dev = observations.shape
    sixteen_size = lax.axis_size(SIXTEEN)
    my_place = lax.axis_index(SIXTEEN)
    group_place = lax.axis_index(WIDE)
    total_strips = BLOCKS_DEV * sixteen_size
    weight = observed.astype(jnp.float32)
    spread_scale = huber_scale[:, None, None]

    def with_count(part, count):
        rows = jnp.zeros((8, count.shape[0]), jnp.float32).at[0].set(count)
        return jnp.concatenate([part, rows], axis=0)

    def terms(row_effect, col_effect):
        return weight[None] * jnp.clip(
            (observations - row_effect[:, :, None] - col_effect[:, None, :]) / spread_scale,
            -HUBER_EDGE,
            HUBER_EDGE,
        )

    def sum_wide(part):
        for axis in WIDE[::-1]:
            part = sum_direct(part, axis)
        return part

    row_effect = jnp.zeros((fields, row_dev), jnp.float32)
    col_effect = jnp.zeros((fields, col_dev), jnp.float32)
    part = with_count(jnp.sum(terms(row_effect, col_effect), axis=2), jnp.sum(weight, axis=1))
    part, jitter, owner_map, neighbours = lax.optimization_barrier(
        (part, jitter, owner_map, neighbours)
    )
    group_map = owner_map[0]
    scalars = jnp.concatenate(
        [neighbours[0, 0], jnp.stack([my_place, group_place, total_strips * STRIP])]
    ).astype(jnp.int32)

    def beside_tiles(part, axis, chunk, tiles, near=()):
        first = sum(CHUNKS[:chunk])
        if chunk:
            part, tiles = lax.optimization_barrier((part, tiles))
        received = sent_to_all(part, axis)
        tiles = covariance_tiles(first, CHUNKS[chunk], scalars, jitter, near, tiles)
        return lax.optimization_barrier((received, tiles))

    edges = jnp.concatenate([observations, weight[None], jitter], axis=0)
    before, after, _ = beside(edges, REACH * STRIP, 1)
    received, tiles = beside_tiles(part, WIDE, 0, None)
    total = jnp.sum(received, axis=0)
    row_count = jnp.maximum(total[fields], 1.0)
    row_effect = huber_scale[:, None] * total[:fields] / row_count[None, :]
    part = with_count(jnp.sum(terms(row_effect, col_effect), axis=1), jnp.sum(weight, axis=0))
    received, tiles = beside_tiles(part, SIXTEEN, 1, tiles)
    total = jnp.sum(received, axis=0)
    col_count = jnp.maximum(total[fields], 1.0)
    col_effect = huber_scale[:, None] * total[:fields] / col_count[None, :]
    part = jnp.sum(terms(row_effect, col_effect), axis=2)
    received, tiles = beside_tiles(part, WIDE, 2, tiles)
    received, before, after = lax.optimization_barrier((received, before, after))
    near = (before[fields + 1 :], after[fields + 1 :])
    row_effect = row_effect + huber_scale[:, None] * jnp.sum(received, axis=0) / row_count[None, :]
    part = jnp.sum(terms(row_effect, col_effect), axis=1)
    part = jnp.concatenate([part, row_effect.reshape(-1, col_dev)], axis=0)
    received, tiles = beside_tiles(part, SIXTEEN, 3, tiles, near)
    total = jnp.sum(received[:, :fields], axis=0)
    col_effect = col_effect + huber_scale[:, None] * total / col_count[None, :]

    def rows_of(place, first):
        rows = lax.dynamic_index_in_dim(received[:, fields:], place % sixteen_size, 0, False)
        return rows.reshape(fields, row_dev)[:, first : first + REACH * STRIP]

    row_before = rows_of(my_place + sixteen_size - 1, row_dev - REACH * STRIP)
    row_after = rows_of(my_place + 1, 0)

    my_targets = lax.dynamic_slice_in_dim(group_map, my_place * BLOCKS_DEV, BLOCKS_DEV)
    r0, r0_before, r0_after, slots = residual_of(
        my_targets, observations, weight, row_effect, before, row_before, after, row_after, col_effect
    )
    owned_r0 = to_owners(slots)
    m1, slots, dots = applied(
        scalars, my_targets, tiles, r0, beside=(r0_before, r0_after), send=True
    )
    before, after, m1 = beside(m1, REACH)
    part = applied(scalars, my_targets, tiles, m1, (0, EARLY_TILES))
    slots = gate(slots, part, before, after, owned_r0)
    owned_m1 = to_owners(slots)
    m2, slots, last = applied(
        scalars, my_targets, tiles, m1, (EARLY_TILES, None), (before, after), part, True
    )
    dots = sum_direct(sum_direct(dots + last, WIDE), SIXTEEN[1])
    slots = gate(slots, owned_m1, dots[None])
    owned_m2 = to_owners(slots)
    dots = sum_direct(dots, SIXTEEN[0])
    owned = owned_table(group_map, sixteen_size, BLOCKS_DEV)
    my_ids = lax.dynamic_index_in_dim(owned, my_place, 0, keepdims=False)
    sources = my_ids // BLOCKS_DEV
    solution_now, part = combined(
        first_kernel, "first", 2, sources, dots, (), in_hbm(owned_r0), in_hbm(owned_m1)
    )
    (residual_now,) = combined(second_kernel, "second", 1, sources, dots, (part,), owned_m2)
    return (solution_now[None, None], residual_now[None, None])


def solution(mesh):
    finer = Mesh(mesh.devices.reshape(4, 2, 4, 4), ("wide_0", "wide_1", "sixteen_0", "sixteen_1"))
    in_specs = (
        P(None, SIXTEEN, WIDE),
        P(),
        P(SIXTEEN, WIDE),
        P(None, SIXTEEN, WIDE),
        P(WIDE, None),
        P(WIDE, None, None),
    )
    out_specs = (P(WIDE, SIXTEEN, None, None, None), P(WIDE, SIXTEEN, None, None, None))
    return jax.shard_map(
        on_device, mesh=finer, in_specs=in_specs, out_specs=out_specs, check_vma=False
    )
```

```python
import functools

import jax
import jax.numpy as jnp
from jax import lax
from jax.experimental import pallas as pl
from jax.experimental.pallas import tpu as pltpu
from jax.sharding import Mesh
from jax.sharding import PartitionSpec as P

BLOCK = 512
BLOCKS_DEV = 8
REACH = 4
NEIGHBOURS = 6
PAIRED = NEIGHBOURS // 2
SWEEPS = 2
STRIP = 4
COL_DEV = 128
WIDE = ("wide_0", "wide_1")
SIXTEEN = ("sixteen_0", "sixteen_1")

HUBER_EDGE = 1.345
SILL_TERM = 0.02
ROOT_THREE = 1.7320508075688772
LOG2_E = 1.4426950408889634
SPREAD = 2.0 * STRIP
CUTOFF = 6.0 * STRIP
BAND = 24
GROUP = 16

OWN_TILES = BLOCKS_DEV + PAIRED * BLOCKS_DEV - 6
HALO_TILES = 2 * (2 + 3 + 4)
CHUNKS = (5, 9, 9, 21)
TILE_SLOTS = 4
OP_SLOTS = 12
OP_FIRST = 4
EXTRA = 8
EARLY_TILES = 18


def sent_to_all(shard, axis):
    peers = lax.axis_size(axis)
    return lax.all_to_all(
        jnp.broadcast_to(shard[None], (peers, *shard.shape)), axis, 0, 0, tiled=True
    )


def over_copies(shard, axis):
    return jnp.sum(sent_to_all(shard, axis), axis=0)


def sum_direct(part, axis):
    peers = lax.axis_size(axis)
    moved = [
        lax.ppermute(part, axis, [(i, (i + k) % peers) for i in range(peers)])
        for k in range(1, peers)
    ]
    return functools.reduce(jnp.add, moved, part)


def swapped(initial, last):
    peers = lax.axis_size(SIXTEEN)
    up = [(i, (i + 1) % peers) for i in range(peers)]
    down = [(j, i) for i, j in up]
    return lax.ppermute(last, SIXTEEN, up), lax.ppermute(initial, SIXTEEN, down)


def beside(shard, width, dim=0):
    length = shard.shape[dim]
    last = lax.slice_in_dim(shard, length - width, length, axis=dim)
    initial = lax.slice_in_dim(shard, 0, width, axis=dim)
    return swapped(*lax.optimization_barrier((initial, last)))


def owned_table(group_map, owners, per_owner):
    total_strips = group_map.shape[0]
    member = (group_map[None, :] == jnp.arange(owners, dtype=jnp.int32)[:, None]).astype(jnp.int32)
    ranked = jnp.cumsum(member, axis=1, dtype=jnp.int32) - 1
    slot_hit = (ranked[:, :, None] == jnp.arange(per_owner, dtype=jnp.int32)[None, None, :]).astype(
        jnp.int32
    ) * member[:, :, None]
    numbers = jnp.arange(total_strips, dtype=jnp.int32)
    return jnp.sum(slot_hit * numbers[None, :, None], axis=1, dtype=jnp.int32)


def offsets_of(list_ref):
    held = [
        functools.reduce(jnp.logical_or, [list_ref[n] == d for n in range(NEIGHBOURS)])
        for d in range(1, REACH)
    ]
    missing = jnp.where(held[0], jnp.where(held[1], jnp.where(held[2], 4, 3), 2), 1)
    return [k + jnp.where(missing <= k, 1, 0) for k in range(1, PAIRED + 1)]


def own_count(offsets):
    return (PAIRED + 1) * BLOCKS_DEV - (offsets[0] + offsets[1] + offsets[2])


def halo_count(offsets):
    return 2 * (offsets[0] + offsets[1] + offsets[2])


def own_pair(t, offsets):
    d1, d2, d3 = offsets
    p = t - BLOCKS_DEV
    n1, n2 = BLOCKS_DEV - d1, 2 * BLOCKS_DEV - d1 - d2
    one = jnp.where(p < n1, p, jnp.where(p < n2, p - n1, p - n2))
    return one, one + jnp.where(p < n1, d1, jnp.where(p < n2, d2, d3))


def halo_pair(q, offsets):
    d1, d2, d3 = offsets
    reach = d1 + d2 + d3
    right = q >= reach
    q = jnp.where(right, q - reach, q)
    step = jnp.where(q < d1, d1, jnp.where(q < d1 + d2, d2, d3))
    pos = jnp.where(q < d1, q, jnp.where(q < d1 + d2, q - d1, q - d1 - d2))
    one = jnp.where(right, BLOCKS_DEV - 1 - pos, pos)
    return one, jnp.where(right, one + step, one - step)


LISTED = OWN_TILES + HALO_TILES


def tiles_kernel(first, count, beside, held, scalar_ref, jitter_ref, *refs):
    beside_refs, refs = refs[:beside], refs[beside + held :]
    tiles_ref, buf, sem = refs
    a, b = ROOT_THREE * CUTOFF / SPREAD, 4.0
    offsets = offsets_of(scalar_ref)
    place, group = scalar_ref[NEIGHBOURS], scalar_ref[NEIGHBOURS + 1]
    total_rows = scalar_ref[NEIGHBOURS + 2]
    row_dev = STRIP * BLOCKS_DEV
    lane = lax.broadcasted_iota(jnp.int32, (GROUP, COL_DEV), 1)
    within = lax.broadcasted_iota(jnp.int32, (STRIP, COL_DEV), 0)
    across = lax.broadcasted_iota(jnp.int32, (STRIP, COL_DEV), 1)
    col_place = (group * COL_DEV + across).astype(jnp.float32)

    def out_copy(t):
        slot = lax.rem(t - first, TILE_SLOTS)
        return pltpu.make_async_copy(buf.at[slot], tiles_ref.at[t], sem.at[slot])

    def live(t):
        mine = (t < OWN_TILES) & (t < own_count(offsets))
        return mine | ((t >= OWN_TILES) & (t < OWN_TILES + halo_count(offsets)))

    def places(block, ref, at):
        row = lax.rem(place * row_dev + STRIP * block + total_rows, total_rows)
        rows = (row + within).astype(jnp.float32) + ref[0, pl.ds(at, STRIP), :]
        cols = col_place + ref[1, pl.ds(at, STRIP), :]
        return jnp.concatenate([rows, cols], axis=0) * (1.0 / CUTOFF)

    def pair_of(t):
        q = t - OWN_TILES
        one, other = own_pair(t, offsets)
        one_q, other_q = halo_pair(q, offsets)
        same = t < BLOCKS_DEV
        mine = t < OWN_TILES
        one = jnp.where(same, t, jnp.where(mine, one, one_q))
        return one, jnp.where(same, t, jnp.where(mine, other, other_q))

    def evaluate(slot, to, frm, sill):
        for rb in range(STRIP):
            row_b = jnp.broadcast_to(frm[rb : rb + 1], (COL_DEV, COL_DEV)).T
            col_b = jnp.broadcast_to(frm[STRIP + rb : STRIP + rb + 1], (COL_DEV, COL_DEV)).T
            for u in range(COL_DEV // 2 // GROUP):
                lo_s = slice(GROUP * u, GROUP * (u + 1))
                hi_s = slice(64 + GROUP * u, 64 + GROUP * (u + 1))
                near = (lane >= GROUP * u - BAND) & (lane < GROUP * (u + 1) + BAND)
                one_m = jnp.where(near, 1.0, 0.0).astype(jnp.bfloat16)
                other_m = jnp.where(near, 0.0, 1.0).astype(jnp.bfloat16)
                row_s = jnp.where(near, row_b[lo_s], row_b[hi_s])
                col_s = jnp.where(near, col_b[lo_s], col_b[hi_s])
                for ra in range(STRIP):
                    dr = row_s - to[ra : ra + 1]
                    dc = col_s - to[STRIP + ra : STRIP + ra + 1]
                    square = dr * dr + dc * dc
                    far = square * lax.rsqrt(jnp.maximum(square, 1e-30))
                    fading = jnp.maximum(1.0 - far, 0.0)
                    fading = fading * fading
                    fading = fading * fading
                    shape = (sill + (sill * (a + b)) * far) + (sill * (a * b)) * square
                    value = shape * fading * jnp.exp2((-a * LOG2_E) * far)
                    hi = value.astype(jnp.bfloat16)
                    lo = (value - hi.astype(jnp.float32)).astype(jnp.bfloat16)
                    lanes = slice(COL_DEV * ra, COL_DEV * (ra + 1))
                    top = rb * COL_DEV + GROUP * u
                    for part, at in ((hi, top), (lo, BLOCK + top)):
                        buf[slot, at : at + GROUP, lanes] = part * one_m
                        buf[slot, at + 64 : at + 64 + GROUP, lanes] = part * other_m

    def one_tile(t, carry):
        slot = lax.rem(t - first, TILE_SLOTS)
        past = jnp.maximum(t - TILE_SLOTS, first)

        @pl.when((t >= first + TILE_SLOTS) & live(past))
        def _():
            out_copy(past).wait()

        @pl.when(live(t))
        def _():
            one, other = pair_of(t)
            sill = jnp.where(one == other, (NEIGHBOURS + 1.0) * SILL_TERM, SILL_TERM)
            inside = jnp.clip(other, 0, BLOCKS_DEV - 1)
            to = places(one, jitter_ref, STRIP * one)
            frm = places(other, jitter_ref, STRIP * inside)
            if beside_refs:
                left = places(other, beside_refs[0], STRIP * jnp.clip(other + REACH, 0, REACH - 1))
                right = places(
                    other, beside_refs[1], STRIP * jnp.clip(other - BLOCKS_DEV, 0, REACH - 1)
                )
                frm = jnp.where(other < 0, left, jnp.where(other < BLOCKS_DEV, frm, right))
            evaluate(slot, to, frm, sill)
            out_copy(t).start()

        return carry

    lax.fori_loop(first, first + count, one_tile, 0)
    for t in range(max(first, first + count - TILE_SLOTS), first + count):

        @pl.when(live(t))
        def _(t=t):
            out_copy(t).wait()


def covariance_tiles(first, count, scalars, jitter, beside_jitter, held):
    extra = [] if held is None else [held]
    ins = [scalars, jitter, *beside_jitter, *extra]
    return pl.pallas_call(
        functools.partial(tiles_kernel, first, count, len(beside_jitter), len(extra)),
        in_specs=[SMEM_SPEC] + [VMEM_SPEC] * (1 + len(beside_jitter)) + [HBM_SPEC] * len(extra),
        out_specs=HBM_SPEC,
        scratch_shapes=[
            pltpu.VMEM((TILE_SLOTS, 2 * BLOCK, BLOCK), jnp.bfloat16),
            pltpu.SemaphoreType.DMA((TILE_SLOTS,)),
        ],
        out_shape=jax.ShapeDtypeStruct((LISTED, 2 * BLOCK, BLOCK), jnp.bfloat16),
        input_output_aliases={len(ins) - 1: 0} if extra else {},
        compiler_params=pltpu.CompilerParams(vmem_limit_bytes=12 << 20),
        cost_estimate=pl.CostEstimate(
            flops=count * 12 * BLOCK * BLOCK,
            bytes_accessed=count * 4 * BLOCK * BLOCK,
            transcendentals=count * BLOCK * BLOCK,
        ),
        name="tiles",
    )(*ins)


def halves(v):
    hi = v.astype(jnp.bfloat16)
    lo = (v - hi.astype(jnp.float32)).astype(jnp.bfloat16)
    return hi, lo


NN = (((1,), (0,)), ((), ()))
NT = (((1,), (1,)), ((), ()))


def product(both, tile_ref, dims):
    fields = both.shape[0] // 2
    main = lax.dot_general(
        both, tile_ref[:BLOCK], dims, preferred_element_type=jnp.float32
    )
    rest = lax.dot_general(
        both[:fields], tile_ref[BLOCK:], dims, preferred_element_type=jnp.float32
    )
    return main[:fields] + (main[fields:] + rest)


def op_kernel(first, last, halo, held, send, scalar_ref, target_ref, *refs):
    refs = list(refs)
    v_ref = refs.pop(0)
    beside_refs = [refs.pop(0), refs.pop(0)] if halo else []
    held_ref = refs.pop(0) if held else None
    tiles_ref, out_ref = refs.pop(0), refs.pop(0)
    edge_refs = [refs.pop(0), refs.pop(0)] if send and not held else []
    slots_ref, dots_ref = (refs.pop(0), refs.pop(0)) if send else (None, None)
    values, both_ref, total, buf, sem, in_sem, out_sem = refs
    fields = total.shape[1]
    offsets = offsets_of(scalar_ref)
    mine = (own_count(offsets) if last is None else last) - first
    count = mine + (halo_count(offsets) if halo else 0)

    def copy(t):
        slot = lax.rem(t, OP_SLOTS)
        at = jnp.where(t < mine, t + first, t - mine + OWN_TILES)
        return pltpu.make_async_copy(tiles_ref.at[at], buf.at[slot], sem.at[slot])

    loads = [(v_ref, 0, BLOCKS_DEV)]
    for side, ref in enumerate(beside_refs):
        loads.append((ref, BLOCKS_DEV + REACH * side, REACH))
    arriving = [
        pltpu.make_async_copy(ref, values.at[pl.ds(at, size)], in_sem.at[i])
        for i, (ref, at, size) in enumerate(loads)
    ]
    if held_ref is not None:
        arriving.append(pltpu.make_async_copy(held_ref, total, in_sem.at[3]))
    for load in arriving:
        load.start()
    for t in range(OP_FIRST):
        copy(t).start()
    for load in arriving:
        load.wait()
    for _, at, size in loads:
        for g in range(at, at + size):
            hi, lo = halves(values[g])
            both_ref[g, :fields] = hi
            both_ref[g, fields:] = lo

    def started(t):
        return jnp.minimum(jnp.minimum(OP_FIRST + 2 * t, t + OP_SLOTS - 1), count)

    def arrive(t):
        following, end = started(t), started(t + 1)
        for more in range(2):

            @pl.when(following + more < end)
            def _(more=more):
                copy(following + more).start()

        copy(t).wait()
        return buf.at[lax.rem(t, OP_SLOTS)]

    def with_itself(t, carry):
        tile = arrive(t)
        total[t] = product(both_ref[t], tile, NN)
        return carry

    def with_another(t, carry):
        tile = arrive(t)
        one, other = own_pair(t + first, offsets)
        total[one] += product(both_ref[other], tile, NN)
        total[other] += product(both_ref[one], tile, NT)
        return carry

    def with_beside(t, carry):
        tile = arrive(t)
        one, other = halo_pair(t - mine, offsets)
        side = BLOCKS_DEV + jnp.where(other < 0, other + REACH, other - BLOCKS_DEV + REACH)
        total[one] += product(both_ref[side], tile, NN)
        return carry

    if first == 0:
        lax.fori_loop(0, BLOCKS_DEV, with_itself, 0)
    lax.fori_loop(max(BLOCKS_DEV - first, 0), mine, with_another, 0)
    if halo:
        lax.fori_loop(mine, count, with_beside, 0)
    leaving = [
        pltpu.make_async_copy(
            total.at[pl.ds(REACH * side, REACH)], ref, out_sem.at[BLOCKS_DEV + 1 + side]
        )
        for side, ref in enumerate(edge_refs)
    ]
    leaving.append(pltpu.make_async_copy(total, out_ref, out_sem.at[BLOCKS_DEV]))
    if send:
        leaving += out_copies(total, slots_ref, target_ref, out_sem)
    for out in leaving:
        out.start()
    if send:
        lane = lax.broadcasted_iota(jnp.int32, (fields, COL_DEV), 1)
        dots = jnp.zeros((fields, COL_DEV), jnp.float32)
        for at, one, other in products_of(values, total, held):
            summed = functools.reduce(jnp.add, [one[g] * other[g] for g in range(BLOCKS_DEV)])
            dots = jnp.where(lane == at, jnp.sum(summed, axis=1, keepdims=True), dots)
        dots = jnp.concatenate([dots, jnp.zeros((COL_DEV - fields, COL_DEV), jnp.float32)], axis=0)
        dots_ref[...] = dots.T[:EXTRA]
    for out in leaving:
        out.wait()


def products_of(v, image, second):
    if second:
        return [(3, v, image)]
    return [(0, v, v), (1, v, image), (2, image, image)]


def out_copies(values_ref, slots_ref, target_ref, sem):
    return [
        pltpu.make_async_copy(values_ref.at[g], slots_ref.at[target_ref[g]], sem.at[g])
        for g in range(BLOCKS_DEV)
    ]


SMEM_SPEC = pl.BlockSpec(memory_space=pltpu.SMEM)
VMEM_SPEC = pl.BlockSpec(memory_space=pltpu.VMEM)
HBM_SPEC = pl.BlockSpec(memory_space=pltpu.HBM)


def in_hbm(x):
    return pltpu.with_memory_space_constraint(x, pltpu.HBM)


def slot_shape(v):
    return pltpu.HBM((lax.axis_size(SIXTEEN), *v.shape[1:]), jnp.float32)


def applied(scalars, targets, tiles, v, tiles_of=(0, None), beside=(), held=None, send=False):
    blocks, fields, _ = v.shape
    edges = send and held is None
    out = pltpu.HBM(v.shape, jnp.float32)
    ins = [in_hbm(x) for x in (v, *beside, held) if x is not None] + [tiles]
    number = (tiles_of[1] or OWN_TILES) - tiles_of[0] + HALO_TILES * bool(beside)
    out = pl.pallas_call(
        functools.partial(op_kernel, *tiles_of, bool(beside), held is not None, send),
        in_specs=[SMEM_SPEC] * 2 + [HBM_SPEC] * len(ins),
        out_specs=[HBM_SPEC] + [HBM_SPEC] * (2 * edges) + [HBM_SPEC, VMEM_SPEC] * send,
        scratch_shapes=[
            pltpu.VMEM((blocks + 2 * REACH, fields, BLOCK), jnp.float32),
            pltpu.VMEM((blocks + 2 * REACH, 2 * fields, BLOCK), jnp.bfloat16),
            pltpu.VMEM(v.shape, jnp.float32),
            pltpu.VMEM((OP_SLOTS, 2 * BLOCK, BLOCK), jnp.bfloat16),
            pltpu.SemaphoreType.DMA((OP_SLOTS,)),
            pltpu.SemaphoreType.DMA((4,)),
            pltpu.SemaphoreType.DMA((BLOCKS_DEV + 3,)),
        ],
        out_shape=[out]
        + [pltpu.HBM((REACH, fields, BLOCK), jnp.float32)] * (2 * edges)
        + [slot_shape(v), jax.ShapeDtypeStruct((EXTRA, COL_DEV), jnp.float32)] * send,
        compiler_params=pltpu.CompilerParams(vmem_limit_bytes=28 << 20),
        cost_estimate=pl.CostEstimate(
            flops=3 * number * 3 * fields * BLOCK * BLOCK,
            bytes_accessed=number * 4 * BLOCK * BLOCK,
            transcendentals=0,
        ),
        name="applied",
    )(scalars, targets, *ins)
    return out if send else out[0]


def gate_kernel(*refs):
    pass


def gate(slots, *others):
    return pl.pallas_call(
        gate_kernel,
        in_specs=[HBM_SPEC] + [VMEM_SPEC] * len(others),
        out_specs=HBM_SPEC,
        out_shape=pltpu.HBM(slots.shape, jnp.float32),
        input_output_aliases={0: 0},
        compiler_params=pltpu.CompilerParams(vmem_limit_bytes=1 << 20),
        name="gate",
    )(slots, *(other[0, :8, :COL_DEV] for other in others))


def residual_kernel(
    target_ref, obs_ref, weight_ref, row_ref, before_ref, before_row_ref, after_ref,
    after_row_ref, col_ref, out_ref, before_out_ref, after_out_ref, slots_ref, buf, sem,
):
    fields = obs_ref.shape[0]
    col = col_ref[...]

    def block(at, obs, weight, row, g):
        for ra in range(STRIP):
            r = STRIP * g + ra
            left = obs[:fields, r, :] - row[:, r : r + 1] - col
            weighted = weight[r : r + 1, :] * left
            buf[at, :, COL_DEV * ra : COL_DEV * (ra + 1)] = weighted

    copies = []
    for g in range(BLOCKS_DEV):
        block(g, obs_ref, weight_ref, row_ref, g)
        copies.append(
            pltpu.make_async_copy(buf.at[g], slots_ref.at[target_ref[g]], sem.at[g])
        )
        copies[-1].start()
    copies.append(
        pltpu.make_async_copy(buf.at[pl.ds(0, BLOCKS_DEV)], out_ref, sem.at[BLOCKS_DEV])
    )
    copies[-1].start()
    sides = ((before_ref, before_row_ref, before_out_ref), (after_ref, after_row_ref, after_out_ref))
    for side, (obs, row, out) in enumerate(sides):
        first = BLOCKS_DEV + REACH * side
        for g in range(REACH):
            block(first + g, obs, obs.at[fields], row, g)
        copies.append(
            pltpu.make_async_copy(
                buf.at[pl.ds(first, REACH)], out, sem.at[BLOCKS_DEV + 1 + side]
            )
        )
        copies[-1].start()
    for copy in copies:
        copy.wait()


def residual_of(targets, observations, weight, row_effect, before, before_row, after, after_row, col):
    fields = observations.shape[0]
    own = pltpu.HBM((BLOCKS_DEV, fields, BLOCK), jnp.float32)
    side = pltpu.HBM((REACH, fields, BLOCK), jnp.float32)
    return pl.pallas_call(
        residual_kernel,
        in_specs=[SMEM_SPEC] + [VMEM_SPEC] * 8,
        out_specs=[HBM_SPEC] * 4,
        scratch_shapes=[
            pltpu.VMEM((BLOCKS_DEV + 2 * REACH, fields, BLOCK), jnp.float32),
            pltpu.SemaphoreType.DMA((BLOCKS_DEV + 3,)),
        ],
        out_shape=[own, side, side, slot_shape(own)],
        compiler_params=pltpu.CompilerParams(vmem_limit_bytes=12 << 20),
        name="residual",
    )(targets, observations, weight, row_effect, before, before_row, after, after_row, col)


def scales_of(dots_ref, scale_ref, part):
    @pl.when(pl.program_id(0) == 0)
    def _():
        scale_ref[...] = step_scales(*(dots_ref[k : k + 1] for k in range(4))).T

    return scale_ref[pl.ds(pl.multiple_of(pl.program_id(0) * part, part), part), :]


def first_kernel(src_ref, dots_ref, *refs):
    ins, (x_ref, r_ref, scale_ref) = refs[:-3], refs[-3:]
    scale = scales_of(dots_ref, scale_ref, x_ref.shape[0])
    for j in range(BLOCKS_DEV):
        r0, m1 = (ref[0] for ref in ins[2 * j : 2 * j + 2])
        x_ref[:, j, :] = scale[:, 0:1] * r0 + scale[:, 1:2] * m1
        r_ref[:, j, :] = scale[:, 2:3] * r0 + scale[:, 3:4] * m1


def second_kernel(src_ref, dots_ref, part_ref, *refs):
    ins, (r_ref, scale_ref) = refs[:-2], refs[-2:]
    scale = scales_of(dots_ref, scale_ref, r_ref.shape[0])
    for j in range(BLOCKS_DEV):
        r_ref[:, j, :] = part_ref[:, j, :] + scale[:, 4:5] * ins[j][0]


def combined(kernel, name, outs, sources, dots, held, *owned):
    _, fields, _ = owned[0].shape
    part = 16
    by_field = pl.BlockSpec((part, BLOCKS_DEV, BLOCK), lambda i, s: (i, 0, 0))
    ins, specs = list(held), [by_field] * len(held)
    for j in range(BLOCKS_DEV):
        for v in owned:
            ins.append(v)
            specs.append(
                pl.BlockSpec(
                    (1, part, BLOCK), functools.partial(lambda j, i, s: (s[j], i, 0), j)
                )
            )
    shape = jax.ShapeDtypeStruct((fields, BLOCKS_DEV, BLOCK), jnp.float32)
    return pl.pallas_call(
        kernel,
        grid_spec=pltpu.PrefetchScalarGridSpec(
            num_scalar_prefetch=1,
            grid=(fields // part,),
            in_specs=[pl.BlockSpec(dots.shape, lambda i, s: (0, 0))] + specs,
            out_specs=[by_field] * outs,
            scratch_shapes=[pltpu.VMEM((COL_DEV, 8), jnp.float32)],
        ),
        out_shape=[shape] * outs,
        compiler_params=pltpu.CompilerParams(vmem_limit_bytes=20 << 20),
        name=name,
    )(sources, dots, *ins)


def to_owners(slots):
    return lax.all_to_all(slots, SIXTEEN, 0, 0, tiled=True)


def step_scales(h00, h01, h11, h12):
    mu = h01 / h00
    var = (h11 - mu * h01) / h00
    a0 = 1.0 / (1.0 + mu)
    beta = var * a0 * a0
    skew = (h12 - mu * h11 - mu * (h11 - mu * h01)) / h00
    a1 = var / (var + skew - var * var * a0)
    x_r0 = a0 + a1 * beta + a1 * a0 * mu
    x_m1 = -a1 * a0
    r_r0 = a0 * mu * (1.0 - a1) - a1 * beta
    r_m1 = -a0 * (1.0 - a1) - a1 * a0 * mu - a1 * beta
    r_m2 = a1 * a0
    zero = jnp.zeros_like(mu)
    return jnp.concatenate([x_r0, x_m1, r_r0, r_m1, r_m2, zero, zero, zero], axis=0)


def on_device(observations, huber_scale, observed, jitter, owner_map, neighbours):
    fields, row_dev, col_dev = observations.shape
    sixteen_size = lax.axis_size(SIXTEEN)
    my_place = lax.axis_index(SIXTEEN)
    group_place = lax.axis_index(WIDE)
    total_strips = BLOCKS_DEV * sixteen_size
    weight = observed.astype(jnp.float32)
    spread_scale = huber_scale[:, None, None]

    def with_count(part, count):
        rows = jnp.zeros((8, count.shape[0]), jnp.float32).at[0].set(count)
        return jnp.concatenate([part, rows], axis=0)

    def terms(row_effect, col_effect):
        return weight[None] * jnp.clip(
            (observations - row_effect[:, :, None] - col_effect[:, None, :]) / spread_scale,
            -HUBER_EDGE,
            HUBER_EDGE,
        )

    def sum_wide(part):
        for axis in WIDE[::-1]:
            part = sum_direct(part, axis)
        return part

    row_effect = jnp.zeros((fields, row_dev), jnp.float32)
    col_effect = jnp.zeros((fields, col_dev), jnp.float32)
    part = with_count(jnp.sum(terms(row_effect, col_effect), axis=2), jnp.sum(weight, axis=1))
    part, jitter, owner_map, neighbours = lax.optimization_barrier(
        (part, jitter, owner_map, neighbours)
    )
    group_map = owner_map[0]
    scalars = jnp.concatenate(
        [neighbours[0, 0], jnp.stack([my_place, group_place, total_strips * STRIP])]
    ).astype(jnp.int32)

    def beside_tiles(part, axis, chunk, tiles, near=()):
        first = sum(CHUNKS[:chunk])
        if chunk:
            part, tiles = lax.optimization_barrier((part, tiles))
        received = sent_to_all(part, axis)
        tiles = covariance_tiles(first, CHUNKS[chunk], scalars, jitter, near, tiles)
        return lax.optimization_barrier((received, tiles))

    edges = jnp.concatenate([observations, weight[None], jitter], axis=0)
    before, after = beside(edges, REACH * STRIP, 1)
    received, tiles = beside_tiles(part, WIDE, 0, None)
    total = jnp.sum(received, axis=0)
    row_count = jnp.maximum(total[fields], 1.0)
    row_effect = huber_scale[:, None] * total[:fields] / row_count[None, :]
    part = with_count(jnp.sum(terms(row_effect, col_effect), axis=1), jnp.sum(weight, axis=0))
    received, tiles = beside_tiles(part, SIXTEEN, 1, tiles)
    total = jnp.sum(received, axis=0)
    col_count = jnp.maximum(total[fields], 1.0)
    col_effect = huber_scale[:, None] * total[:fields] / col_count[None, :]
    part = with_count(jnp.sum(terms(row_effect, col_effect), axis=2), jnp.zeros_like(row_count))
    received, tiles = beside_tiles(part, WIDE, 2, tiles)
    received, before, after = lax.optimization_barrier((received, before, after))
    near = (before[fields + 1 :], after[fields + 1 :])
    total = jnp.sum(received, axis=0)
    row_effect = row_effect + huber_scale[:, None] * total[:fields] / row_count[None, :]
    part = jnp.sum(terms(row_effect, col_effect), axis=1)
    part = jnp.concatenate([part, row_effect.reshape(-1, col_dev)], axis=0)
    received, tiles = beside_tiles(part, SIXTEEN, 3, tiles, near)
    total = jnp.sum(received[:, :fields], axis=0)
    col_effect = col_effect + huber_scale[:, None] * total / col_count[None, :]

    def rows_of(place, first):
        rows = lax.dynamic_index_in_dim(received[:, fields:], place % sixteen_size, 0, False)
        return rows.reshape(fields, row_dev)[:, first : first + REACH * STRIP]

    row_before = rows_of(my_place + sixteen_size - 1, row_dev - REACH * STRIP)
    row_after = rows_of(my_place + 1, 0)

    my_targets = lax.dynamic_slice_in_dim(group_map, my_place * BLOCKS_DEV, BLOCKS_DEV)
    r0, r0_before, r0_after, slots = residual_of(
        my_targets, observations, weight, row_effect, before, row_before, after, row_after, col_effect
    )
    owned_r0 = to_owners(slots)
    m1, initial, last, slots, dots = applied(
        scalars, my_targets, tiles, r0, beside=(r0_before, r0_after), send=True
    )
    before, after = swapped(initial, last)
    part = applied(scalars, my_targets, tiles, m1, (0, EARLY_TILES))
    slots = gate(slots, part, before, after, owned_r0)
    owned_m1 = to_owners(slots)
    m2, slots, last = applied(
        scalars, my_targets, tiles, m1, (EARLY_TILES, None), (before, after), part, True
    )
    dots = sum_direct(sum_direct(dots + last, WIDE), SIXTEEN[1])
    slots = gate(slots, owned_m1, dots[None])
    owned_m2 = to_owners(slots)
    dots = sum_direct(dots, SIXTEEN[0])
    owned = owned_table(group_map, sixteen_size, BLOCKS_DEV)
    my_ids = lax.dynamic_index_in_dim(owned, my_place, 0, keepdims=False)
    sources = my_ids // BLOCKS_DEV
    solution_now, part = combined(
        first_kernel, "first", 2, sources, dots, (), in_hbm(owned_r0), in_hbm(owned_m1)
    )
    (residual_now,) = combined(second_kernel, "second", 1, sources, dots, (part,), owned_m2)
    return (solution_now[None, None], residual_now[None, None])


def solution(mesh):
    finer = Mesh(mesh.devices.reshape(4, 2, 4, 4), ("wide_0", "wide_1", "sixteen_0", "sixteen_1"))
    in_specs = (
        P(None, SIXTEEN, WIDE),
        P(),
        P(SIXTEEN, WIDE),
        P(None, SIXTEEN, WIDE),
        P(WIDE, None),
        P(WIDE, None, None),
    )
    out_specs = (P(WIDE, SIXTEEN, None, None, None), P(WIDE, SIXTEEN, None, None, None))
    return jax.shard_map(
        on_device, mesh=finer, in_specs=in_specs, out_specs=out_specs, check_vma=False
    )
```

```python
import functools

import jax
import jax.numpy as jnp
from jax import lax
from jax.experimental import pallas as pl
from jax.experimental.pallas import tpu as pltpu
from jax.sharding import Mesh
from jax.sharding import PartitionSpec as P

BLOCK = 512
BLOCKS_DEV = 8
REACH = 4
NEIGHBOURS = 6
PAIRED = NEIGHBOURS // 2
SWEEPS = 2
STRIP = 4
COL_DEV = 128
WIDE = ("wide_0", "wide_1")
SIXTEEN = ("sixteen_0", "sixteen_1")

HUBER_EDGE = 1.345
SILL_TERM = 0.02
ROOT_THREE = 1.7320508075688772
LOG2_E = 1.4426950408889634
SPREAD = 2.0 * STRIP
CUTOFF = 6.0 * STRIP
BAND = 24
GROUP = 16

OWN_TILES = BLOCKS_DEV + PAIRED * BLOCKS_DEV - 6
HALO_TILES = 2 * (2 + 3 + 4)
CHUNKS = (5, 9, 9, 21)
TILE_SLOTS = 4
OP_SLOTS = 12
OP_FIRST = 4
EXTRA = 8
EARLY_TILES = 23


def sent_to_all(shard, axis):
    peers = lax.axis_size(axis)
    return lax.all_to_all(
        jnp.broadcast_to(shard[None], (peers, *shard.shape)), axis, 0, 0, tiled=True
    )


def over_copies(shard, axis):
    return jnp.sum(sent_to_all(shard, axis), axis=0)


def sum_direct(part, axis):
    peers = lax.axis_size(axis)
    moved = [
        lax.ppermute(part, axis, [(i, (i + k) % peers) for i in range(peers)])
        for k in range(1, peers)
    ]
    return functools.reduce(jnp.add, moved, part)


def swapped(initial, last):
    peers = lax.axis_size(SIXTEEN)
    up = [(i, (i + 1) % peers) for i in range(peers)]
    down = [(j, i) for i, j in up]
    return lax.ppermute(last, SIXTEEN, up), lax.ppermute(initial, SIXTEEN, down)


def beside(shard, width, dim=0):
    length = shard.shape[dim]
    last = lax.slice_in_dim(shard, length - width, length, axis=dim)
    initial = lax.slice_in_dim(shard, 0, width, axis=dim)
    return swapped(*lax.optimization_barrier((initial, last)))


def owned_table(group_map, owners, per_owner):
    total_strips = group_map.shape[0]
    member = (group_map[None, :] == jnp.arange(owners, dtype=jnp.int32)[:, None]).astype(jnp.int32)
    ranked = jnp.cumsum(member, axis=1, dtype=jnp.int32) - 1
    slot_hit = (ranked[:, :, None] == jnp.arange(per_owner, dtype=jnp.int32)[None, None, :]).astype(
        jnp.int32
    ) * member[:, :, None]
    numbers = jnp.arange(total_strips, dtype=jnp.int32)
    return jnp.sum(slot_hit * numbers[None, :, None], axis=1, dtype=jnp.int32)


def offsets_of(list_ref):
    held = [
        functools.reduce(jnp.logical_or, [list_ref[n] == d for n in range(NEIGHBOURS)])
        for d in range(1, REACH)
    ]
    missing = jnp.where(held[0], jnp.where(held[1], jnp.where(held[2], 4, 3), 2), 1)
    return [k + jnp.where(missing <= k, 1, 0) for k in range(1, PAIRED + 1)]


def own_count(offsets):
    return (PAIRED + 1) * BLOCKS_DEV - (offsets[0] + offsets[1] + offsets[2])


def halo_count(offsets):
    return 2 * (offsets[0] + offsets[1] + offsets[2])


def own_pair(t, offsets):
    d1, d2, d3 = offsets
    p = t - BLOCKS_DEV
    n1, n2 = BLOCKS_DEV - d1, 2 * BLOCKS_DEV - d1 - d2
    one = jnp.where(p < n1, p, jnp.where(p < n2, p - n1, p - n2))
    return one, one + jnp.where(p < n1, d1, jnp.where(p < n2, d2, d3))


def halo_pair(q, offsets):
    d1, d2, d3 = offsets
    reach = d1 + d2 + d3
    right = q >= reach
    q = jnp.where(right, q - reach, q)
    step = jnp.where(q < d1, d1, jnp.where(q < d1 + d2, d2, d3))
    pos = jnp.where(q < d1, q, jnp.where(q < d1 + d2, q - d1, q - d1 - d2))
    one = jnp.where(right, BLOCKS_DEV - 1 - pos, pos)
    return one, jnp.where(right, one + step, one - step)


LISTED = OWN_TILES + HALO_TILES


def tiles_kernel(first, count, beside, held, scalar_ref, jitter_ref, *refs):
    beside_refs, refs = refs[:beside], refs[beside + held :]
    tiles_ref, buf, sem = refs
    a, b = ROOT_THREE * CUTOFF / SPREAD, 4.0
    offsets = offsets_of(scalar_ref)
    place, group = scalar_ref[NEIGHBOURS], scalar_ref[NEIGHBOURS + 1]
    total_rows = scalar_ref[NEIGHBOURS + 2]
    row_dev = STRIP * BLOCKS_DEV
    lane = lax.broadcasted_iota(jnp.int32, (GROUP, COL_DEV), 1)
    within = lax.broadcasted_iota(jnp.int32, (STRIP, COL_DEV), 0)
    across = lax.broadcasted_iota(jnp.int32, (STRIP, COL_DEV), 1)
    col_place = (group * COL_DEV + across).astype(jnp.float32)

    def out_copy(t):
        slot = lax.rem(t - first, TILE_SLOTS)
        return pltpu.make_async_copy(buf.at[slot], tiles_ref.at[t], sem.at[slot])

    def live(t):
        mine = (t < OWN_TILES) & (t < own_count(offsets))
        return mine | ((t >= OWN_TILES) & (t < OWN_TILES + halo_count(offsets)))

    def places(block, ref, at):
        row = lax.rem(place * row_dev + STRIP * block + total_rows, total_rows)
        rows = (row + within).astype(jnp.float32) + ref[0, pl.ds(at, STRIP), :]
        cols = col_place + ref[1, pl.ds(at, STRIP), :]
        return jnp.concatenate([rows, cols], axis=0) * (1.0 / CUTOFF)

    def pair_of(t):
        q = t - OWN_TILES
        one, other = own_pair(t, offsets)
        one_q, other_q = halo_pair(q, offsets)
        same = t < BLOCKS_DEV
        mine = t < OWN_TILES
        one = jnp.where(same, t, jnp.where(mine, one, one_q))
        return one, jnp.where(same, t, jnp.where(mine, other, other_q))

    def evaluate(slot, to, frm, sill):
        for rb in range(STRIP):
            row_b = jnp.broadcast_to(frm[rb : rb + 1], (COL_DEV, COL_DEV)).T
            col_b = jnp.broadcast_to(frm[STRIP + rb : STRIP + rb + 1], (COL_DEV, COL_DEV)).T
            for u in range(COL_DEV // 2 // GROUP):
                lo_s = slice(GROUP * u, GROUP * (u + 1))
                hi_s = slice(64 + GROUP * u, 64 + GROUP * (u + 1))
                near = (lane >= GROUP * u - BAND) & (lane < GROUP * (u + 1) + BAND)
                one_m = jnp.where(near, 1.0, 0.0).astype(jnp.bfloat16)
                other_m = jnp.where(near, 0.0, 1.0).astype(jnp.bfloat16)
                row_s = jnp.where(near, row_b[lo_s], row_b[hi_s])
                col_s = jnp.where(near, col_b[lo_s], col_b[hi_s])
                for ra in range(STRIP):
                    dr = row_s - to[ra : ra + 1]
                    dc = col_s - to[STRIP + ra : STRIP + ra + 1]
                    square = dr * dr + dc * dc
                    far = square * lax.rsqrt(jnp.maximum(square, 1e-30))
                    fading = jnp.maximum(1.0 - far, 0.0)
                    fading = fading * fading
                    fading = fading * fading
                    shape = (sill + (sill * (a + b)) * far) + (sill * (a * b)) * square
                    value = shape * fading * jnp.exp2((-a * LOG2_E) * far)
                    hi = value.astype(jnp.bfloat16)
                    lo = (value - hi.astype(jnp.float32)).astype(jnp.bfloat16)
                    lanes = slice(COL_DEV * ra, COL_DEV * (ra + 1))
                    top = rb * COL_DEV + GROUP * u
                    for part, at in ((hi, top), (lo, BLOCK + top)):
                        buf[slot, at : at + GROUP, lanes] = part * one_m
                        buf[slot, at + 64 : at + 64 + GROUP, lanes] = part * other_m

    def one_tile(t, carry):
        slot = lax.rem(t - first, TILE_SLOTS)
        past = jnp.maximum(t - TILE_SLOTS, first)

        @pl.when((t >= first + TILE_SLOTS) & live(past))
        def _():
            out_copy(past).wait()

        @pl.when(live(t))
        def _():
            one, other = pair_of(t)
            sill = jnp.where(one == other, (NEIGHBOURS + 1.0) * SILL_TERM, SILL_TERM)
            inside = jnp.clip(other, 0, BLOCKS_DEV - 1)
            to = places(one, jitter_ref, STRIP * one)
            frm = places(other, jitter_ref, STRIP * inside)
            if beside_refs:
                left = places(other, beside_refs[0], STRIP * jnp.clip(other + REACH, 0, REACH - 1))
                right = places(
                    other, beside_refs[1], STRIP * jnp.clip(other - BLOCKS_DEV, 0, REACH - 1)
                )
                frm = jnp.where(other < 0, left, jnp.where(other < BLOCKS_DEV, frm, right))
            evaluate(slot, to, frm, sill)
            out_copy(t).start()

        return carry

    lax.fori_loop(first, first + count, one_tile, 0)
    for t in range(max(first, first + count - TILE_SLOTS), first + count):

        @pl.when(live(t))
        def _(t=t):
            out_copy(t).wait()


def covariance_tiles(first, count, scalars, jitter, beside_jitter, held):
    extra = [] if held is None else [held]
    ins = [scalars, jitter, *beside_jitter, *extra]
    return pl.pallas_call(
        functools.partial(tiles_kernel, first, count, len(beside_jitter), len(extra)),
        in_specs=[SMEM_SPEC] + [VMEM_SPEC] * (1 + len(beside_jitter)) + [HBM_SPEC] * len(extra),
        out_specs=HBM_SPEC,
        scratch_shapes=[
            pltpu.VMEM((TILE_SLOTS, 2 * BLOCK, BLOCK), jnp.bfloat16),
            pltpu.SemaphoreType.DMA((TILE_SLOTS,)),
        ],
        out_shape=jax.ShapeDtypeStruct((LISTED, 2 * BLOCK, BLOCK), jnp.bfloat16),
        input_output_aliases={len(ins) - 1: 0} if extra else {},
        compiler_params=pltpu.CompilerParams(vmem_limit_bytes=12 << 20),
        cost_estimate=pl.CostEstimate(
            flops=count * 12 * BLOCK * BLOCK,
            bytes_accessed=count * 4 * BLOCK * BLOCK,
            transcendentals=count * BLOCK * BLOCK,
        ),
        name="tiles",
    )(*ins)


def halves(v):
    hi = v.astype(jnp.bfloat16)
    lo = (v - hi.astype(jnp.float32)).astype(jnp.bfloat16)
    return hi, lo


NN = (((1,), (0,)), ((), ()))
NT = (((1,), (1,)), ((), ()))


def product(both, tile_ref, dims):
    fields = both.shape[0] // 2
    main = lax.dot_general(
        both, tile_ref[:BLOCK], dims, preferred_element_type=jnp.float32
    )
    rest = lax.dot_general(
        both[:fields], tile_ref[BLOCK:], dims, preferred_element_type=jnp.float32
    )
    return main[:fields] + (main[fields:] + rest)


def op_kernel(first, last, halo, held, send, scalar_ref, target_ref, *refs):
    refs = list(refs)
    v_ref = refs.pop(0)
    beside_refs = [refs.pop(0), refs.pop(0)] if halo else []
    held_ref = refs.pop(0) if held else None
    tiles_ref = refs.pop(0)
    out_ref = None if send and held else refs.pop(0)
    edge_refs = [refs.pop(0), refs.pop(0)] if send and not held else []
    slots_ref, dots_ref = (refs.pop(0), refs.pop(0)) if send else (None, None)
    values, both_ref, total, buf, sem, in_sem, out_sem = refs
    fields = total.shape[1]
    offsets = offsets_of(scalar_ref)
    mine = (own_count(offsets) if last is None else last) - first
    count = mine + (halo_count(offsets) if halo else 0)

    def copy(t):
        slot = lax.rem(t, OP_SLOTS)
        at = jnp.where(t < mine, t + first, t - mine + OWN_TILES)
        return pltpu.make_async_copy(tiles_ref.at[at], buf.at[slot], sem.at[slot])

    loads = [(v_ref, 0, BLOCKS_DEV)]
    for side, ref in enumerate(beside_refs):
        loads.append((ref, BLOCKS_DEV + REACH * side, REACH))
    arriving = [
        pltpu.make_async_copy(ref, values.at[pl.ds(at, size)], in_sem.at[i])
        for i, (ref, at, size) in enumerate(loads)
    ]
    if held_ref is not None:
        arriving.append(pltpu.make_async_copy(held_ref, total, in_sem.at[3]))
    for load in arriving:
        load.start()
    for t in range(OP_FIRST):
        copy(t).start()
    for load in arriving:
        load.wait()
    for _, at, size in loads:
        for g in range(at, at + size):
            hi, lo = halves(values[g])
            both_ref[g, :fields] = hi
            both_ref[g, fields:] = lo

    def started(t):
        return jnp.minimum(jnp.minimum(OP_FIRST + 2 * t, t + OP_SLOTS - 1), count)

    def arrive(t):
        following, end = started(t), started(t + 1)
        for more in range(2):

            @pl.when(following + more < end)
            def _(more=more):
                copy(following + more).start()

        copy(t).wait()
        return buf.at[lax.rem(t, OP_SLOTS)]

    def with_itself(t, carry):
        tile = arrive(t)
        total[t] = product(both_ref[t], tile, NN)
        return carry

    def with_another(t, carry):
        tile = arrive(t)
        one, other = own_pair(t + first, offsets)
        total[one] += product(both_ref[other], tile, NN)
        total[other] += product(both_ref[one], tile, NT)
        return carry

    def with_beside(t, carry):
        tile = arrive(t)
        one, other = halo_pair(t - mine, offsets)
        side = BLOCKS_DEV + jnp.where(other < 0, other + REACH, other - BLOCKS_DEV + REACH)
        total[one] += product(both_ref[side], tile, NN)
        return carry

    if first == 0:
        lax.fori_loop(0, BLOCKS_DEV, with_itself, 0)
    lax.fori_loop(max(BLOCKS_DEV - first, 0), mine, with_another, 0)
    if halo:
        lax.fori_loop(mine, count, with_beside, 0)
    leaving = [
        pltpu.make_async_copy(
            total.at[pl.ds(REACH * side, REACH)], ref, out_sem.at[BLOCKS_DEV + 1 + side]
        )
        for side, ref in enumerate(edge_refs)
    ]
    if out_ref is not None:
        leaving.append(pltpu.make_async_copy(total, out_ref, out_sem.at[BLOCKS_DEV]))
    if send:
        leaving += out_copies(total, slots_ref, target_ref, out_sem)
    for out in leaving:
        out.start()
    if send:
        lane = lax.broadcasted_iota(jnp.int32, (fields, COL_DEV), 1)
        dots = jnp.zeros((fields, COL_DEV), jnp.float32)
        for at, one, other in products_of(values, total, held):
            summed = functools.reduce(jnp.add, [one[g] * other[g] for g in range(BLOCKS_DEV)])
            dots = jnp.where(lane == at, jnp.sum(summed, axis=1, keepdims=True), dots)
        dots = jnp.concatenate([dots, jnp.zeros((COL_DEV - fields, COL_DEV), jnp.float32)], axis=0)
        dots_ref[...] = dots.T[:EXTRA]
    for out in leaving:
        out.wait()


def products_of(v, image, second):
    if second:
        return [(3, v, image)]
    return [(0, v, v), (1, v, image), (2, image, image)]


def out_copies(values_ref, slots_ref, target_ref, sem):
    return [
        pltpu.make_async_copy(values_ref.at[g], slots_ref.at[target_ref[g]], sem.at[g])
        for g in range(BLOCKS_DEV)
    ]


SMEM_SPEC = pl.BlockSpec(memory_space=pltpu.SMEM)
VMEM_SPEC = pl.BlockSpec(memory_space=pltpu.VMEM)
HBM_SPEC = pl.BlockSpec(memory_space=pltpu.HBM)


def in_hbm(x):
    return pltpu.with_memory_space_constraint(x, pltpu.HBM)


def slot_shape(v):
    return pltpu.HBM((lax.axis_size(SIXTEEN), *v.shape[1:]), jnp.float32)


def applied(scalars, targets, tiles, v, tiles_of=(0, None), beside=(), held=None, send=False):
    blocks, fields, _ = v.shape
    edges = send and held is None
    whole = not send or edges
    out = pltpu.HBM(v.shape, jnp.float32)
    ins = [in_hbm(x) for x in (v, *beside, held) if x is not None] + [tiles]
    number = (tiles_of[1] or OWN_TILES) - tiles_of[0] + HALO_TILES * bool(beside)
    out = pl.pallas_call(
        functools.partial(op_kernel, *tiles_of, bool(beside), held is not None, send),
        in_specs=[SMEM_SPEC] * 2 + [HBM_SPEC] * len(ins),
        out_specs=[HBM_SPEC] * whole + [HBM_SPEC] * (2 * edges) + [HBM_SPEC, VMEM_SPEC] * send,
        scratch_shapes=[
            pltpu.VMEM((blocks + 2 * REACH, fields, BLOCK), jnp.float32),
            pltpu.VMEM((blocks + 2 * REACH, 2 * fields, BLOCK), jnp.bfloat16),
            pltpu.VMEM(v.shape, jnp.float32),
            pltpu.VMEM((OP_SLOTS, 2 * BLOCK, BLOCK), jnp.bfloat16),
            pltpu.SemaphoreType.DMA((OP_SLOTS,)),
            pltpu.SemaphoreType.DMA((4,)),
            pltpu.SemaphoreType.DMA((BLOCKS_DEV + 3,)),
        ],
        out_shape=[out] * whole
        + [pltpu.HBM((REACH, fields, BLOCK), jnp.float32)] * (2 * edges)
        + [slot_shape(v), jax.ShapeDtypeStruct((EXTRA, COL_DEV), jnp.float32)] * send,
        compiler_params=pltpu.CompilerParams(vmem_limit_bytes=28 << 20),
        cost_estimate=pl.CostEstimate(
            flops=3 * number * 3 * fields * BLOCK * BLOCK,
            bytes_accessed=number * 4 * BLOCK * BLOCK,
            transcendentals=0,
        ),
        name="applied",
    )(scalars, targets, *ins)
    return out if send else out[0]


def gate_kernel(*refs):
    pass


def gate(slots, *others):
    return pl.pallas_call(
        gate_kernel,
        in_specs=[HBM_SPEC] + [HBM_SPEC if other.ndim == 3 else VMEM_SPEC for other in others],
        out_specs=HBM_SPEC,
        out_shape=pltpu.HBM(slots.shape, jnp.float32),
        input_output_aliases={0: 0},
        compiler_params=pltpu.CompilerParams(vmem_limit_bytes=1 << 20),
        name="gate",
    )(slots, *(in_hbm(other) if other.ndim == 3 else other for other in others))


def residual_kernel(
    target_ref, obs_ref, weight_ref, row_ref, before_ref, before_row_ref, after_ref,
    after_row_ref, col_ref, out_ref, before_out_ref, after_out_ref, slots_ref, buf, sem,
):
    fields = obs_ref.shape[0]
    col = col_ref[...]

    def block(at, obs, weight, row, g):
        for ra in range(STRIP):
            r = STRIP * g + ra
            left = obs[:fields, r, :] - row[:, r : r + 1] - col
            weighted = weight[r : r + 1, :] * left
            buf[at, :, COL_DEV * ra : COL_DEV * (ra + 1)] = weighted

    copies = []
    for g in range(BLOCKS_DEV):
        block(g, obs_ref, weight_ref, row_ref, g)
        copies.append(
            pltpu.make_async_copy(buf.at[g], slots_ref.at[target_ref[g]], sem.at[g])
        )
        copies[-1].start()
    copies.append(
        pltpu.make_async_copy(buf.at[pl.ds(0, BLOCKS_DEV)], out_ref, sem.at[BLOCKS_DEV])
    )
    copies[-1].start()
    sides = ((before_ref, before_row_ref, before_out_ref), (after_ref, after_row_ref, after_out_ref))
    for side, (obs, row, out) in enumerate(sides):
        first = BLOCKS_DEV + REACH * side
        for g in range(REACH):
            block(first + g, obs, obs.at[fields], row, g)
        copies.append(
            pltpu.make_async_copy(
                buf.at[pl.ds(first, REACH)], out, sem.at[BLOCKS_DEV + 1 + side]
            )
        )
        copies[-1].start()
    for copy in copies:
        copy.wait()


def residual_of(targets, observations, weight, row_effect, before, before_row, after, after_row, col):
    fields = observations.shape[0]
    own = pltpu.HBM((BLOCKS_DEV, fields, BLOCK), jnp.float32)
    side = pltpu.HBM((REACH, fields, BLOCK), jnp.float32)
    return pl.pallas_call(
        residual_kernel,
        in_specs=[SMEM_SPEC] + [VMEM_SPEC] * 8,
        out_specs=[HBM_SPEC] * 4,
        scratch_shapes=[
            pltpu.VMEM((BLOCKS_DEV + 2 * REACH, fields, BLOCK), jnp.float32),
            pltpu.SemaphoreType.DMA((BLOCKS_DEV + 3,)),
        ],
        out_shape=[own, side, side, slot_shape(own)],
        compiler_params=pltpu.CompilerParams(vmem_limit_bytes=12 << 20),
        name="residual",
    )(targets, observations, weight, row_effect, before, before_row, after, after_row, col)


def scales_of(dots_ref, scale_ref, part):
    @pl.when(pl.program_id(0) == 0)
    def _():
        scale_ref[...] = step_scales(*(dots_ref[k : k + 1] for k in range(4))).T

    return scale_ref[pl.ds(pl.multiple_of(pl.program_id(0) * part, part), part), :]


def first_kernel(src_ref, dots_ref, *refs):
    ins, (x_ref, r_ref, scale_ref) = refs[:-3], refs[-3:]
    scale = scales_of(dots_ref, scale_ref, x_ref.shape[0])
    for j in range(BLOCKS_DEV):
        r0, m1 = (ref[0] for ref in ins[2 * j : 2 * j + 2])
        x_ref[:, j, :] = scale[:, 0:1] * r0 + scale[:, 1:2] * m1
        r_ref[:, j, :] = scale[:, 2:3] * r0 + scale[:, 3:4] * m1


def second_kernel(src_ref, dots_ref, part_ref, *refs):
    ins, (r_ref, scale_ref) = refs[:-2], refs[-2:]
    scale = scales_of(dots_ref, scale_ref, r_ref.shape[0])
    for j in range(BLOCKS_DEV):
        r_ref[:, j, :] = part_ref[:, j, :] + scale[:, 4:5] * ins[j][0]


def combined(kernel, name, outs, sources, dots, held, *owned):
    _, fields, _ = owned[0].shape
    part = 16
    by_field = pl.BlockSpec((part, BLOCKS_DEV, BLOCK), lambda i, s: (i, 0, 0))
    ins, specs = list(held), [by_field] * len(held)
    for j in range(BLOCKS_DEV):
        for v in owned:
            ins.append(v)
            specs.append(
                pl.BlockSpec(
                    (1, part, BLOCK), functools.partial(lambda j, i, s: (s[j], i, 0), j)
                )
            )
    shape = jax.ShapeDtypeStruct((fields, BLOCKS_DEV, BLOCK), jnp.float32)
    return pl.pallas_call(
        kernel,
        grid_spec=pltpu.PrefetchScalarGridSpec(
            num_scalar_prefetch=1,
            grid=(fields // part,),
            in_specs=[pl.BlockSpec(dots.shape, lambda i, s: (0, 0))] + specs,
            out_specs=[by_field] * outs,
            scratch_shapes=[pltpu.VMEM((COL_DEV, 8), jnp.float32)],
        ),
        out_shape=[shape] * outs,
        compiler_params=pltpu.CompilerParams(vmem_limit_bytes=20 << 20),
        name=name,
    )(sources, dots, *ins)


def to_owners(slots):
    return lax.all_to_all(slots, SIXTEEN, 0, 0, tiled=True)


def step_scales(h00, h01, h11, h12):
    mu = h01 / h00
    var = (h11 - mu * h01) / h00
    a0 = 1.0 / (1.0 + mu)
    beta = var * a0 * a0
    skew = (h12 - mu * h11 - mu * (h11 - mu * h01)) / h00
    a1 = var / (var + skew - var * var * a0)
    x_r0 = a0 + a1 * beta + a1 * a0 * mu
    x_m1 = -a1 * a0
    r_r0 = a0 * mu * (1.0 - a1) - a1 * beta
    r_m1 = -a0 * (1.0 - a1) - a1 * a0 * mu - a1 * beta
    r_m2 = a1 * a0
    zero = jnp.zeros_like(mu)
    return jnp.concatenate([x_r0, x_m1, r_r0, r_m1, r_m2, zero, zero, zero], axis=0)


def on_device(observations, huber_scale, observed, jitter, owner_map, neighbours):
    fields, row_dev, col_dev = observations.shape
    sixteen_size = lax.axis_size(SIXTEEN)
    my_place = lax.axis_index(SIXTEEN)
    group_place = lax.axis_index(WIDE)
    total_strips = BLOCKS_DEV * sixteen_size
    weight = observed.astype(jnp.float32)
    spread_scale = huber_scale[:, None, None]

    def with_count(part, count):
        rows = jnp.zeros((8, count.shape[0]), jnp.float32).at[0].set(count)
        return jnp.concatenate([part, rows], axis=0)

    def terms(row_effect, col_effect):
        return weight[None] * jnp.clip(
            (observations - row_effect[:, :, None] - col_effect[:, None, :]) / spread_scale,
            -HUBER_EDGE,
            HUBER_EDGE,
        )

    def sum_wide(part):
        for axis in WIDE[::-1]:
            part = sum_direct(part, axis)
        return part

    row_effect = jnp.zeros((fields, row_dev), jnp.float32)
    col_effect = jnp.zeros((fields, col_dev), jnp.float32)
    part = with_count(jnp.sum(terms(row_effect, col_effect), axis=2), jnp.sum(weight, axis=1))
    part, jitter, owner_map, neighbours = lax.optimization_barrier(
        (part, jitter, owner_map, neighbours)
    )
    group_map = owner_map[0]
    scalars = jnp.concatenate(
        [neighbours[0, 0], jnp.stack([my_place, group_place, total_strips * STRIP])]
    ).astype(jnp.int32)

    def beside_tiles(part, axis, chunk, tiles, near=()):
        first = sum(CHUNKS[:chunk])
        if chunk:
            part, tiles = lax.optimization_barrier((part, tiles))
        received = sent_to_all(part, axis)
        tiles = covariance_tiles(first, CHUNKS[chunk], scalars, jitter, near, tiles)
        return lax.optimization_barrier((received, tiles))

    edges = jnp.concatenate([observations, weight[None], jitter], axis=0)
    before, after = beside(edges, REACH * STRIP, 1)
    received, tiles = beside_tiles(part, WIDE, 0, None)
    total = jnp.sum(received, axis=0)
    row_count = jnp.maximum(total[fields], 1.0)
    row_effect = huber_scale[:, None] * total[:fields] / row_count[None, :]
    part = with_count(jnp.sum(terms(row_effect, col_effect), axis=1), jnp.sum(weight, axis=0))
    received, tiles = beside_tiles(part, SIXTEEN, 1, tiles)
    total = jnp.sum(received, axis=0)
    col_count = jnp.maximum(total[fields], 1.0)
    col_effect = huber_scale[:, None] * total[:fields] / col_count[None, :]
    part = with_count(jnp.sum(terms(row_effect, col_effect), axis=2), jnp.zeros_like(row_count))
    received, tiles = beside_tiles(part, WIDE, 2, tiles)
    received, before, after = lax.optimization_barrier((received, before, after))
    near = (before[fields + 1 :], after[fields + 1 :])
    total = jnp.sum(received, axis=0)
    row_effect = row_effect + huber_scale[:, None] * total[:fields] / row_count[None, :]
    part = jnp.sum(terms(row_effect, col_effect), axis=1)
    part = jnp.concatenate([part, row_effect.reshape(-1, col_dev)], axis=0)
    received, tiles = beside_tiles(part, SIXTEEN, 3, tiles, near)
    total = jnp.sum(received[:, :fields], axis=0)
    col_effect = col_effect + huber_scale[:, None] * total / col_count[None, :]

    def rows_of(place, first):
        rows = lax.dynamic_index_in_dim(received[:, fields:], place % sixteen_size, 0, False)
        return rows.reshape(fields, row_dev)[:, first : first + REACH * STRIP]

    row_before = rows_of(my_place + sixteen_size - 1, row_dev - REACH * STRIP)
    row_after = rows_of(my_place + 1, 0)

    my_targets = lax.dynamic_slice_in_dim(group_map, my_place * BLOCKS_DEV, BLOCKS_DEV)
    r0, r0_before, r0_after, slots = residual_of(
        my_targets, observations, weight, row_effect, before, row_before, after, row_after, col_effect
    )
    owned_r0 = to_owners(slots)
    m1, initial, last, slots, dots = applied(
        scalars, my_targets, tiles, r0, beside=(r0_before, r0_after), send=True
    )
    before, after = swapped(initial, last)
    part = applied(scalars, my_targets, tiles, m1, (0, EARLY_TILES))
    slots = gate(slots, part, before, after)
    owned_m1 = to_owners(slots)
    slots, last = applied(
        scalars, my_targets, tiles, m1, (EARLY_TILES, None), (before, after), part, True
    )
    dots = sum_direct(sum_wide(dots + last), SIXTEEN[1])
    slots = gate(slots, dots)
    owned_m2 = to_owners(slots)
    dots = sum_direct(dots, SIXTEEN[0])
    owned = owned_table(group_map, sixteen_size, BLOCKS_DEV)
    my_ids = lax.dynamic_index_in_dim(owned, my_place, 0, keepdims=False)
    sources = my_ids // BLOCKS_DEV
    solution_now, part = combined(
        first_kernel, "first", 2, sources, dots, (), in_hbm(owned_r0), in_hbm(owned_m1)
    )
    (residual_now,) = combined(second_kernel, "second", 1, sources, dots, (part,), owned_m2)
    return (solution_now[None, None], residual_now[None, None])


def solution(mesh):
    finer = Mesh(mesh.devices.reshape(4, 2, 4, 4), ("wide_0", "wide_1", "sixteen_0", "sixteen_1"))
    in_specs = (
        P(None, SIXTEEN, WIDE),
        P(),
        P(SIXTEEN, WIDE),
        P(None, SIXTEEN, WIDE),
        P(WIDE, None),
        P(WIDE, None, None),
    )
    out_specs = (P(WIDE, SIXTEEN, None, None, None), P(WIDE, SIXTEEN, None, None, None))
    return jax.shard_map(
        on_device, mesh=finer, in_specs=in_specs, out_specs=out_specs, check_vma=False
    )
```

```python
import functools

import jax
import jax.numpy as jnp
from jax import lax
from jax.experimental import pallas as pl
from jax.experimental.pallas import tpu as pltpu
from jax.sharding import Mesh
from jax.sharding import PartitionSpec as P

BLOCK = 512
BLOCKS_DEV = 8
REACH = 4
NEIGHBOURS = 6
PAIRED = NEIGHBOURS // 2
SWEEPS = 2
STRIP = 4
COL_DEV = 128
WIDE = ("wide_0", "wide_1")
SIXTEEN = ("sixteen_0", "sixteen_1")

HUBER_EDGE = 1.345
SILL_TERM = 0.02
ROOT_THREE = 1.7320508075688772
LOG2_E = 1.4426950408889634
SPREAD = 2.0 * STRIP
CUTOFF = 6.0 * STRIP
BAND = 24
GROUP = 16

OWN_TILES = BLOCKS_DEV + PAIRED * BLOCKS_DEV - 6
HALO_TILES = 2 * (2 + 3 + 4)
CHUNKS = (3, 9, 9, 23)
TILE_SLOTS = 4
OP_SLOTS = 12
OP_FIRST = 4
EXTRA = 8
EARLY_TILES = 21


def sent_to_all(shard, axis):
    peers = lax.axis_size(axis)
    return lax.all_to_all(
        jnp.broadcast_to(shard[None], (peers, *shard.shape)), axis, 0, 0, tiled=True
    )


def over_copies(shard, axis):
    return jnp.sum(sent_to_all(shard, axis), axis=0)


def sum_direct(part, axis):
    peers = lax.axis_size(axis)
    moved = [
        lax.ppermute(part, axis, [(i, (i + k) % peers) for i in range(peers)])
        for k in range(1, peers)
    ]
    return functools.reduce(jnp.add, moved, part)


def swapped(initial, last):
    peers = lax.axis_size(SIXTEEN)
    up = [(i, (i + 1) % peers) for i in range(peers)]
    down = [(j, i) for i, j in up]
    return lax.ppermute(last, SIXTEEN, up), lax.ppermute(initial, SIXTEEN, down)


def beside(shard, width, dim=0):
    length = shard.shape[dim]
    last = lax.slice_in_dim(shard, length - width, length, axis=dim)
    initial = lax.slice_in_dim(shard, 0, width, axis=dim)
    return swapped(*lax.optimization_barrier((initial, last)))


def owned_table(group_map, owners, per_owner):
    total_strips = group_map.shape[0]
    member = (group_map[None, :] == jnp.arange(owners, dtype=jnp.int32)[:, None]).astype(jnp.int32)
    ranked = jnp.cumsum(member, axis=1, dtype=jnp.int32) - 1
    slot_hit = (ranked[:, :, None] == jnp.arange(per_owner, dtype=jnp.int32)[None, None, :]).astype(
        jnp.int32
    ) * member[:, :, None]
    numbers = jnp.arange(total_strips, dtype=jnp.int32)
    return jnp.sum(slot_hit * numbers[None, :, None], axis=1, dtype=jnp.int32)


def offsets_of(list_ref):
    held = [
        functools.reduce(jnp.logical_or, [list_ref[n] == d for n in range(NEIGHBOURS)])
        for d in range(1, REACH)
    ]
    missing = jnp.where(held[0], jnp.where(held[1], jnp.where(held[2], 4, 3), 2), 1)
    return [k + jnp.where(missing <= k, 1, 0) for k in range(1, PAIRED + 1)]


def own_count(offsets):
    return (PAIRED + 1) * BLOCKS_DEV - (offsets[0] + offsets[1] + offsets[2])


def halo_count(offsets):
    return 2 * (offsets[0] + offsets[1] + offsets[2])


def own_pair(t, offsets):
    d1, d2, d3 = offsets
    p = t - BLOCKS_DEV
    n1, n2 = BLOCKS_DEV - d1, 2 * BLOCKS_DEV - d1 - d2
    one = jnp.where(p < n1, p, jnp.where(p < n2, p - n1, p - n2))
    return one, one + jnp.where(p < n1, d1, jnp.where(p < n2, d2, d3))


def halo_pair(q, offsets):
    d1, d2, d3 = offsets
    reach = d1 + d2 + d3
    right = q >= reach
    q = jnp.where(right, q - reach, q)
    step = jnp.where(q < d1, d1, jnp.where(q < d1 + d2, d2, d3))
    pos = jnp.where(q < d1, q, jnp.where(q < d1 + d2, q - d1, q - d1 - d2))
    one = jnp.where(right, BLOCKS_DEV - 1 - pos, pos)
    return one, jnp.where(right, one + step, one - step)


LISTED = OWN_TILES + HALO_TILES


def tiles_kernel(first, count, beside, held, scalar_ref, jitter_ref, *refs):
    beside_refs, refs = refs[:beside], refs[beside + held :]
    tiles_ref, buf, sem = refs
    a, b = ROOT_THREE * CUTOFF / SPREAD, 4.0
    offsets = offsets_of(scalar_ref)
    place, group = scalar_ref[NEIGHBOURS], scalar_ref[NEIGHBOURS + 1]
    total_rows = scalar_ref[NEIGHBOURS + 2]
    row_dev = STRIP * BLOCKS_DEV
    lane = lax.broadcasted_iota(jnp.int32, (GROUP, COL_DEV), 1)
    within = lax.broadcasted_iota(jnp.int32, (STRIP, COL_DEV), 0)
    across = lax.broadcasted_iota(jnp.int32, (STRIP, COL_DEV), 1)
    col_place = (group * COL_DEV + across).astype(jnp.float32)

    def out_copy(t):
        slot = lax.rem(t - first, TILE_SLOTS)
        return pltpu.make_async_copy(buf.at[slot], tiles_ref.at[t], sem.at[slot])

    def live(t):
        mine = (t < OWN_TILES) & (t < own_count(offsets))
        return mine | ((t >= OWN_TILES) & (t < OWN_TILES + halo_count(offsets)))

    def places(block, ref, at):
        row = lax.rem(place * row_dev + STRIP * block + total_rows, total_rows)
        rows = (row + within).astype(jnp.float32) + ref[0, pl.ds(at, STRIP), :]
        cols = col_place + ref[1, pl.ds(at, STRIP), :]
        return jnp.concatenate([rows, cols], axis=0) * (1.0 / CUTOFF)

    def pair_of(t):
        q = t - OWN_TILES
        one, other = own_pair(t, offsets)
        one_q, other_q = halo_pair(q, offsets)
        same = t < BLOCKS_DEV
        mine = t < OWN_TILES
        one = jnp.where(same, t, jnp.where(mine, one, one_q))
        return one, jnp.where(same, t, jnp.where(mine, other, other_q))

    def evaluate(slot, to, frm, sill):
        for rb in range(STRIP):
            row_b = jnp.broadcast_to(frm[rb : rb + 1], (COL_DEV, COL_DEV)).T
            col_b = jnp.broadcast_to(frm[STRIP + rb : STRIP + rb + 1], (COL_DEV, COL_DEV)).T
            for u in range(COL_DEV // 2 // GROUP):
                lo_s = slice(GROUP * u, GROUP * (u + 1))
                hi_s = slice(64 + GROUP * u, 64 + GROUP * (u + 1))
                near = (lane >= GROUP * u - BAND) & (lane < GROUP * (u + 1) + BAND)
                one_m = jnp.where(near, 1.0, 0.0).astype(jnp.bfloat16)
                other_m = jnp.where(near, 0.0, 1.0).astype(jnp.bfloat16)
                row_s = jnp.where(near, row_b[lo_s], row_b[hi_s])
                col_s = jnp.where(near, col_b[lo_s], col_b[hi_s])
                for ra in range(STRIP):
                    dr = row_s - to[ra : ra + 1]
                    dc = col_s - to[STRIP + ra : STRIP + ra + 1]
                    square = dr * dr + dc * dc
                    far = square * lax.rsqrt(jnp.maximum(square, 1e-30))
                    fading = jnp.maximum(1.0 - far, 0.0)
                    fading = fading * fading
                    fading = fading * fading
                    shape = (sill + (sill * (a + b)) * far) + (sill * (a * b)) * square
                    value = shape * fading * jnp.exp2((-a * LOG2_E) * far)
                    hi = value.astype(jnp.bfloat16)
                    lo = (value - hi.astype(jnp.float32)).astype(jnp.bfloat16)
                    lanes = slice(COL_DEV * ra, COL_DEV * (ra + 1))
                    top = rb * COL_DEV + GROUP * u
                    for part, at in ((hi, top), (lo, BLOCK + top)):
                        buf[slot, at : at + GROUP, lanes] = part * one_m
                        buf[slot, at + 64 : at + 64 + GROUP, lanes] = part * other_m

    def one_tile(t, carry):
        slot = lax.rem(t - first, TILE_SLOTS)
        past = jnp.maximum(t - TILE_SLOTS, first)

        @pl.when((t >= first + TILE_SLOTS) & live(past))
        def _():
            out_copy(past).wait()

        @pl.when(live(t))
        def _():
            one, other = pair_of(t)
            sill = jnp.where(one == other, (NEIGHBOURS + 1.0) * SILL_TERM, SILL_TERM)
            inside = jnp.clip(other, 0, BLOCKS_DEV - 1)
            to = places(one, jitter_ref, STRIP * one)
            frm = places(other, jitter_ref, STRIP * inside)
            if beside_refs:
                left = places(other, beside_refs[0], STRIP * jnp.clip(other + REACH, 0, REACH - 1))
                right = places(
                    other, beside_refs[1], STRIP * jnp.clip(other - BLOCKS_DEV, 0, REACH - 1)
                )
                frm = jnp.where(other < 0, left, jnp.where(other < BLOCKS_DEV, frm, right))
            evaluate(slot, to, frm, sill)
            out_copy(t).start()

        return carry

    lax.fori_loop(first, first + count, one_tile, 0)
    for t in range(max(first, first + count - TILE_SLOTS), first + count):

        @pl.when(live(t))
        def _(t=t):
            out_copy(t).wait()


def covariance_tiles(first, count, scalars, jitter, beside_jitter, held):
    extra = [] if held is None else [held]
    ins = [scalars, jitter, *beside_jitter, *extra]
    return pl.pallas_call(
        functools.partial(tiles_kernel, first, count, len(beside_jitter), len(extra)),
        in_specs=[SMEM_SPEC] + [VMEM_SPEC] * (1 + len(beside_jitter)) + [HBM_SPEC] * len(extra),
        out_specs=HBM_SPEC,
        scratch_shapes=[
            pltpu.VMEM((TILE_SLOTS, 2 * BLOCK, BLOCK), jnp.bfloat16),
            pltpu.SemaphoreType.DMA((TILE_SLOTS,)),
        ],
        out_shape=jax.ShapeDtypeStruct((LISTED, 2 * BLOCK, BLOCK), jnp.bfloat16),
        input_output_aliases={len(ins) - 1: 0} if extra else {},
        compiler_params=pltpu.CompilerParams(vmem_limit_bytes=12 << 20),
        cost_estimate=pl.CostEstimate(
            flops=count * 12 * BLOCK * BLOCK,
            bytes_accessed=count * 4 * BLOCK * BLOCK,
            transcendentals=count * BLOCK * BLOCK,
        ),
        name="tiles",
    )(*ins)


def halves(v):
    hi = v.astype(jnp.bfloat16)
    lo = (v - hi.astype(jnp.float32)).astype(jnp.bfloat16)
    return hi, lo


NN = (((1,), (0,)), ((), ()))
NT = (((1,), (1,)), ((), ()))


def product(both, tile_ref, dims):
    fields = both.shape[0] // 2
    main = lax.dot_general(
        both, tile_ref[:BLOCK], dims, preferred_element_type=jnp.float32
    )
    rest = lax.dot_general(
        both[:fields], tile_ref[BLOCK:], dims, preferred_element_type=jnp.float32
    )
    return main[:fields] + (main[fields:] + rest)


def op_kernel(first, last, pieces, halo, held, send, scalar_ref, target_ref, *refs):
    refs = list(refs)
    v_refs = [refs.pop(0) for _ in range(pieces)]
    beside_refs = [refs.pop(0), refs.pop(0)] if halo else []
    held_ref = refs.pop(0) if held else None
    tiles_ref = refs.pop(0)
    out_ref = None if send else refs.pop(0)
    edge_refs = [refs.pop(0), refs.pop(0)] if send and not held else []
    slots_ref, dots_ref = (refs.pop(0), refs.pop(0)) if send else (None, None)
    values, both_ref, total, buf, sem, in_sem, out_sem = refs
    fields = total.shape[1]
    offsets = offsets_of(scalar_ref)
    mine = (own_count(offsets) if last is None else last) - first
    count = mine + (halo_count(offsets) if halo else 0)

    def copy(t):
        slot = lax.rem(t, OP_SLOTS)
        at = jnp.where(t < mine, t + first, t - mine + OWN_TILES)
        return pltpu.make_async_copy(tiles_ref.at[at], buf.at[slot], sem.at[slot])

    size = BLOCKS_DEV // pieces
    loads = [(ref, size * i, size) for i, ref in enumerate(v_refs)]
    for side, ref in enumerate(beside_refs):
        loads.append((ref, BLOCKS_DEV + REACH * side, REACH))
    arriving = [
        pltpu.make_async_copy(ref, values.at[pl.ds(at, size)], in_sem.at[i])
        for i, (ref, at, size) in enumerate(loads)
    ]
    if held_ref is not None:
        arriving.append(pltpu.make_async_copy(held_ref, total, in_sem.at[4]))
    for load in arriving:
        load.start()
    for t in range(OP_FIRST):
        copy(t).start()
    for load in arriving:
        load.wait()
    for _, at, size in loads:
        for g in range(at, at + size):
            hi, lo = halves(values[g])
            both_ref[g, :fields] = hi
            both_ref[g, fields:] = lo

    def started(t):
        return jnp.minimum(jnp.minimum(OP_FIRST + 2 * t, t + OP_SLOTS - 1), count)

    def arrive(t):
        following, end = started(t), started(t + 1)
        for more in range(2):

            @pl.when(following + more < end)
            def _(more=more):
                copy(following + more).start()

        copy(t).wait()
        return buf.at[lax.rem(t, OP_SLOTS)]

    def with_itself(t, carry):
        tile = arrive(t)
        total[t] = product(both_ref[t], tile, NN)
        return carry

    def with_another(t, carry):
        tile = arrive(t)
        one, other = own_pair(t + first, offsets)
        total[one] += product(both_ref[other], tile, NN)
        total[other] += product(both_ref[one], tile, NT)
        return carry

    def with_beside(t, carry):
        tile = arrive(t)
        one, other = halo_pair(t - mine, offsets)
        side = BLOCKS_DEV + jnp.where(other < 0, other + REACH, other - BLOCKS_DEV + REACH)
        total[one] += product(both_ref[side], tile, NN)
        return carry

    if first == 0:
        lax.fori_loop(0, BLOCKS_DEV, with_itself, 0)
    lax.fori_loop(max(BLOCKS_DEV - first, 0), mine, with_another, 0)
    if halo:
        lax.fori_loop(mine, count, with_beside, 0)
    leaving = [
        pltpu.make_async_copy(
            total.at[pl.ds(REACH * side, REACH)], ref, out_sem.at[BLOCKS_DEV + 1 + side]
        )
        for side, ref in enumerate(edge_refs)
    ]
    if out_ref is not None:
        leaving.append(pltpu.make_async_copy(total, out_ref, out_sem.at[BLOCKS_DEV]))
    if send:
        leaving += out_copies(total, slots_ref, target_ref, out_sem)
    for out in leaving:
        out.start()
    if send:
        lane = lax.broadcasted_iota(jnp.int32, (fields, COL_DEV), 1)
        dots = jnp.zeros((fields, COL_DEV), jnp.float32)
        for at, one, other in products_of(values, total, held):
            summed = functools.reduce(jnp.add, [one[g] * other[g] for g in range(BLOCKS_DEV)])
            dots = jnp.where(lane == at, jnp.sum(summed, axis=1, keepdims=True), dots)
        dots = jnp.concatenate([dots, jnp.zeros((COL_DEV - fields, COL_DEV), jnp.float32)], axis=0)
        dots_ref[...] = dots.T[:EXTRA]
    for out in leaving:
        out.wait()


def products_of(v, image, second):
    if second:
        return [(3, v, image)]
    return [(0, v, v), (1, v, image), (2, image, image)]


def out_copies(values_ref, slots_ref, target_ref, sem):
    return [
        pltpu.make_async_copy(values_ref.at[g], slots_ref.at[target_ref[g]], sem.at[g])
        for g in range(BLOCKS_DEV)
    ]


SMEM_SPEC = pl.BlockSpec(memory_space=pltpu.SMEM)
VMEM_SPEC = pl.BlockSpec(memory_space=pltpu.VMEM)
HBM_SPEC = pl.BlockSpec(memory_space=pltpu.HBM)


def in_hbm(x):
    return pltpu.with_memory_space_constraint(x, pltpu.HBM)


def slot_shape(v):
    return pltpu.HBM((lax.axis_size(SIXTEEN), *v.shape[1:]), jnp.float32)


def applied(scalars, targets, tiles, v, tiles_of=(0, None), beside=(), held=None, send=False):
    _, fields, _ = v[0].shape
    blocks = BLOCKS_DEV
    shape = (blocks, fields, BLOCK)
    edges = send and held is None
    out = pltpu.HBM(shape, jnp.float32)
    ins = [in_hbm(x) for x in (*v, *beside, held) if x is not None] + [tiles]
    number = (tiles_of[1] or OWN_TILES) - tiles_of[0] + HALO_TILES * bool(beside)
    out = pl.pallas_call(
        functools.partial(op_kernel, *tiles_of, len(v), bool(beside), held is not None, send),
        in_specs=[SMEM_SPEC] * 2 + [HBM_SPEC] * len(ins),
        out_specs=[HBM_SPEC] * (not send) + [HBM_SPEC] * (2 * edges) + [HBM_SPEC, VMEM_SPEC] * send,
        scratch_shapes=[
            pltpu.VMEM((blocks + 2 * REACH, fields, BLOCK), jnp.float32),
            pltpu.VMEM((blocks + 2 * REACH, 2 * fields, BLOCK), jnp.bfloat16),
            pltpu.VMEM(shape, jnp.float32),
            pltpu.VMEM((OP_SLOTS, 2 * BLOCK, BLOCK), jnp.bfloat16),
            pltpu.SemaphoreType.DMA((OP_SLOTS,)),
            pltpu.SemaphoreType.DMA((5,)),
            pltpu.SemaphoreType.DMA((BLOCKS_DEV + 3,)),
        ],
        out_shape=[out] * (not send)
        + [pltpu.HBM((REACH, fields, BLOCK), jnp.float32)] * (2 * edges)
        + [slot_shape(out), jax.ShapeDtypeStruct((EXTRA, COL_DEV), jnp.float32)] * send,
        compiler_params=pltpu.CompilerParams(vmem_limit_bytes=28 << 20),
        cost_estimate=pl.CostEstimate(
            flops=3 * number * 3 * fields * BLOCK * BLOCK,
            bytes_accessed=number * 4 * BLOCK * BLOCK,
            transcendentals=0,
        ),
        name="applied",
    )(scalars, targets, *ins)
    return out if send else out[0]


def gate_kernel(*refs):
    pass


def gate(slots, *others):
    return pl.pallas_call(
        gate_kernel,
        in_specs=[HBM_SPEC] + [HBM_SPEC if other.ndim == 3 else VMEM_SPEC for other in others],
        out_specs=HBM_SPEC,
        out_shape=pltpu.HBM(slots.shape, jnp.float32),
        input_output_aliases={0: 0},
        compiler_params=pltpu.CompilerParams(vmem_limit_bytes=1 << 20),
        name="gate",
    )(slots, *(in_hbm(other) if other.ndim == 3 else other for other in others))


def residual_kernel(
    target_ref, obs_ref, weight_ref, row_ref, before_ref, before_row_ref, after_ref,
    after_row_ref, col_ref, out_ref, before_out_ref, after_out_ref, slots_ref, buf, sem,
):
    fields = obs_ref.shape[0]
    col = col_ref[...]

    def block(at, obs, weight, row, g):
        for ra in range(STRIP):
            r = STRIP * g + ra
            left = obs[:fields, r, :] - row[:, r : r + 1] - col
            weighted = weight[r : r + 1, :] * left
            buf[at, :, COL_DEV * ra : COL_DEV * (ra + 1)] = weighted

    copies = []
    for g in range(BLOCKS_DEV):
        block(g, obs_ref, weight_ref, row_ref, g)
        copies.append(
            pltpu.make_async_copy(buf.at[g], slots_ref.at[target_ref[g]], sem.at[g])
        )
        copies[-1].start()
    copies.append(
        pltpu.make_async_copy(buf.at[pl.ds(0, BLOCKS_DEV)], out_ref, sem.at[BLOCKS_DEV])
    )
    copies[-1].start()
    sides = ((before_ref, before_row_ref, before_out_ref), (after_ref, after_row_ref, after_out_ref))
    for side, (obs, row, out) in enumerate(sides):
        first = BLOCKS_DEV + REACH * side
        for g in range(REACH):
            block(first + g, obs, obs.at[fields], row, g)
        copies.append(
            pltpu.make_async_copy(
                buf.at[pl.ds(first, REACH)], out, sem.at[BLOCKS_DEV + 1 + side]
            )
        )
        copies[-1].start()
    for copy in copies:
        copy.wait()


def residual_of(targets, observations, weight, row_effect, before, before_row, after, after_row, col):
    fields = observations.shape[0]
    own = pltpu.HBM((BLOCKS_DEV, fields, BLOCK), jnp.float32)
    side = pltpu.HBM((REACH, fields, BLOCK), jnp.float32)
    return pl.pallas_call(
        residual_kernel,
        in_specs=[SMEM_SPEC] + [VMEM_SPEC] * 8,
        out_specs=[HBM_SPEC] * 4,
        scratch_shapes=[
            pltpu.VMEM((BLOCKS_DEV + 2 * REACH, fields, BLOCK), jnp.float32),
            pltpu.SemaphoreType.DMA((BLOCKS_DEV + 3,)),
        ],
        out_shape=[own, side, side, slot_shape(own)],
        compiler_params=pltpu.CompilerParams(vmem_limit_bytes=12 << 20),
        name="residual",
    )(targets, observations, weight, row_effect, before, before_row, after, after_row, col)


def scales_of(dots_ref, scale_ref, part):
    @pl.when(pl.program_id(0) == 0)
    def _():
        scale_ref[...] = step_scales(*(dots_ref[k : k + 1] for k in range(4))).T

    return scale_ref[pl.ds(pl.multiple_of(pl.program_id(0) * part, part), part), :]


def first_kernel(src_ref, dots_ref, *refs):
    ins, (x_ref, r_ref, scale_ref) = refs[:-3], refs[-3:]
    scale = scales_of(dots_ref, scale_ref, x_ref.shape[0])
    for j in range(BLOCKS_DEV):
        r0, m1 = (ref[0] for ref in ins[2 * j : 2 * j + 2])
        x_ref[:, j, :] = scale[:, 0:1] * r0 + scale[:, 1:2] * m1
        r_ref[:, j, :] = scale[:, 2:3] * r0 + scale[:, 3:4] * m1


def second_kernel(src_ref, dots_ref, part_ref, *refs):
    ins, (r_ref, scale_ref) = refs[:-2], refs[-2:]
    scale = scales_of(dots_ref, scale_ref, r_ref.shape[0])
    for j in range(BLOCKS_DEV):
        r_ref[:, j, :] = part_ref[:, j, :] + scale[:, 4:5] * ins[j][0]


def combined(kernel, name, outs, sources, dots, held, *owned):
    _, fields, _ = owned[0].shape
    part = 16
    by_field = pl.BlockSpec((part, BLOCKS_DEV, BLOCK), lambda i, s: (i, 0, 0))
    ins, specs = list(held), [by_field] * len(held)
    for j in range(BLOCKS_DEV):
        for v in owned:
            ins.append(v)
            specs.append(
                pl.BlockSpec(
                    (1, part, BLOCK), functools.partial(lambda j, i, s: (s[j], i, 0), j)
                )
            )
    shape = jax.ShapeDtypeStruct((fields, BLOCKS_DEV, BLOCK), jnp.float32)
    return pl.pallas_call(
        kernel,
        grid_spec=pltpu.PrefetchScalarGridSpec(
            num_scalar_prefetch=1,
            grid=(fields // part,),
            in_specs=[pl.BlockSpec(dots.shape, lambda i, s: (0, 0))] + specs,
            out_specs=[by_field] * outs,
            scratch_shapes=[pltpu.VMEM((COL_DEV, 8), jnp.float32)],
        ),
        out_shape=[shape] * outs,
        compiler_params=pltpu.CompilerParams(vmem_limit_bytes=20 << 20),
        name=name,
    )(sources, dots, *ins)


def to_owners(slots):
    return lax.all_to_all(slots, SIXTEEN, 0, 0, tiled=True)


def step_scales(h00, h01, h11, h12):
    mu = h01 / h00
    var = (h11 - mu * h01) / h00
    a0 = 1.0 / (1.0 + mu)
    beta = var * a0 * a0
    skew = (h12 - mu * h11 - mu * (h11 - mu * h01)) / h00
    a1 = var / (var + skew - var * var * a0)
    x_r0 = a0 + a1 * beta + a1 * a0 * mu
    x_m1 = -a1 * a0
    r_r0 = a0 * mu * (1.0 - a1) - a1 * beta
    r_m1 = -a0 * (1.0 - a1) - a1 * a0 * mu - a1 * beta
    r_m2 = a1 * a0
    zero = jnp.zeros_like(mu)
    return jnp.concatenate([x_r0, x_m1, r_r0, r_m1, r_m2, zero, zero, zero], axis=0)


def on_device(observations, huber_scale, observed, jitter, owner_map, neighbours):
    fields, row_dev, col_dev = observations.shape
    sixteen_size = lax.axis_size(SIXTEEN)
    my_place = lax.axis_index(SIXTEEN)
    group_place = lax.axis_index(WIDE)
    total_strips = BLOCKS_DEV * sixteen_size
    weight = observed.astype(jnp.float32)
    spread_scale = huber_scale[:, None, None]

    def with_count(part, count):
        rows = jnp.zeros((8, count.shape[0]), jnp.float32).at[0].set(count)
        return jnp.concatenate([part, rows], axis=0)

    def terms(row_effect, col_effect):
        return weight[None] * jnp.clip(
            (observations - row_effect[:, :, None] - col_effect[:, None, :]) / spread_scale,
            -HUBER_EDGE,
            HUBER_EDGE,
        )

    def sum_wide(part):
        for axis in WIDE[::-1]:
            part = sum_direct(part, axis)
        return part

    row_effect = jnp.zeros((fields, row_dev), jnp.float32)
    col_effect = jnp.zeros((fields, col_dev), jnp.float32)
    part = with_count(jnp.sum(terms(row_effect, col_effect), axis=2), jnp.sum(weight, axis=1))
    part, jitter, owner_map, neighbours = lax.optimization_barrier(
        (part, jitter, owner_map, neighbours)
    )
    group_map = owner_map[0]
    scalars = jnp.concatenate(
        [neighbours[0, 0], jnp.stack([my_place, group_place, total_strips * STRIP])]
    ).astype(jnp.int32)

    def beside_tiles(part, axis, chunk, tiles, near=()):
        first = sum(CHUNKS[:chunk])
        if chunk:
            part, tiles = lax.optimization_barrier((part, tiles))
        received = sent_to_all(part, axis)
        tiles = covariance_tiles(first, CHUNKS[chunk], scalars, jitter, near, tiles)
        return lax.optimization_barrier((received, tiles))

    edges = jnp.concatenate([observations, weight[None], jitter], axis=0)
    before, after = beside(edges, REACH * STRIP, 1)
    received, tiles = beside_tiles(part, WIDE, 0, None)
    total = jnp.sum(received, axis=0)
    row_count = jnp.maximum(total[fields], 1.0)
    row_effect = huber_scale[:, None] * total[:fields] / row_count[None, :]
    part = with_count(jnp.sum(terms(row_effect, col_effect), axis=1), jnp.sum(weight, axis=0))
    received, tiles = beside_tiles(part, SIXTEEN, 1, tiles)
    total = jnp.sum(received, axis=0)
    col_count = jnp.maximum(total[fields], 1.0)
    col_effect = huber_scale[:, None] * total[:fields] / col_count[None, :]
    part = with_count(jnp.sum(terms(row_effect, col_effect), axis=2), jnp.zeros_like(row_count))
    received, tiles = beside_tiles(part, WIDE, 2, tiles)
    received, before, after = lax.optimization_barrier((received, before, after))
    near = (before[fields + 1 :], after[fields + 1 :])
    total = jnp.sum(received, axis=0)
    row_effect = row_effect + huber_scale[:, None] * total[:fields] / row_count[None, :]
    part = jnp.sum(terms(row_effect, col_effect), axis=1)
    part = jnp.concatenate([part, row_effect.reshape(-1, col_dev)], axis=0)
    received, tiles = beside_tiles(part, SIXTEEN, 3, tiles, near)
    total = jnp.sum(received[:, :fields], axis=0)
    col_effect = col_effect + huber_scale[:, None] * total / col_count[None, :]

    def rows_of(place, first):
        rows = lax.dynamic_index_in_dim(received[:, fields:], place % sixteen_size, 0, False)
        return rows.reshape(fields, row_dev)[:, first : first + REACH * STRIP]

    row_before = rows_of(my_place + sixteen_size - 1, row_dev - REACH * STRIP)
    row_after = rows_of(my_place + 1, 0)

    my_targets = lax.dynamic_slice_in_dim(group_map, my_place * BLOCKS_DEV, BLOCKS_DEV)
    r0, r0_before, r0_after, slots = residual_of(
        my_targets, observations, weight, row_effect, before, row_before, after, row_after, col_effect
    )
    owned_r0 = to_owners(slots)
    *m1, slots, dots = applied(
        scalars, my_targets, tiles, (r0,), beside=(r0_before, r0_after), send=True
    )
    before, after = swapped(*m1)
    part = applied(scalars, my_targets, tiles, m1, (0, EARLY_TILES))
    slots = gate(slots, part, before, after)
    owned_m1 = to_owners(slots)
    slots, last = applied(
        scalars, my_targets, tiles, m1, (EARLY_TILES, None), (before, after), part, True
    )
    dots = sum_direct(sum_wide(dots + last), SIXTEEN[1])
    slots = gate(slots, dots)
    owned_m2 = to_owners(slots)
    dots = sum_direct(dots, SIXTEEN[0])
    owned = owned_table(group_map, sixteen_size, BLOCKS_DEV)
    my_ids = lax.dynamic_index_in_dim(owned, my_place, 0, keepdims=False)
    sources = my_ids // BLOCKS_DEV
    solution_now, part = combined(
        first_kernel, "first", 2, sources, dots, (), in_hbm(owned_r0), in_hbm(owned_m1)
    )
    (residual_now,) = combined(second_kernel, "second", 1, sources, dots, (part,), owned_m2)
    return (solution_now[None, None], residual_now[None, None])


def solution(mesh):
    finer = Mesh(mesh.devices.reshape(4, 2, 4, 4), ("wide_0", "wide_1", "sixteen_0", "sixteen_1"))
    in_specs = (
        P(None, SIXTEEN, WIDE),
        P(),
        P(SIXTEEN, WIDE),
        P(None, SIXTEEN, WIDE),
        P(WIDE, None),
        P(WIDE, None, None),
    )
    out_specs = (P(WIDE, SIXTEEN, None, None, None), P(WIDE, SIXTEEN, None, None, None))
    return jax.shard_map(
        on_device, mesh=finer, in_specs=in_specs, out_specs=out_specs, check_vma=False
    )
```

```python
import functools

import jax
import jax.numpy as jnp
from jax import lax
from jax.experimental import pallas as pl
from jax.experimental.pallas import tpu as pltpu
from jax.sharding import Mesh
from jax.sharding import PartitionSpec as P

BLOCK = 512
BLOCKS_DEV = 8
REACH = 4
NEIGHBOURS = 6
PAIRED = NEIGHBOURS // 2
SWEEPS = 2
STRIP = 4
COL_DEV = 128
WIDE = ("wide_0", "wide_1")
SIXTEEN = ("sixteen_0", "sixteen_1")

HUBER_EDGE = 1.345
SILL_TERM = 0.02
ROOT_THREE = 1.7320508075688772
LOG2_E = 1.4426950408889634
SPREAD = 2.0 * STRIP
CUTOFF = 6.0 * STRIP
BAND = 24
GROUP = 16

OWN_TILES = BLOCKS_DEV + PAIRED * BLOCKS_DEV - 6
HALO_TILES = 2 * (2 + 3 + 4)
CHUNKS = (5, 9, 9, 21)
TILE_SLOTS = 4
OP_SLOTS = 12
OP_FIRST = 4
EXTRA = 8
EARLY_TILES = 21


def sent_to_all(shard, axis):
    peers = lax.axis_size(axis)
    return lax.all_to_all(
        jnp.broadcast_to(shard[None], (peers, *shard.shape)), axis, 0, 0, tiled=True
    )


def over_copies(shard, axis):
    return jnp.sum(sent_to_all(shard, axis), axis=0)


def sum_direct(part, axis):
    peers = lax.axis_size(axis)
    moved = [
        lax.ppermute(part, axis, [(i, (i + k) % peers) for i in range(peers)])
        for k in range(1, peers)
    ]
    return functools.reduce(jnp.add, moved, part)


def swapped(initial, last):
    peers = lax.axis_size(SIXTEEN)
    up = [(i, (i + 1) % peers) for i in range(peers)]
    down = [(j, i) for i, j in up]
    return lax.ppermute(last, SIXTEEN, up), lax.ppermute(initial, SIXTEEN, down)


def beside(shard, width, dim=0):
    length = shard.shape[dim]
    last = lax.slice_in_dim(shard, length - width, length, axis=dim)
    initial = lax.slice_in_dim(shard, 0, width, axis=dim)
    return swapped(*lax.optimization_barrier((initial, last)))


def owned_table(group_map, owners, per_owner):
    total_strips = group_map.shape[0]
    member = (group_map[None, :] == jnp.arange(owners, dtype=jnp.int32)[:, None]).astype(jnp.int32)
    ranked = jnp.cumsum(member, axis=1, dtype=jnp.int32) - 1
    slot_hit = (ranked[:, :, None] == jnp.arange(per_owner, dtype=jnp.int32)[None, None, :]).astype(
        jnp.int32
    ) * member[:, :, None]
    numbers = jnp.arange(total_strips, dtype=jnp.int32)
    return jnp.sum(slot_hit * numbers[None, :, None], axis=1, dtype=jnp.int32)


def offsets_of(list_ref):
    held = [
        functools.reduce(jnp.logical_or, [list_ref[n] == d for n in range(NEIGHBOURS)])
        for d in range(1, REACH)
    ]
    missing = jnp.where(held[0], jnp.where(held[1], jnp.where(held[2], 4, 3), 2), 1)
    return [k + jnp.where(missing <= k, 1, 0) for k in range(1, PAIRED + 1)]


def own_count(offsets):
    return (PAIRED + 1) * BLOCKS_DEV - (offsets[0] + offsets[1] + offsets[2])


def halo_count(offsets):
    return 2 * (offsets[0] + offsets[1] + offsets[2])


def own_pair(t, offsets):
    d1, d2, d3 = offsets
    p = t - BLOCKS_DEV
    n1, n2 = BLOCKS_DEV - d1, 2 * BLOCKS_DEV - d1 - d2
    one = jnp.where(p < n1, p, jnp.where(p < n2, p - n1, p - n2))
    return one, one + jnp.where(p < n1, d1, jnp.where(p < n2, d2, d3))


def halo_pair(q, offsets):
    d1, d2, d3 = offsets
    reach = d1 + d2 + d3
    right = q >= reach
    q = jnp.where(right, q - reach, q)
    step = jnp.where(q < d1, d1, jnp.where(q < d1 + d2, d2, d3))
    pos = jnp.where(q < d1, q, jnp.where(q < d1 + d2, q - d1, q - d1 - d2))
    one = jnp.where(right, BLOCKS_DEV - 1 - pos, pos)
    return one, jnp.where(right, one + step, one - step)


LISTED = OWN_TILES + HALO_TILES


def tiles_kernel(first, count, beside, held, scalar_ref, jitter_ref, *refs):
    beside_refs, refs = refs[:beside], refs[beside + held :]
    tiles_ref, buf, sem = refs
    a, b = ROOT_THREE * CUTOFF / SPREAD, 4.0
    offsets = offsets_of(scalar_ref)
    place, group = scalar_ref[NEIGHBOURS], scalar_ref[NEIGHBOURS + 1]
    total_rows = scalar_ref[NEIGHBOURS + 2]
    row_dev = STRIP * BLOCKS_DEV
    lane = lax.broadcasted_iota(jnp.int32, (GROUP, COL_DEV), 1)
    within = lax.broadcasted_iota(jnp.int32, (STRIP, COL_DEV), 0)
    across = lax.broadcasted_iota(jnp.int32, (STRIP, COL_DEV), 1)
    col_place = (group * COL_DEV + across).astype(jnp.float32)

    def out_copy(t):
        slot = lax.rem(t - first, TILE_SLOTS)
        return pltpu.make_async_copy(buf.at[slot], tiles_ref.at[t], sem.at[slot])

    def live(t):
        mine = (t < OWN_TILES) & (t < own_count(offsets))
        return mine | ((t >= OWN_TILES) & (t < OWN_TILES + halo_count(offsets)))

    def places(block, ref, at):
        row = lax.rem(place * row_dev + STRIP * block + total_rows, total_rows)
        rows = (row + within).astype(jnp.float32) + ref[0, pl.ds(at, STRIP), :]
        cols = col_place + ref[1, pl.ds(at, STRIP), :]
        return jnp.concatenate([rows, cols], axis=0) * (1.0 / CUTOFF)

    def pair_of(t):
        q = t - OWN_TILES
        one, other = own_pair(t, offsets)
        one_q, other_q = halo_pair(q, offsets)
        same = t < BLOCKS_DEV
        mine = t < OWN_TILES
        one = jnp.where(same, t, jnp.where(mine, one, one_q))
        return one, jnp.where(same, t, jnp.where(mine, other, other_q))

    def evaluate(slot, to, frm, sill):
        for rb in range(STRIP):
            row_b = jnp.broadcast_to(frm[rb : rb + 1], (COL_DEV, COL_DEV)).T
            col_b = jnp.broadcast_to(frm[STRIP + rb : STRIP + rb + 1], (COL_DEV, COL_DEV)).T
            for u in range(COL_DEV // 2 // GROUP):
                lo_s = slice(GROUP * u, GROUP * (u + 1))
                hi_s = slice(64 + GROUP * u, 64 + GROUP * (u + 1))
                near = (lane >= GROUP * u - BAND) & (lane < GROUP * (u + 1) + BAND)
                one_m = jnp.where(near, 1.0, 0.0).astype(jnp.bfloat16)
                other_m = jnp.where(near, 0.0, 1.0).astype(jnp.bfloat16)
                row_s = jnp.where(near, row_b[lo_s], row_b[hi_s])
                col_s = jnp.where(near, col_b[lo_s], col_b[hi_s])
                for ra in range(STRIP):
                    dr = row_s - to[ra : ra + 1]
                    dc = col_s - to[STRIP + ra : STRIP + ra + 1]
                    square = dr * dr + dc * dc
                    far = square * lax.rsqrt(jnp.maximum(square, 1e-30))
                    fading = jnp.maximum(1.0 - far, 0.0)
                    fading = fading * fading
                    fading = fading * fading
                    shape = (sill + (sill * (a + b)) * far) + (sill * (a * b)) * square
                    value = shape * fading * jnp.exp2((-a * LOG2_E) * far)
                    hi = value.astype(jnp.bfloat16)
                    lo = (value - hi.astype(jnp.float32)).astype(jnp.bfloat16)
                    lanes = slice(COL_DEV * ra, COL_DEV * (ra + 1))
                    top = rb * COL_DEV + GROUP * u
                    for part, at in ((hi, top), (lo, BLOCK + top)):
                        buf[slot, at : at + GROUP, lanes] = part * one_m
                        buf[slot, at + 64 : at + 64 + GROUP, lanes] = part * other_m

    def one_tile(t, carry):
        slot = lax.rem(t - first, TILE_SLOTS)
        past = jnp.maximum(t - TILE_SLOTS, first)

        @pl.when((t >= first + TILE_SLOTS) & live(past))
        def _():
            out_copy(past).wait()

        @pl.when(live(t))
        def _():
            one, other = pair_of(t)
            sill = jnp.where(one == other, (NEIGHBOURS + 1.0) * SILL_TERM, SILL_TERM)
            inside = jnp.clip(other, 0, BLOCKS_DEV - 1)
            to = places(one, jitter_ref, STRIP * one)
            frm = places(other, jitter_ref, STRIP * inside)
            if beside_refs:
                left = places(other, beside_refs[0], STRIP * jnp.clip(other + REACH, 0, REACH - 1))
                right = places(
                    other, beside_refs[1], STRIP * jnp.clip(other - BLOCKS_DEV, 0, REACH - 1)
                )
                frm = jnp.where(other < 0, left, jnp.where(other < BLOCKS_DEV, frm, right))
            evaluate(slot, to, frm, sill)
            out_copy(t).start()

        return carry

    lax.fori_loop(first, first + count, one_tile, 0)
    for t in range(max(first, first + count - TILE_SLOTS), first + count):

        @pl.when(live(t))
        def _(t=t):
            out_copy(t).wait()


def covariance_tiles(first, count, scalars, jitter, beside_jitter, held):
    extra = [] if held is None else [held]
    ins = [scalars, jitter, *beside_jitter, *extra]
    return pl.pallas_call(
        functools.partial(tiles_kernel, first, count, len(beside_jitter), len(extra)),
        in_specs=[SMEM_SPEC] + [VMEM_SPEC] * (1 + len(beside_jitter)) + [HBM_SPEC] * len(extra),
        out_specs=HBM_SPEC,
        scratch_shapes=[
            pltpu.VMEM((TILE_SLOTS, 2 * BLOCK, BLOCK), jnp.bfloat16),
            pltpu.SemaphoreType.DMA((TILE_SLOTS,)),
        ],
        out_shape=jax.ShapeDtypeStruct((LISTED, 2 * BLOCK, BLOCK), jnp.bfloat16),
        input_output_aliases={len(ins) - 1: 0} if extra else {},
        compiler_params=pltpu.CompilerParams(vmem_limit_bytes=12 << 20),
        cost_estimate=pl.CostEstimate(
            flops=count * 12 * BLOCK * BLOCK,
            bytes_accessed=count * 4 * BLOCK * BLOCK,
            transcendentals=count * BLOCK * BLOCK,
        ),
        name="tiles",
    )(*ins)


def halves(v):
    hi = v.astype(jnp.bfloat16)
    lo = (v - hi.astype(jnp.float32)).astype(jnp.bfloat16)
    return hi, lo


NN = (((1,), (0,)), ((), ()))
NT = (((1,), (1,)), ((), ()))


def product(both, tile_ref, dims):
    fields = both.shape[0] // 2
    main = lax.dot_general(
        both, tile_ref[:BLOCK], dims, preferred_element_type=jnp.float32
    )
    rest = lax.dot_general(
        both[:fields], tile_ref[BLOCK:], dims, preferred_element_type=jnp.float32
    )
    return main[:fields] + (main[fields:] + rest)


def op_kernel(first, last, pieces, halo, held, send, scalar_ref, target_ref, *refs):
    refs = list(refs)
    v_refs = [refs.pop(0) for _ in range(pieces)]
    beside_refs = [refs.pop(0), refs.pop(0)] if halo else []
    held_ref = refs.pop(0) if held else None
    tiles_ref = refs.pop(0)
    out_ref = None if send else refs.pop(0)
    edge_refs = [refs.pop(0), refs.pop(0)] if send and not held else []
    slots_ref, dots_ref = (refs.pop(0), refs.pop(0)) if send else (None, None)
    values, both_ref, total, buf, sem, in_sem, out_sem = refs
    fields = total.shape[1]
    offsets = offsets_of(scalar_ref)
    mine = (own_count(offsets) if last is None else last) - first
    count = mine + (halo_count(offsets) if halo else 0)

    def copy(t):
        slot = lax.rem(t, OP_SLOTS)
        at = jnp.where(t < mine, t + first, t - mine + OWN_TILES)
        return pltpu.make_async_copy(tiles_ref.at[at], buf.at[slot], sem.at[slot])

    size = BLOCKS_DEV // pieces
    loads = [(ref, size * i, size) for i, ref in enumerate(v_refs)]
    for side, ref in enumerate(beside_refs):
        loads.append((ref, BLOCKS_DEV + REACH * side, REACH))
    arriving = [
        pltpu.make_async_copy(ref, values.at[pl.ds(at, size)], in_sem.at[i])
        for i, (ref, at, size) in enumerate(loads)
    ]
    if held_ref is not None:
        arriving.append(pltpu.make_async_copy(held_ref, total, in_sem.at[4]))
    for load in arriving:
        load.start()
    for t in range(OP_FIRST):
        copy(t).start()
    for load in arriving:
        load.wait()
    for _, at, size in loads:
        for g in range(at, at + size):
            hi, lo = halves(values[g])
            both_ref[g, :fields] = hi
            both_ref[g, fields:] = lo

    def started(t):
        return jnp.minimum(jnp.minimum(OP_FIRST + 2 * t, t + OP_SLOTS - 1), count)

    def arrive(t):
        following, end = started(t), started(t + 1)
        for more in range(2):

            @pl.when(following + more < end)
            def _(more=more):
                copy(following + more).start()

        copy(t).wait()
        return buf.at[lax.rem(t, OP_SLOTS)]

    def with_itself(t, carry):
        tile = arrive(t)
        total[t] = product(both_ref[t], tile, NN)
        return carry

    def with_another(t, carry):
        tile = arrive(t)
        one, other = own_pair(t + first, offsets)
        total[one] += product(both_ref[other], tile, NN)
        total[other] += product(both_ref[one], tile, NT)
        return carry

    def with_beside(t, carry):
        tile = arrive(t)
        one, other = halo_pair(t - mine, offsets)
        side = BLOCKS_DEV + jnp.where(other < 0, other + REACH, other - BLOCKS_DEV + REACH)
        total[one] += product(both_ref[side], tile, NN)
        return carry

    if first == 0:
        lax.fori_loop(0, BLOCKS_DEV, with_itself, 0)
    lax.fori_loop(max(BLOCKS_DEV - first, 0), mine, with_another, 0)
    if halo:
        lax.fori_loop(mine, count, with_beside, 0)
    leaving = [
        pltpu.make_async_copy(
            total.at[pl.ds(REACH * side, REACH)], ref, out_sem.at[BLOCKS_DEV + 1 + side]
        )
        for side, ref in enumerate(edge_refs)
    ]
    if out_ref is not None:
        leaving.append(pltpu.make_async_copy(total, out_ref, out_sem.at[BLOCKS_DEV]))
    if send:
        leaving += out_copies(total, slots_ref, target_ref, out_sem)
    for out in leaving:
        out.start()
    if send:
        lane = lax.broadcasted_iota(jnp.int32, (fields, COL_DEV), 1)
        dots = jnp.zeros((fields, COL_DEV), jnp.float32)
        for at, one, other in products_of(values, total, held):
            summed = functools.reduce(jnp.add, [one[g] * other[g] for g in range(BLOCKS_DEV)])
            dots = jnp.where(lane == at, jnp.sum(summed, axis=1, keepdims=True), dots)
        dots = jnp.concatenate([dots, jnp.zeros((COL_DEV - fields, COL_DEV), jnp.float32)], axis=0)
        dots_ref[...] = dots.T[:EXTRA]
    for out in leaving:
        out.wait()


def products_of(v, image, second):
    if second:
        return [(3, v, image)]
    return [(0, v, v), (1, v, image), (2, image, image)]


def out_copies(values_ref, slots_ref, target_ref, sem):
    return [
        pltpu.make_async_copy(values_ref.at[g], slots_ref.at[target_ref[g]], sem.at[g])
        for g in range(BLOCKS_DEV)
    ]


SMEM_SPEC = pl.BlockSpec(memory_space=pltpu.SMEM)
VMEM_SPEC = pl.BlockSpec(memory_space=pltpu.VMEM)
HBM_SPEC = pl.BlockSpec(memory_space=pltpu.HBM)


def in_hbm(x):
    return pltpu.with_memory_space_constraint(x, pltpu.HBM)


def slot_shape(v):
    return pltpu.HBM((lax.axis_size(SIXTEEN), *v.shape[1:]), jnp.float32)


def applied(scalars, targets, tiles, v, tiles_of=(0, None), beside=(), held=None, send=False):
    _, fields, _ = v[0].shape
    blocks = BLOCKS_DEV
    shape = (blocks, fields, BLOCK)
    edges = send and held is None
    out = pltpu.HBM(shape, jnp.float32)
    ins = [in_hbm(x) for x in (*v, *beside, held) if x is not None] + [tiles]
    number = (tiles_of[1] or OWN_TILES) - tiles_of[0] + HALO_TILES * bool(beside)
    out = pl.pallas_call(
        functools.partial(op_kernel, *tiles_of, len(v), bool(beside), held is not None, send),
        in_specs=[SMEM_SPEC] * 2 + [HBM_SPEC] * len(ins),
        out_specs=[HBM_SPEC] * (not send) + [HBM_SPEC] * (2 * edges) + [HBM_SPEC, VMEM_SPEC] * send,
        scratch_shapes=[
            pltpu.VMEM((blocks + 2 * REACH, fields, BLOCK), jnp.float32),
            pltpu.VMEM((blocks + 2 * REACH, 2 * fields, BLOCK), jnp.bfloat16),
            pltpu.VMEM(shape, jnp.float32),
            pltpu.VMEM((OP_SLOTS, 2 * BLOCK, BLOCK), jnp.bfloat16),
            pltpu.SemaphoreType.DMA((OP_SLOTS,)),
            pltpu.SemaphoreType.DMA((5,)),
            pltpu.SemaphoreType.DMA((BLOCKS_DEV + 3,)),
        ],
        out_shape=[out] * (not send)
        + [pltpu.HBM((REACH, fields, BLOCK), jnp.float32)] * (2 * edges)
        + [slot_shape(out), jax.ShapeDtypeStruct((EXTRA, COL_DEV), jnp.float32)] * send,
        compiler_params=pltpu.CompilerParams(vmem_limit_bytes=28 << 20),
        cost_estimate=pl.CostEstimate(
            flops=3 * number * 3 * fields * BLOCK * BLOCK,
            bytes_accessed=number * 4 * BLOCK * BLOCK,
            transcendentals=0,
        ),
        name="applied",
    )(scalars, targets, *ins)
    return out if send else out[0]


def gate_kernel(*refs):
    pass


def gate(slots, *others):
    return pl.pallas_call(
        gate_kernel,
        in_specs=[HBM_SPEC] + [HBM_SPEC if other.ndim == 3 else VMEM_SPEC for other in others],
        out_specs=HBM_SPEC,
        out_shape=pltpu.HBM(slots.shape, jnp.float32),
        input_output_aliases={0: 0},
        compiler_params=pltpu.CompilerParams(vmem_limit_bytes=1 << 20),
        name="gate",
    )(slots, *(in_hbm(other) if other.ndim == 3 else other for other in others))


def residual_kernel(
    target_ref, obs_ref, weight_ref, row_ref, before_ref, before_row_ref, after_ref,
    after_row_ref, col_ref, out_ref, before_out_ref, after_out_ref, slots_ref, buf, sem,
):
    fields = obs_ref.shape[0]
    col = col_ref[...]

    def block(at, obs, weight, row, g):
        for ra in range(STRIP):
            r = STRIP * g + ra
            left = obs[:fields, r, :] - row[:, r : r + 1] - col
            weighted = weight[r : r + 1, :] * left
            buf[at, :, COL_DEV * ra : COL_DEV * (ra + 1)] = weighted

    copies = []
    for g in range(BLOCKS_DEV):
        block(g, obs_ref, weight_ref, row_ref, g)
        copies.append(
            pltpu.make_async_copy(buf.at[g], slots_ref.at[target_ref[g]], sem.at[g])
        )
        copies[-1].start()
    copies.append(
        pltpu.make_async_copy(buf.at[pl.ds(0, BLOCKS_DEV)], out_ref, sem.at[BLOCKS_DEV])
    )
    copies[-1].start()
    sides = ((before_ref, before_row_ref, before_out_ref), (after_ref, after_row_ref, after_out_ref))
    for side, (obs, row, out) in enumerate(sides):
        first = BLOCKS_DEV + REACH * side
        for g in range(REACH):
            block(first + g, obs, obs.at[fields], row, g)
        copies.append(
            pltpu.make_async_copy(
                buf.at[pl.ds(first, REACH)], out, sem.at[BLOCKS_DEV + 1 + side]
            )
        )
        copies[-1].start()
    for copy in copies:
        copy.wait()


def residual_of(targets, observations, weight, row_effect, before, before_row, after, after_row, col):
    fields = observations.shape[0]
    own = pltpu.HBM((BLOCKS_DEV, fields, BLOCK), jnp.float32)
    side = pltpu.HBM((REACH, fields, BLOCK), jnp.float32)
    return pl.pallas_call(
        residual_kernel,
        in_specs=[SMEM_SPEC] + [VMEM_SPEC] * 8,
        out_specs=[HBM_SPEC] * 4,
        scratch_shapes=[
            pltpu.VMEM((BLOCKS_DEV + 2 * REACH, fields, BLOCK), jnp.float32),
            pltpu.SemaphoreType.DMA((BLOCKS_DEV + 3,)),
        ],
        out_shape=[own, side, side, slot_shape(own)],
        compiler_params=pltpu.CompilerParams(vmem_limit_bytes=12 << 20),
        name="residual",
    )(targets, observations, weight, row_effect, before, before_row, after, after_row, col)


def scales_of(dots_ref, scale_ref, part):
    @pl.when(pl.program_id(0) == 0)
    def _():
        scale_ref[...] = step_scales(*(dots_ref[k : k + 1] for k in range(4))).T

    return scale_ref[pl.ds(pl.multiple_of(pl.program_id(0) * part, part), part), :]


def first_kernel(src_ref, dots_ref, *refs):
    ins, (x_ref, r_ref, scale_ref) = refs[:-3], refs[-3:]
    scale = scales_of(dots_ref, scale_ref, x_ref.shape[0])
    for j in range(BLOCKS_DEV):
        r0, m1 = (ref[0] for ref in ins[2 * j : 2 * j + 2])
        x_ref[:, j, :] = scale[:, 0:1] * r0 + scale[:, 1:2] * m1
        r_ref[:, j, :] = scale[:, 2:3] * r0 + scale[:, 3:4] * m1


def second_kernel(src_ref, dots_ref, part_ref, *refs):
    ins, (r_ref, scale_ref) = refs[:-2], refs[-2:]
    scale = scales_of(dots_ref, scale_ref, r_ref.shape[0])
    for j in range(BLOCKS_DEV):
        r_ref[:, j, :] = part_ref[:, j, :] + scale[:, 4:5] * ins[j][0]


def combined(kernel, name, outs, sources, dots, held, *owned):
    _, fields, _ = owned[0].shape
    part = 16
    by_field = pl.BlockSpec((part, BLOCKS_DEV, BLOCK), lambda i, s: (i, 0, 0))
    ins, specs = list(held), [by_field] * len(held)
    for j in range(BLOCKS_DEV):
        for v in owned:
            ins.append(v)
            specs.append(
                pl.BlockSpec(
                    (1, part, BLOCK), functools.partial(lambda j, i, s: (s[j], i, 0), j)
                )
            )
    shape = jax.ShapeDtypeStruct((fields, BLOCKS_DEV, BLOCK), jnp.float32)
    return pl.pallas_call(
        kernel,
        grid_spec=pltpu.PrefetchScalarGridSpec(
            num_scalar_prefetch=1,
            grid=(fields // part,),
            in_specs=[pl.BlockSpec(dots.shape, lambda i, s: (0, 0))] + specs,
            out_specs=[by_field] * outs,
            scratch_shapes=[pltpu.VMEM((COL_DEV, 8), jnp.float32)],
        ),
        out_shape=[shape] * outs,
        compiler_params=pltpu.CompilerParams(vmem_limit_bytes=20 << 20),
        name=name,
    )(sources, dots, *ins)


def to_owners(slots):
    return lax.all_to_all(slots, SIXTEEN, 0, 0, tiled=True)


def step_scales(h00, h01, h11, h12):
    mu = h01 / h00
    var = (h11 - mu * h01) / h00
    a0 = 1.0 / (1.0 + mu)
    beta = var * a0 * a0
    skew = (h12 - mu * h11 - mu * (h11 - mu * h01)) / h00
    a1 = var / (var + skew - var * var * a0)
    x_r0 = a0 + a1 * beta + a1 * a0 * mu
    x_m1 = -a1 * a0
    r_r0 = a0 * mu * (1.0 - a1) - a1 * beta
    r_m1 = -a0 * (1.0 - a1) - a1 * a0 * mu - a1 * beta
    r_m2 = a1 * a0
    zero = jnp.zeros_like(mu)
    return jnp.concatenate([x_r0, x_m1, r_r0, r_m1, r_m2, zero, zero, zero], axis=0)


def on_device(observations, huber_scale, observed, jitter, owner_map, neighbours):
    fields, row_dev, col_dev = observations.shape
    sixteen_size = lax.axis_size(SIXTEEN)
    my_place = lax.axis_index(SIXTEEN)
    group_place = lax.axis_index(WIDE)
    total_strips = BLOCKS_DEV * sixteen_size
    weight = observed.astype(jnp.float32)
    spread_scale = huber_scale[:, None, None]

    def with_count(part, count):
        rows = jnp.zeros((8, count.shape[0]), jnp.float32).at[0].set(count)
        return jnp.concatenate([part, rows], axis=0)

    def terms(row_effect, col_effect):
        return weight[None] * jnp.clip(
            (observations - row_effect[:, :, None] - col_effect[:, None, :]) / spread_scale,
            -HUBER_EDGE,
            HUBER_EDGE,
        )

    def sum_wide(part):
        for axis in WIDE[::-1]:
            part = sum_direct(part, axis)
        return part

    row_effect = jnp.zeros((fields, row_dev), jnp.float32)
    col_effect = jnp.zeros((fields, col_dev), jnp.float32)
    part = with_count(jnp.sum(terms(row_effect, col_effect), axis=2), jnp.sum(weight, axis=1))
    part, jitter, owner_map, neighbours = lax.optimization_barrier(
        (part, jitter, owner_map, neighbours)
    )
    group_map = owner_map[0]
    scalars = jnp.concatenate(
        [neighbours[0, 0], jnp.stack([my_place, group_place, total_strips * STRIP])]
    ).astype(jnp.int32)

    def beside_tiles(part, axis, chunk, tiles, near=()):
        first = sum(CHUNKS[:chunk])
        if chunk:
            part, tiles = lax.optimization_barrier((part, tiles))
        received = sent_to_all(part, axis)
        tiles = covariance_tiles(first, CHUNKS[chunk], scalars, jitter, near, tiles)
        return lax.optimization_barrier((received, tiles))

    edges = jnp.concatenate([observations, weight[None], jitter], axis=0)
    before, after = beside(edges, REACH * STRIP, 1)
    received, tiles = beside_tiles(part, WIDE, 0, None)
    total = jnp.sum(received, axis=0)
    row_count = jnp.maximum(total[fields], 1.0)
    row_effect = huber_scale[:, None] * total[:fields] / row_count[None, :]
    part = with_count(jnp.sum(terms(row_effect, col_effect), axis=1), jnp.sum(weight, axis=0))
    received, tiles = beside_tiles(part, SIXTEEN, 1, tiles)
    total = jnp.sum(received, axis=0)
    col_count = jnp.maximum(total[fields], 1.0)
    col_effect = huber_scale[:, None] * total[:fields] / col_count[None, :]
    part = with_count(jnp.sum(terms(row_effect, col_effect), axis=2), jnp.zeros_like(row_count))
    received, tiles = beside_tiles(part, WIDE, 2, tiles)
    received, before, after = lax.optimization_barrier((received, before, after))
    near = (before[fields + 1 :], after[fields + 1 :])
    total = jnp.sum(received, axis=0)
    row_effect = row_effect + huber_scale[:, None] * total[:fields] / row_count[None, :]
    part = jnp.sum(terms(row_effect, col_effect), axis=1)
    part = jnp.concatenate([part, row_effect.reshape(-1, col_dev)], axis=0)
    received, tiles = beside_tiles(part, SIXTEEN, 3, tiles, near)
    total = jnp.sum(received[:, :fields], axis=0)
    col_effect = col_effect + huber_scale[:, None] * total / col_count[None, :]

    def rows_of(place, first):
        rows = lax.dynamic_index_in_dim(received[:, fields:], place % sixteen_size, 0, False)
        return rows.reshape(fields, row_dev)[:, first : first + REACH * STRIP]

    row_before = rows_of(my_place + sixteen_size - 1, row_dev - REACH * STRIP)
    row_after = rows_of(my_place + 1, 0)

    my_targets = lax.dynamic_slice_in_dim(group_map, my_place * BLOCKS_DEV, BLOCKS_DEV)
    r0, r0_before, r0_after, slots = residual_of(
        my_targets, observations, weight, row_effect, before, row_before, after, row_after, col_effect
    )
    owned_r0 = to_owners(slots)
    *m1, slots, dots = applied(
        scalars, my_targets, tiles, (r0,), beside=(r0_before, r0_after), send=True
    )
    before, after = swapped(*m1)
    part = applied(scalars, my_targets, tiles, m1, (0, EARLY_TILES))
    slots = gate(slots, part, before, after)
    owned_m1 = to_owners(slots)
    slots, last = applied(
        scalars, my_targets, tiles, m1, (EARLY_TILES, None), (before, after), part, True
    )
    dots = sum_direct(sum_wide(dots + last), SIXTEEN[1])
    slots = gate(slots, dots)
    owned_m2 = to_owners(slots)
    dots = sum_direct(dots, SIXTEEN[0])
    owned = owned_table(group_map, sixteen_size, BLOCKS_DEV)
    my_ids = lax.dynamic_index_in_dim(owned, my_place, 0, keepdims=False)
    sources = my_ids // BLOCKS_DEV
    solution_now, part = combined(
        first_kernel, "first", 2, sources, dots, (), in_hbm(owned_r0), in_hbm(owned_m1)
    )
    (residual_now,) = combined(second_kernel, "second", 1, sources, dots, (part,), owned_m2)
    return (solution_now[None, None], residual_now[None, None])


def solution(mesh):
    finer = Mesh(mesh.devices.reshape(4, 2, 4, 4), ("wide_0", "wide_1", "sixteen_0", "sixteen_1"))
    in_specs = (
        P(None, SIXTEEN, WIDE),
        P(),
        P(SIXTEEN, WIDE),
        P(None, SIXTEEN, WIDE),
        P(WIDE, None),
        P(WIDE, None, None),
    )
    out_specs = (P(WIDE, SIXTEEN, None, None, None), P(WIDE, SIXTEEN, None, None, None))
    return jax.shard_map(
        on_device, mesh=finer, in_specs=in_specs, out_specs=out_specs, check_vma=False
    )
```

```python
import functools

import jax
import jax.numpy as jnp
from jax import lax
from jax.experimental import pallas as pl
from jax.experimental.pallas import tpu as pltpu
from jax.sharding import Mesh
from jax.sharding import PartitionSpec as P

BLOCK = 512
BLOCKS_DEV = 8
REACH = 4
NEIGHBOURS = 6
PAIRED = NEIGHBOURS // 2
SWEEPS = 2
STRIP = 4
COL_DEV = 128
WIDE = ("wide_0", "wide_1")
SIXTEEN = ("sixteen_0", "sixteen_1")

HUBER_EDGE = 1.345
SILL_TERM = 0.02
ROOT_THREE = 1.7320508075688772
LOG2_E = 1.4426950408889634
SPREAD = 2.0 * STRIP
CUTOFF = 6.0 * STRIP
BAND = 24
GROUP = 16

OWN_TILES = BLOCKS_DEV + PAIRED * BLOCKS_DEV - 6
HALO_TILES = 2 * (2 + 3 + 4)
CHUNKS = (5, 9, 9, 21)
TILE_SLOTS = 4
OP_SLOTS = 12
OP_FIRST = 4
EXTRA = 8
EARLY_TILES = 21


def sent_to_all(shard, axis):
    peers = lax.axis_size(axis)
    return lax.all_to_all(
        jnp.broadcast_to(shard[None], (peers, *shard.shape)), axis, 0, 0, tiled=True
    )


def over_copies(shard, axis):
    return jnp.sum(sent_to_all(shard, axis), axis=0)


def sum_direct(part, axis, beside=None):
    peers = lax.axis_size(axis)
    moved = [
        lax.ppermute(part, axis, [(i, (i + k) % peers) for i in range(peers)])
        for k in range(1, peers)
    ]
    if beside is not None:
        part, beside = lax.optimization_barrier((part, beside))
    total = functools.reduce(jnp.add, moved, part)
    return total if beside is None else (total, beside)


def swapped(initial, last):
    peers = lax.axis_size(SIXTEEN)
    up = [(i, (i + 1) % peers) for i in range(peers)]
    down = [(j, i) for i, j in up]
    return lax.ppermute(last, SIXTEEN, up), lax.ppermute(initial, SIXTEEN, down)


def beside(shard, width, dim=0):
    length = shard.shape[dim]
    last = lax.slice_in_dim(shard, length - width, length, axis=dim)
    initial = lax.slice_in_dim(shard, 0, width, axis=dim)
    return swapped(*lax.optimization_barrier((initial, last)))


def owned_table(group_map, owners, per_owner):
    total_strips = group_map.shape[0]
    member = (group_map[None, :] == jnp.arange(owners, dtype=jnp.int32)[:, None]).astype(jnp.int32)
    ranked = jnp.cumsum(member, axis=1, dtype=jnp.int32) - 1
    slot_hit = (ranked[:, :, None] == jnp.arange(per_owner, dtype=jnp.int32)[None, None, :]).astype(
        jnp.int32
    ) * member[:, :, None]
    numbers = jnp.arange(total_strips, dtype=jnp.int32)
    return jnp.sum(slot_hit * numbers[None, :, None], axis=1, dtype=jnp.int32)


def offsets_of(list_ref):
    held = [
        functools.reduce(jnp.logical_or, [list_ref[n] == d for n in range(NEIGHBOURS)])
        for d in range(1, REACH)
    ]
    missing = jnp.where(held[0], jnp.where(held[1], jnp.where(held[2], 4, 3), 2), 1)
    return [k + jnp.where(missing <= k, 1, 0) for k in range(1, PAIRED + 1)]


def own_count(offsets):
    return (PAIRED + 1) * BLOCKS_DEV - (offsets[0] + offsets[1] + offsets[2])


def halo_count(offsets):
    return 2 * (offsets[0] + offsets[1] + offsets[2])


def own_pair(t, offsets):
    d1, d2, d3 = offsets
    p = t - BLOCKS_DEV
    n1, n2 = BLOCKS_DEV - d1, 2 * BLOCKS_DEV - d1 - d2
    one = jnp.where(p < n1, p, jnp.where(p < n2, p - n1, p - n2))
    return one, one + jnp.where(p < n1, d1, jnp.where(p < n2, d2, d3))


def halo_pair(q, offsets):
    d1, d2, d3 = offsets
    reach = d1 + d2 + d3
    right = q >= reach
    q = jnp.where(right, q - reach, q)
    step = jnp.where(q < d1, d1, jnp.where(q < d1 + d2, d2, d3))
    pos = jnp.where(q < d1, q, jnp.where(q < d1 + d2, q - d1, q - d1 - d2))
    one = jnp.where(right, BLOCKS_DEV - 1 - pos, pos)
    return one, jnp.where(right, one + step, one - step)


LISTED = OWN_TILES + HALO_TILES


def tiles_kernel(first, count, beside, held, scalar_ref, jitter_ref, *refs):
    beside_refs, refs = refs[:beside], refs[beside + held :]
    tiles_ref, buf, sem = refs
    a, b = ROOT_THREE * CUTOFF / SPREAD, 4.0
    offsets = offsets_of(scalar_ref)
    place, group = scalar_ref[NEIGHBOURS], scalar_ref[NEIGHBOURS + 1]
    total_rows = scalar_ref[NEIGHBOURS + 2]
    row_dev = STRIP * BLOCKS_DEV
    lane = lax.broadcasted_iota(jnp.int32, (GROUP, COL_DEV), 1)
    within = lax.broadcasted_iota(jnp.int32, (STRIP, COL_DEV), 0)
    across = lax.broadcasted_iota(jnp.int32, (STRIP, COL_DEV), 1)
    col_place = (group * COL_DEV + across).astype(jnp.float32)

    def out_copy(t):
        slot = lax.rem(t - first, TILE_SLOTS)
        return pltpu.make_async_copy(buf.at[slot], tiles_ref.at[t], sem.at[slot])

    def live(t):
        mine = (t < OWN_TILES) & (t < own_count(offsets))
        return mine | ((t >= OWN_TILES) & (t < OWN_TILES + halo_count(offsets)))

    def places(block, ref, at):
        row = lax.rem(place * row_dev + STRIP * block + total_rows, total_rows)
        rows = (row + within).astype(jnp.float32) + ref[0, pl.ds(at, STRIP), :]
        cols = col_place + ref[1, pl.ds(at, STRIP), :]
        return jnp.concatenate([rows, cols], axis=0) * (1.0 / CUTOFF)

    def pair_of(t):
        q = t - OWN_TILES
        one, other = own_pair(t, offsets)
        one_q, other_q = halo_pair(q, offsets)
        same = t < BLOCKS_DEV
        mine = t < OWN_TILES
        one = jnp.where(same, t, jnp.where(mine, one, one_q))
        return one, jnp.where(same, t, jnp.where(mine, other, other_q))

    def evaluate(slot, to, frm, sill):
        for rb in range(STRIP):
            row_b = jnp.broadcast_to(frm[rb : rb + 1], (COL_DEV, COL_DEV)).T
            col_b = jnp.broadcast_to(frm[STRIP + rb : STRIP + rb + 1], (COL_DEV, COL_DEV)).T
            for u in range(COL_DEV // 2 // GROUP):
                lo_s = slice(GROUP * u, GROUP * (u + 1))
                hi_s = slice(64 + GROUP * u, 64 + GROUP * (u + 1))
                near = (lane >= GROUP * u - BAND) & (lane < GROUP * (u + 1) + BAND)
                one_m = jnp.where(near, 1.0, 0.0).astype(jnp.bfloat16)
                other_m = jnp.where(near, 0.0, 1.0).astype(jnp.bfloat16)
                row_s = jnp.where(near, row_b[lo_s], row_b[hi_s])
                col_s = jnp.where(near, col_b[lo_s], col_b[hi_s])
                for ra in range(STRIP):
                    dr = row_s - to[ra : ra + 1]
                    dc = col_s - to[STRIP + ra : STRIP + ra + 1]
                    square = dr * dr + dc * dc
                    far = square * lax.rsqrt(jnp.maximum(square, 1e-30))
                    fading = jnp.maximum(1.0 - far, 0.0)
                    fading = fading * fading
                    fading = fading * fading
                    shape = (sill + (sill * (a + b)) * far) + (sill * (a * b)) * square
                    value = shape * fading * jnp.exp2((-a * LOG2_E) * far)
                    hi = value.astype(jnp.bfloat16)
                    lo = (value - hi.astype(jnp.float32)).astype(jnp.bfloat16)
                    lanes = slice(COL_DEV * ra, COL_DEV * (ra + 1))
                    top = rb * COL_DEV + GROUP * u
                    for part, at in ((hi, top), (lo, BLOCK + top)):
                        buf[slot, at : at + GROUP, lanes] = part * one_m
                        buf[slot, at + 64 : at + 64 + GROUP, lanes] = part * other_m

    def one_tile(t, carry):
        slot = lax.rem(t - first, TILE_SLOTS)
        past = jnp.maximum(t - TILE_SLOTS, first)

        @pl.when((t >= first + TILE_SLOTS) & live(past))
        def _():
            out_copy(past).wait()

        @pl.when(live(t))
        def _():
            one, other = pair_of(t)
            sill = jnp.where(one == other, (NEIGHBOURS + 1.0) * SILL_TERM, SILL_TERM)
            inside = jnp.clip(other, 0, BLOCKS_DEV - 1)
            to = places(one, jitter_ref, STRIP * one)
            frm = places(other, jitter_ref, STRIP * inside)
            if beside_refs:
                left = places(other, beside_refs[0], STRIP * jnp.clip(other + REACH, 0, REACH - 1))
                right = places(
                    other, beside_refs[1], STRIP * jnp.clip(other - BLOCKS_DEV, 0, REACH - 1)
                )
                frm = jnp.where(other < 0, left, jnp.where(other < BLOCKS_DEV, frm, right))
            evaluate(slot, to, frm, sill)
            out_copy(t).start()

        return carry

    lax.fori_loop(first, first + count, one_tile, 0)
    for t in range(max(first, first + count - TILE_SLOTS), first + count):

        @pl.when(live(t))
        def _(t=t):
            out_copy(t).wait()


def covariance_tiles(first, count, scalars, jitter, beside_jitter, held):
    extra = [] if held is None else [held]
    ins = [scalars, jitter, *beside_jitter, *extra]
    return pl.pallas_call(
        functools.partial(tiles_kernel, first, count, len(beside_jitter), len(extra)),
        in_specs=[SMEM_SPEC] + [VMEM_SPEC] * (1 + len(beside_jitter)) + [HBM_SPEC] * len(extra),
        out_specs=HBM_SPEC,
        scratch_shapes=[
            pltpu.VMEM((TILE_SLOTS, 2 * BLOCK, BLOCK), jnp.bfloat16),
            pltpu.SemaphoreType.DMA((TILE_SLOTS,)),
        ],
        out_shape=jax.ShapeDtypeStruct((LISTED, 2 * BLOCK, BLOCK), jnp.bfloat16),
        input_output_aliases={len(ins) - 1: 0} if extra else {},
        compiler_params=pltpu.CompilerParams(vmem_limit_bytes=12 << 20),
        cost_estimate=pl.CostEstimate(
            flops=count * 12 * BLOCK * BLOCK,
            bytes_accessed=count * 4 * BLOCK * BLOCK,
            transcendentals=count * BLOCK * BLOCK,
        ),
        name="tiles",
    )(*ins)


def halves(v):
    hi = v.astype(jnp.bfloat16)
    lo = (v - hi.astype(jnp.float32)).astype(jnp.bfloat16)
    return hi, lo


NN = (((1,), (0,)), ((), ()))
NT = (((1,), (1,)), ((), ()))


def product(both, tile_ref, dims):
    fields = both.shape[0] // 2
    main = lax.dot_general(
        both, tile_ref[:BLOCK], dims, preferred_element_type=jnp.float32
    )
    rest = lax.dot_general(
        both[:fields], tile_ref[BLOCK:], dims, preferred_element_type=jnp.float32
    )
    return main[:fields] + (main[fields:] + rest)


def op_kernel(first, last, pieces, halo, held, send, scalar_ref, target_ref, *refs):
    refs = list(refs)
    v_refs = [refs.pop(0) for _ in range(pieces)]
    beside_refs = [refs.pop(0), refs.pop(0)] if halo else []
    held_ref = refs.pop(0) if held else None
    tiles_ref = refs.pop(0)
    out_ref = None if send else refs.pop(0)
    edge_refs = [refs.pop(0), refs.pop(0)] if send and not held else []
    slots_ref, dots_ref = (refs.pop(0), refs.pop(0)) if send else (None, None)
    values, both_ref, total, buf, sem, in_sem, out_sem = refs
    fields = total.shape[1]
    offsets = offsets_of(scalar_ref)
    mine = (own_count(offsets) if last is None else last) - first
    count = mine + (halo_count(offsets) if halo else 0)

    def copy(t):
        slot = lax.rem(t, OP_SLOTS)
        at = jnp.where(t < mine, t + first, t - mine + OWN_TILES)
        return pltpu.make_async_copy(tiles_ref.at[at], buf.at[slot], sem.at[slot])

    size = BLOCKS_DEV // pieces
    loads = [(ref, size * i, size) for i, ref in enumerate(v_refs)]
    for side, ref in enumerate(beside_refs):
        loads.append((ref, BLOCKS_DEV + REACH * side, REACH))
    arriving = [
        pltpu.make_async_copy(ref, values.at[pl.ds(at, size)], in_sem.at[i])
        for i, (ref, at, size) in enumerate(loads)
    ]
    if held_ref is not None:
        arriving.append(pltpu.make_async_copy(held_ref, total, in_sem.at[4]))
    for load in arriving:
        load.start()
    for t in range(OP_FIRST):
        copy(t).start()
    for load in arriving:
        load.wait()
    for _, at, size in loads:
        for g in range(at, at + size):
            hi, lo = halves(values[g])
            both_ref[g, :fields] = hi
            both_ref[g, fields:] = lo

    def started(t):
        return jnp.minimum(jnp.minimum(OP_FIRST + 2 * t, t + OP_SLOTS - 1), count)

    def arrive(t):
        following, end = started(t), started(t + 1)
        for more in range(2):

            @pl.when(following + more < end)
            def _(more=more):
                copy(following + more).start()

        copy(t).wait()
        return buf.at[lax.rem(t, OP_SLOTS)]

    def with_itself(t, carry):
        tile = arrive(t)
        total[t] = product(both_ref[t], tile, NN)
        return carry

    def with_another(t, carry):
        tile = arrive(t)
        one, other = own_pair(t + first, offsets)
        total[one] += product(both_ref[other], tile, NN)
        total[other] += product(both_ref[one], tile, NT)
        return carry

    def with_beside(t, carry):
        tile = arrive(t)
        one, other = halo_pair(t - mine, offsets)
        side = BLOCKS_DEV + jnp.where(other < 0, other + REACH, other - BLOCKS_DEV + REACH)
        total[one] += product(both_ref[side], tile, NN)
        return carry

    if first == 0:
        lax.fori_loop(0, BLOCKS_DEV, with_itself, 0)
    lax.fori_loop(max(BLOCKS_DEV - first, 0), mine, with_another, 0)
    if halo:
        lax.fori_loop(mine, count, with_beside, 0)
    leaving = [
        pltpu.make_async_copy(
            total.at[pl.ds(REACH * side, REACH)], ref, out_sem.at[BLOCKS_DEV + 1 + side]
        )
        for side, ref in enumerate(edge_refs)
    ]
    if out_ref is not None:
        leaving.append(pltpu.make_async_copy(total, out_ref, out_sem.at[BLOCKS_DEV]))
    if send:
        leaving += out_copies(total, slots_ref, target_ref, out_sem)
    for out in leaving:
        out.start()
    if send:
        lane = lax.broadcasted_iota(jnp.int32, (fields, COL_DEV), 1)
        dots = jnp.zeros((fields, COL_DEV), jnp.float32)
        for at, one, other in products_of(values, total, held):
            summed = functools.reduce(jnp.add, [one[g] * other[g] for g in range(BLOCKS_DEV)])
            dots = jnp.where(lane == at, jnp.sum(summed, axis=1, keepdims=True), dots)
        dots = jnp.concatenate([dots, jnp.zeros((COL_DEV - fields, COL_DEV), jnp.float32)], axis=0)
        dots_ref[...] = dots.T[:EXTRA]
    for out in leaving:
        out.wait()


def products_of(v, image, second):
    if second:
        return [(3, v, image)]
    return [(0, v, v), (1, v, image), (2, image, image)]


def out_copies(values_ref, slots_ref, target_ref, sem):
    return [
        pltpu.make_async_copy(values_ref.at[g], slots_ref.at[target_ref[g]], sem.at[g])
        for g in range(BLOCKS_DEV)
    ]


SMEM_SPEC = pl.BlockSpec(memory_space=pltpu.SMEM)
VMEM_SPEC = pl.BlockSpec(memory_space=pltpu.VMEM)
HBM_SPEC = pl.BlockSpec(memory_space=pltpu.HBM)


def in_hbm(x):
    return pltpu.with_memory_space_constraint(x, pltpu.HBM)


def slot_shape(v):
    return pltpu.HBM((lax.axis_size(SIXTEEN), *v.shape[1:]), jnp.float32)


def applied(scalars, targets, tiles, v, tiles_of=(0, None), beside=(), held=None, send=False):
    _, fields, _ = v[0].shape
    blocks = BLOCKS_DEV
    shape = (blocks, fields, BLOCK)
    edges = send and held is None
    out = pltpu.HBM(shape, jnp.float32)
    ins = [in_hbm(x) for x in (*v, *beside, held) if x is not None] + [tiles]
    number = (tiles_of[1] or OWN_TILES) - tiles_of[0] + HALO_TILES * bool(beside)
    out = pl.pallas_call(
        functools.partial(op_kernel, *tiles_of, len(v), bool(beside), held is not None, send),
        in_specs=[SMEM_SPEC] * 2 + [HBM_SPEC] * len(ins),
        out_specs=[HBM_SPEC] * (not send) + [HBM_SPEC] * (2 * edges) + [HBM_SPEC, VMEM_SPEC] * send,
        scratch_shapes=[
            pltpu.VMEM((blocks + 2 * REACH, fields, BLOCK), jnp.float32),
            pltpu.VMEM((blocks + 2 * REACH, 2 * fields, BLOCK), jnp.bfloat16),
            pltpu.VMEM(shape, jnp.float32),
            pltpu.VMEM((OP_SLOTS, 2 * BLOCK, BLOCK), jnp.bfloat16),
            pltpu.SemaphoreType.DMA((OP_SLOTS,)),
            pltpu.SemaphoreType.DMA((5,)),
            pltpu.SemaphoreType.DMA((BLOCKS_DEV + 3,)),
        ],
        out_shape=[out] * (not send)
        + [pltpu.HBM((REACH, fields, BLOCK), jnp.float32)] * (2 * edges)
        + [slot_shape(out), jax.ShapeDtypeStruct((EXTRA, COL_DEV), jnp.float32)] * send,
        compiler_params=pltpu.CompilerParams(vmem_limit_bytes=28 << 20),
        cost_estimate=pl.CostEstimate(
            flops=3 * number * 3 * fields * BLOCK * BLOCK,
            bytes_accessed=number * 4 * BLOCK * BLOCK,
            transcendentals=0,
        ),
        name="applied",
    )(scalars, targets, *ins)
    return out if send else out[0]


def gate_kernel(*refs):
    pass


def gate(slots, *others):
    return pl.pallas_call(
        gate_kernel,
        in_specs=[HBM_SPEC] + [HBM_SPEC if other.ndim == 3 else VMEM_SPEC for other in others],
        out_specs=HBM_SPEC,
        out_shape=pltpu.HBM(slots.shape, jnp.float32),
        input_output_aliases={0: 0},
        compiler_params=pltpu.CompilerParams(vmem_limit_bytes=1 << 20),
        name="gate",
    )(slots, *(in_hbm(other) if other.ndim == 3 else other for other in others))


def residual_kernel(
    target_ref, obs_ref, weight_ref, row_ref, before_ref, before_row_ref, after_ref,
    after_row_ref, col_ref, out_ref, before_out_ref, after_out_ref, slots_ref, buf, sem,
):
    fields = obs_ref.shape[0]
    col = col_ref[...]

    def block(at, obs, weight, row, g):
        for ra in range(STRIP):
            r = STRIP * g + ra
            left = obs[:fields, r, :] - row[:, r : r + 1] - col
            weighted = weight[r : r + 1, :] * left
            buf[at, :, COL_DEV * ra : COL_DEV * (ra + 1)] = weighted

    copies = []
    for g in range(BLOCKS_DEV):
        block(g, obs_ref, weight_ref, row_ref, g)
        copies.append(
            pltpu.make_async_copy(buf.at[g], slots_ref.at[target_ref[g]], sem.at[g])
        )
        copies[-1].start()
    copies.append(
        pltpu.make_async_copy(buf.at[pl.ds(0, BLOCKS_DEV)], out_ref, sem.at[BLOCKS_DEV])
    )
    copies[-1].start()
    sides = ((before_ref, before_row_ref, before_out_ref), (after_ref, after_row_ref, after_out_ref))
    for side, (obs, row, out) in enumerate(sides):
        first = BLOCKS_DEV + REACH * side
        for g in range(REACH):
            block(first + g, obs, obs.at[fields], row, g)
        copies.append(
            pltpu.make_async_copy(
                buf.at[pl.ds(first, REACH)], out, sem.at[BLOCKS_DEV + 1 + side]
            )
        )
        copies[-1].start()
    for copy in copies:
        copy.wait()


def residual_of(targets, observations, weight, row_effect, before, before_row, after, after_row, col):
    fields = observations.shape[0]
    own = pltpu.HBM((BLOCKS_DEV, fields, BLOCK), jnp.float32)
    side = pltpu.HBM((REACH, fields, BLOCK), jnp.float32)
    return pl.pallas_call(
        residual_kernel,
        in_specs=[SMEM_SPEC] + [VMEM_SPEC] * 8,
        out_specs=[HBM_SPEC] * 4,
        scratch_shapes=[
            pltpu.VMEM((BLOCKS_DEV + 2 * REACH, fields, BLOCK), jnp.float32),
            pltpu.SemaphoreType.DMA((BLOCKS_DEV + 3,)),
        ],
        out_shape=[own, side, side, slot_shape(own)],
        compiler_params=pltpu.CompilerParams(vmem_limit_bytes=12 << 20),
        name="residual",
    )(targets, observations, weight, row_effect, before, before_row, after, after_row, col)


def scales_of(dots_ref, scale_ref, part):
    @pl.when(pl.program_id(0) == 0)
    def _():
        scale_ref[...] = step_scales(*(dots_ref[k : k + 1] for k in range(4))).T

    return scale_ref[pl.ds(pl.multiple_of(pl.program_id(0) * part, part), part), :]


def gather_kernel(src_ref, *refs):
    ins, outs = refs[:-2], refs[-2:]
    for j in range(BLOCKS_DEV):
        for k, out_ref in enumerate(outs):
            out_ref[:, j, :] = ins[2 * j + k][0]


def combine_kernel(src_ref, dots_ref, r0_ref, m1_ref, *refs):
    ins, (x_ref, r_ref, scale_ref) = refs[:-3], refs[-3:]
    scale = scales_of(dots_ref, scale_ref, r_ref.shape[0])
    for j in range(BLOCKS_DEV):
        r0, m1 = r0_ref[:, j, :], m1_ref[:, j, :]
        x_ref[:, j, :] = scale[:, 0:1] * r0 + scale[:, 1:2] * m1
        r_ref[:, j, :] = scale[:, 2:3] * r0 + scale[:, 3:4] * m1 + scale[:, 4:5] * ins[j][0]


def combined(kernel, name, sources, dots, held, *owned):
    _, fields, _ = owned[0].shape
    part = 16
    by_field = pl.BlockSpec((part, BLOCKS_DEV, BLOCK), lambda i, s: (i, 0, 0))
    ins, specs = dots + held, [pl.BlockSpec(x.shape, lambda i, s: (0, 0)) for x in dots]
    specs += [by_field] * len(held)
    for j in range(BLOCKS_DEV):
        for v in owned:
            ins.append(v)
            specs.append(
                pl.BlockSpec(
                    (1, part, BLOCK), functools.partial(lambda j, i, s: (s[j], i, 0), j)
                )
            )
    form = jax.ShapeDtypeStruct if dots else pltpu.HBM
    shape = form((fields, BLOCKS_DEV, BLOCK), jnp.float32)
    return pl.pallas_call(
        kernel,
        grid_spec=pltpu.PrefetchScalarGridSpec(
            num_scalar_prefetch=1,
            grid=(fields // part,),
            in_specs=specs,
            out_specs=[by_field] * 2,
            scratch_shapes=[pltpu.VMEM((COL_DEV, 8), jnp.float32)] * len(dots),
        ),
        out_shape=[shape] * 2,
        compiler_params=pltpu.CompilerParams(vmem_limit_bytes=20 << 20),
        cost_estimate=pl.CostEstimate(
            flops=0, bytes_accessed=16 * fields * BLOCKS_DEV * BLOCK, transcendentals=0
        ),
        name=name,
    )(sources, *ins)


def to_owners(slots):
    return lax.all_to_all(slots, SIXTEEN, 0, 0, tiled=True)


def step_scales(h00, h01, h11, h12):
    mu = h01 / h00
    var = (h11 - mu * h01) / h00
    a0 = 1.0 / (1.0 + mu)
    beta = var * a0 * a0
    skew = (h12 - mu * h11 - mu * (h11 - mu * h01)) / h00
    a1 = var / (var + skew - var * var * a0)
    x_r0 = a0 + a1 * beta + a1 * a0 * mu
    x_m1 = -a1 * a0
    r_r0 = a0 * mu * (1.0 - a1) - a1 * beta
    r_m1 = -a0 * (1.0 - a1) - a1 * a0 * mu - a1 * beta
    r_m2 = a1 * a0
    zero = jnp.zeros_like(mu)
    return jnp.concatenate([x_r0, x_m1, r_r0, r_m1, r_m2, zero, zero, zero], axis=0)


def on_device(observations, huber_scale, observed, jitter, owner_map, neighbours):
    fields, row_dev, col_dev = observations.shape
    sixteen_size = lax.axis_size(SIXTEEN)
    my_place = lax.axis_index(SIXTEEN)
    group_place = lax.axis_index(WIDE)
    total_strips = BLOCKS_DEV * sixteen_size
    weight = observed.astype(jnp.float32)
    spread_scale = huber_scale[:, None, None]

    def with_count(part, count):
        rows = jnp.zeros((8, count.shape[0]), jnp.float32).at[0].set(count)
        return jnp.concatenate([part, rows], axis=0)

    def terms(row_effect, col_effect):
        return weight[None] * jnp.clip(
            (observations - row_effect[:, :, None] - col_effect[:, None, :]) / spread_scale,
            -HUBER_EDGE,
            HUBER_EDGE,
        )

    def sum_wide(part):
        for axis in WIDE[::-1]:
            part = sum_direct(part, axis)
        return part

    row_effect = jnp.zeros((fields, row_dev), jnp.float32)
    col_effect = jnp.zeros((fields, col_dev), jnp.float32)
    part = with_count(jnp.sum(terms(row_effect, col_effect), axis=2), jnp.sum(weight, axis=1))
    part, jitter, owner_map, neighbours = lax.optimization_barrier(
        (part, jitter, owner_map, neighbours)
    )
    group_map = owner_map[0]
    scalars = jnp.concatenate(
        [neighbours[0, 0], jnp.stack([my_place, group_place, total_strips * STRIP])]
    ).astype(jnp.int32)

    def beside_tiles(part, axis, chunk, tiles, near=()):
        first = sum(CHUNKS[:chunk])
        if chunk:
            part, tiles = lax.optimization_barrier((part, tiles))
        received = sent_to_all(part, axis)
        tiles = covariance_tiles(first, CHUNKS[chunk], scalars, jitter, near, tiles)
        return lax.optimization_barrier((received, tiles))

    edges = jnp.concatenate([observations, weight[None], jitter], axis=0)
    before, after = beside(edges, REACH * STRIP, 1)
    received, tiles = beside_tiles(part, WIDE, 0, None)
    total = jnp.sum(received, axis=0)
    row_count = jnp.maximum(total[fields], 1.0)
    row_effect = huber_scale[:, None] * total[:fields] / row_count[None, :]
    part = with_count(jnp.sum(terms(row_effect, col_effect), axis=1), jnp.sum(weight, axis=0))
    received, tiles = beside_tiles(part, SIXTEEN, 1, tiles)
    total = jnp.sum(received, axis=0)
    col_count = jnp.maximum(total[fields], 1.0)
    col_effect = huber_scale[:, None] * total[:fields] / col_count[None, :]
    part = with_count(jnp.sum(terms(row_effect, col_effect), axis=2), jnp.zeros_like(row_count))
    received, tiles = beside_tiles(part, WIDE, 2, tiles)
    received, before, after = lax.optimization_barrier((received, before, after))
    near = (before[fields + 1 :], after[fields + 1 :])
    total = jnp.sum(received, axis=0)
    row_effect = row_effect + huber_scale[:, None] * total[:fields] / row_count[None, :]
    part = jnp.sum(terms(row_effect, col_effect), axis=1)
    part = jnp.concatenate([part, row_effect.reshape(-1, col_dev)], axis=0)
    received, tiles = beside_tiles(part, SIXTEEN, 3, tiles, near)
    total = jnp.sum(received[:, :fields], axis=0)
    col_effect = col_effect + huber_scale[:, None] * total / col_count[None, :]

    def rows_of(place, first):
        rows = lax.dynamic_index_in_dim(received[:, fields:], place % sixteen_size, 0, False)
        return rows.reshape(fields, row_dev)[:, first : first + REACH * STRIP]

    row_before = rows_of(my_place + sixteen_size - 1, row_dev - REACH * STRIP)
    row_after = rows_of(my_place + 1, 0)

    my_targets = lax.dynamic_slice_in_dim(group_map, my_place * BLOCKS_DEV, BLOCKS_DEV)
    r0, r0_before, r0_after, slots = residual_of(
        my_targets, observations, weight, row_effect, before, row_before, after, row_after, col_effect
    )
    owned_r0 = to_owners(slots)
    *m1, slots, dots = applied(
        scalars, my_targets, tiles, (r0,), beside=(r0_before, r0_after), send=True
    )
    before, after = swapped(*m1)
    part = applied(scalars, my_targets, tiles, m1, (0, EARLY_TILES))
    slots = gate(slots, part, before, after)
    owned_m1 = to_owners(slots)
    slots, last = applied(
        scalars, my_targets, tiles, m1, (EARLY_TILES, None), (before, after), part, True
    )
    dots = sum_direct(sum_wide(dots + last), SIXTEEN[1])
    slots = gate(slots, dots)
    owned_m2 = to_owners(slots)
    owned = owned_table(group_map, sixteen_size, BLOCKS_DEV)
    my_ids = lax.dynamic_index_in_dim(owned, my_place, 0, keepdims=False)
    sources = my_ids // BLOCKS_DEV
    early = combined(gather_kernel, "gather", sources, [], [], in_hbm(owned_r0), in_hbm(owned_m1))
    dots, early = sum_direct(dots, SIXTEEN[0], early)
    solution_now, residual_now = combined(
        combine_kernel, "combine", sources, [dots], list(map(in_hbm, early)), owned_m2
    )
    return (solution_now[None, None], residual_now[None, None])


def solution(mesh):
    finer = Mesh(mesh.devices.reshape(4, 2, 4, 4), ("wide_0", "wide_1", "sixteen_0", "sixteen_1"))
    in_specs = (
        P(None, SIXTEEN, WIDE),
        P(),
        P(SIXTEEN, WIDE),
        P(None, SIXTEEN, WIDE),
        P(WIDE, None),
        P(WIDE, None, None),
    )
    out_specs = (P(WIDE, SIXTEEN, None, None, None), P(WIDE, SIXTEEN, None, None, None))
    return jax.shard_map(
        on_device, mesh=finer, in_specs=in_specs, out_specs=out_specs, check_vma=False
    )
```
